256 devices in a mesh: gx: 32 (over z, x), gy: 4 (over y), gz: 2 (over core).
Axes of the slice: x: 4, y: 4, z: 8, core: 2. Of those that a mesh axis runs over, the one named last changes fastest.
Arguments:
- viscosity: bfloat16 [8, 2048, 1024], P('gz', 'gx', 'gy'), may hold values from 0.29882812 to 3
- velocity: bfloat16 [2, 8, 2048, 1024], P(None, 'gz', 'gx', 'gy'), may hold values from -6 to 6
- log_friction: float32 [2048, 1024], P('gx', 'gy'), may hold values from -1 to 1
- step_dir: float32 [2048, 1024], P('gx', 'gy'), may hold values from -6 to 6
- obs_weight: float32 [2048, 1024], P('gx', 'gy'), may hold values from 1 to 8
- tile_mask: int32 [32, 16], P('gx', 'gy'), may hold values from 0 to 2
- contact: int32 [2048, 1024], P('gx', 'gy'), may hold values 0 or 1
Outputs:
- depth_response: float32 [2, 2048, 1024], P(None, 'gx', 'gy')
- hess_vec: float32 [2048, 1024], P('gx', ('gy', 'gz'))
The draws below stay inside these ranges and needn't reach their ends.
Inputs may be any that keep to these rules, and one draw needn't show every extreme that they name: `tile_mask`: each tile's class: 0 ocean, 1 floating ice, 2 grounded ice.
All inputs are finite; a program needn't handle non-finite values. No bound on the sum of `contact` on one device may be relied on, other than what follows from the above.
Results may differ from the reference program's by a relative error of at most 0.0024.
Values may be sent and summed in bfloat16 or wider, within the bound.
A program may use at most 64 MiB of HBM per device.

```python
import math
import jax
import jax.numpy as jnp

ITERS = 8
SWEEPS = 2
TILE = 64
NX = 2048
NY = 1024
NZ = 8


def plant(result, key, low, high):
    longest = result.shape.index(max(result.shape))
    spots = []
    for shift in (0, 1):
        where = [jax.random.randint(jax.random.fold_in(key, axis), (), 0, length) for axis, length in enumerate(result.shape)]
        where[longest] = (where[longest] + shift) % result.shape[longest]
        spots.append(tuple(where))
    return result.at[spots[0]].set(low).at[spots[1]].set(high)


def shard_levels(own_key, dims, shards, smallest, top_value):
    loudness = 1.0
    for axis_at, shards_of in shards:
        draws = jax.random.uniform(jax.random.fold_in(jax.random.fold_in(own_key, 6), axis_at), (shards_of,), jnp.float32, smallest / len(shards), top_value / len(shards))
        loudness = loudness * jnp.repeat(jnp.exp(draws), dims[axis_at] // shards_of).reshape((-1,) + (1,) * (len(dims) - 1 - axis_at))
    return loudness


def noise(key, dims, deviation, limit, split=(), dtype=jnp.bfloat16):
    values = deviation * jax.random.normal(key, dims, jnp.float32)
    if split:
        values = values * shard_levels(key, dims, split, -0.22, 0.18)
    return jnp.clip(values, -limit, limit).astype(dtype)


def setup_inputs(seed: int = 0) -> dict:
    arg_keys = jax.random.split(jax.random.key(seed), 8)
    viscosity = jnp.clip(jnp.exp(math.log(3.0) - 2.306499 * jax.random.uniform(arg_keys[0], (NZ, NX, NY), jnp.float32) ** shard_levels(arg_keys[0], (NZ, NX, NY), ((0, 2), (1, 32), (2, 4)), -0.2, 0.2)), 0.29882812, 3.0).astype(jnp.bfloat16)
    velocity = noise(arg_keys[1], (2, NZ, NX, NY), 1.0, 6.0, ((1, 2), (2, 32), (3, 4)))
    log_friction = jnp.clip(jax.random.uniform(arg_keys[2], (NX, NY), jnp.float32, -1.0, 1.0) * shard_levels(arg_keys[2], (NX, NY), ((0, 32), (1, 4)), -0.4, 0.0), -1.0, 1.0)
    step_dir = noise(arg_keys[3], (NX, NY), 1.0, 6.0, ((0, 32), (1, 4)), jnp.float32)
    obs_weight = jnp.clip(jnp.exp(math.log(8.0) - 2.0794415 * jax.random.uniform(arg_keys[4], (NX, NY), jnp.float32) ** shard_levels(arg_keys[4], (NX, NY), ((0, 32), (1, 4)), -0.2, 0.2)), 1.0, 8.0)
    tile_mask = plant(jax.random.randint(arg_keys[5], (NX // TILE, NY // TILE), 0, 3), jax.random.fold_in(arg_keys[5], 1), 0, 2).astype(jnp.int32)
    contact = plant((jax.random.randint(arg_keys[6], (NX, NY), 0, 4) < 3).astype(jnp.int32), jax.random.fold_in(arg_keys[6], 1), 0, 1)
    return dict(viscosity=viscosity, velocity=velocity, log_friction=log_friction, step_dir=step_dir, obs_weight=obs_weight, tile_mask=tile_mask, contact=contact)


ASPECT = 16.0
LOWER = 0.1
UPPER = 2.0


def expand(tiles):
    return jnp.repeat(jnp.repeat(tiles, TILE, axis=0), TILE, axis=1)


def coefficients(values):
    center_eta = values[1:-1, 1:-1, 1:-1]

    def flat(beside):
        return jnp.where(beside > 0, 0.5 * (center_eta + beside), center_eta)

    def vertical(beside):
        return jnp.where(beside > 0, ASPECT * 0.5 * (center_eta + beside), jnp.zeros_like(center_eta))

    return (flat(values[1:-1, :-2, 1:-1]), flat(values[1:-1, 2:, 1:-1]),
            flat(values[1:-1, 1:-1, :-2]), flat(values[1:-1, 1:-1, 2:]),
            vertical(values[:-2, 1:-1, 1:-1]), vertical(values[2:, 1:-1, 1:-1]))


def stencil(padded, face_terms, diagonal, ice_cells):
    shifted_all = (padded[:, 1:-1, :-2, 1:-1], padded[:, 1:-1, 2:, 1:-1],
                   padded[:, 1:-1, 1:-1, :-2], padded[:, 1:-1, 1:-1, 2:],
                   padded[:, :-2, 1:-1, 1:-1], padded[:, 2:, 1:-1, 1:-1])
    beside = face_terms[0] * shifted_all[0].astype(jnp.float32)
    for factor, shifted in zip(face_terms[1:], shifted_all[1:]):
        beside = beside + factor * shifted.astype(jnp.float32)
    center = padded[:, 1:-1, 1:-1, 1:-1].astype(jnp.float32)
    return ice_cells * (diagonal * center - beside) + (1.0 - ice_cells) * center


def chebyshev(operator, inverse_diag, forcing):
    centre_value = (UPPER + LOWER) / 2.0
    half_width = (UPPER - LOWER) / 2.0
    sigma_ratio = centre_value / half_width
    solution = jnp.zeros(forcing.shape, jnp.float32)
    for sweep_index in range(SWEEPS):
        if sweep_index == 0:
            residual = forcing
        else:
            residual = forcing - operator(solution.astype(jnp.bfloat16))
        direction = inverse_diag * residual / centre_value
        rho_now = 1.0 / sigma_ratio
        for iter_index in range(ITERS):
            solution = solution + direction
            if iter_index + 1 < ITERS:
                residual = residual - operator(direction.astype(jnp.bfloat16))
                rho_next = 1.0 / (2.0 * sigma_ratio - rho_now)
                direction = (rho_next * rho_now) * direction + (2.0 * rho_next / half_width) * inverse_diag * residual
                rho_now = rho_next
    return solution


def reference(viscosity, velocity, log_friction, step_dir, obs_weight, tile_mask, contact):
    ice_cells = expand(tile_mask > 0).astype(jnp.float32)
    grounded = expand(tile_mask == 2).astype(jnp.float32)
    friction = jnp.exp(log_friction) * grounded * contact.astype(jnp.float32)
    values = jnp.pad(viscosity.astype(jnp.float32), 1)
    face_terms = coefficients(values)
    layers = viscosity.shape[0]
    bottom = (jnp.arange(layers) == 0).astype(jnp.float32)[:, None, None]
    diagonal = face_terms[0] + face_terms[1] + face_terms[2] + face_terms[3] + face_terms[4] + face_terms[5] + friction * bottom
    inverse_diag = ice_cells / diagonal + (1.0 - ice_cells)

    def operator(field):
        padded = jnp.pad(field, ((0, 0), (1, 1), (1, 1), (1, 1)))
        return stencil(padded, face_terms, diagonal, ice_cells)

    u_base = velocity[:, 0].astype(jnp.float32)
    forcing = (-(friction * step_dir) * u_base)[:, None] * bottom
    response = chebyshev(operator, inverse_diag, forcing)
    depth_response = jnp.sum(response, axis=1)
    adjoint_rhs = jnp.broadcast_to((ice_cells * obs_weight * depth_response)[:, None], response.shape)
    multiplier = chebyshev(operator, inverse_diag, adjoint_rhs)
    hess_vec = -friction * jnp.sum(u_base * multiplier[:, 0], axis=0)
    return depth_response, hess_vec
```

```python
import functools
import math

import jax
import jax.numpy as jnp
from jax import lax
from jax.experimental import pallas as pl
from jax.experimental.pallas import tpu as pltpu
from jax.sharding import PartitionSpec as P

MESH = pl.DeviceIdType.MESH
F32 = jnp.float32
BF16 = jnp.bfloat16

SWEEP = 8
ASPECT = 16.0
LOWER = 0.1
UPPER = 2.0
CENTRE = (UPPER + LOWER) / 2.0
HALF = (UPPER - LOWER) / 2.0
SIGMA = CENTRE / HALF

DELTA = CENTRE - 1.0
LINEAR = DELTA + CENTRE
ORDER = (3, 6, 1, 4, 5, 2, 7)
ANGLES = [math.pi * j / SWEEP for j in ORDER]
PS = [2.0 * DELTA - 2.0 * CENTRE * math.cos(t) for t in ANGLES]
QS = [
    DELTA * DELTA - 2.0 * CENTRE * DELTA * math.cos(t) + CENTRE * CENTRE - (HALF * math.sin(t)) ** 2
    for t in ANGLES
]
TOP = math.cosh(SWEEP * math.acosh(SIGMA))
SCALE = 2.0 ** (2 * SWEEP - 2) / (TOP * TOP) / HALF ** (2 * SWEEP)

WIDE = 16
NX, NY, NZ = 64, 128, 8
ROWS = NX // 2 + WIDE
XT = NX + 2 * WIDE
LANES = 4 * (NY + 2 * WIDE)
TILES = LANES // 128
CHUNK = 4
DIRS = [(dx, dy) for dx in (-1, 0, 1) for dy in (-1, 0, 1) if (dx, dy) != (0, 0)]


def lanes_of(shape):
    return lax.broadcasted_iota(jnp.int32, shape, len(shape) - 1)


def turned(value, by):
    by %= 128
    return value if by == 0 else pltpu.roll(value, by, value.ndim - 1)


def triple_low(own, left, right):
    lane = lanes_of(own[0].shape)

    def put(piece, to):
        return turned(piece[0], to - piece[1])

    a, b = turned(own[0], 16), turned(own[1], 48)
    t0 = jnp.where(lane < 16, put(left[0], 0), a)
    t1 = jnp.where(lane < 16, a, jnp.where(lane < 32, put(right[0], 16), jnp.where(lane < 48, put(left[1], 32), b)))
    t2 = jnp.where(lane < 48, b, put(right[1], 48))
    return t0, t1, t2


def triple_high(own, left, right):
    lane = lanes_of(own[0].shape)

    def put(piece, to):
        return turned(piece[0], to - piece[1])

    a, b = turned(own[0], 80), turned(own[1], 112)
    t2 = jnp.where(lane < 80, put(left[0], 64), a)
    t3 = jnp.where(
        lane < 80, a, jnp.where(lane < 96, put(right[0], 80), jnp.where(lane < 112, put(left[1], 96), b))
    )
    t4 = jnp.where(lane < 112, b, put(right[1], 112))
    return t2, t3, t4


def joined_tiles(low, high):
    middle = jnp.where(lanes_of(low[2].shape) < 64, low[2], high[0])
    return jnp.concatenate([low[0], low[1], middle, high[1], high[2]], axis=-1)


def kernel(
    gx_n,
    gy_n,
    visc_ref,
    vel_ref,
    logf_ref,
    step_ref,
    obs_ref,
    contact_ref,
    tile_ref,
    depth_ref,
    hess_ref,
    visc,
    edge_l,
    edge_r,
    pack_l,
    pack_r,
    base,
    logf,
    step,
    obs,
    contact,
    flat,
    flat_pack,
    flat_l,
    flat_r,
    rhs,
    rhs_pack,
    rhs_l,
    rhs_r,
    depth,
    hess,
    vlow,
    vhigh,
    flow,
    fhigh,
    clow,
    chigh,
    dlow,
    dhigh,
    gs,
    inv,
    u_buf,
    t_buf,
    local_sem,
    swap_send,
    swap_recv,
    a_send,
    a_recv,
    b_send,
    b_recv,
    c_send,
    c_recv,
):
    gx, gy, gz = lax.axis_index("gx"), lax.axis_index("gy"), lax.axis_index("gz")
    yb = 2 * gy + gz
    y_n = 2 * gy_n

    def there(dx, dy):
        nx, ny = gx + dx, yb + dy
        return (nx >= 0) & (nx < gx_n) & (ny >= 0) & (ny < y_n)

    def device(dx, dy):
        ny = yb + dy
        return (gx + dx, lax.div(ny, 2), lax.rem(ny, 2))

    own_cols = pl.ds(pl.multiple_of(gz * NY, NY), NY)
    other_cols = pl.ds(pl.multiple_of((1 - gz) * NY, NY), NY)
    own_rows = pl.ds(WIDE, NX)
    layers = visc_ref.shape[0]
    mine = pl.ds(gz * layers, layers)
    partner = (gx, gy, 1 - gz)

    local = [
        pltpu.make_async_copy(visc_ref.at[:, :, own_cols], visc.at[mine, own_rows], local_sem.at[0]),
        pltpu.make_async_copy(vel_ref.at[:, 0, :, own_cols], base.at[gz], local_sem.at[1]),
        pltpu.make_async_copy(logf_ref.at[:, own_cols], logf, local_sem.at[2]),
        pltpu.make_async_copy(step_ref.at[:, own_cols], step, local_sem.at[3]),
        pltpu.make_async_copy(contact_ref.at[:, own_cols], contact, local_sem.at[4]),
        pltpu.make_async_copy(obs_ref.at[:, own_cols], obs, local_sem.at[5]),
    ]
    for copy in local:
        copy.start()

    barrier = pltpu.get_barrier_semaphore()
    met = 0
    for d in DIRS:
        here = there(*d)
        met = met + here.astype(jnp.int32)

        @pl.when(here)
        def _():
            pl.semaphore_signal(barrier, inc=1, device_id=device(*d), device_id_type=MESH)

    @pl.when(gx == 0)
    def _():
        visc[:, 0:WIDE, :] = jnp.zeros((NZ, WIDE, NY), BF16)
        flat[:, 0:WIDE, :] = jnp.zeros((3, WIDE, NY), F32)
        rhs[:, 0:WIDE, :] = jnp.zeros((2, WIDE, NY), F32)

    @pl.when(gx == gx_n - 1)
    def _():
        visc[:, XT - WIDE : XT, :] = jnp.zeros((NZ, WIDE, NY), BF16)
        flat[:, XT - WIDE : XT, :] = jnp.zeros((3, WIDE, NY), F32)
        rhs[:, XT - WIDE : XT, :] = jnp.zeros((2, WIDE, NY), F32)

    for dy, ends in ((-1, (edge_l, flat_l, rhs_l)), (1, (edge_r, flat_r, rhs_r))):
        for dx, first, count in ((-1, 0, WIDE), (0, WIDE, NX), (1, WIDE + NX, WIDE)):

            @pl.when(jnp.logical_not(there(dx, dy)))
            def _():
                for end in ends:
                    end[first : first + count, :] = jnp.zeros((count, 128), end.dtype)

    pl.semaphore_wait(barrier, met)

    swap = [
        pltpu.make_async_remote_copy(
            visc_ref.at[:, :, other_cols],
            visc.at[mine, own_rows],
            swap_send.at[0],
            swap_recv.at[0],
            device_id=partner,
            device_id_type=MESH,
        ),
        pltpu.make_async_remote_copy(
            vel_ref.at[:, 0, :, other_cols],
            base.at[gz],
            swap_send.at[1],
            swap_recv.at[1],
            device_id=partner,
            device_id_type=MESH,
        ),
    ]
    for copy in swap:
        copy.start()

    for copy in local[1:]:
        copy.wait()

    lane = lanes_of((NX, NY))
    left_class, right_class = tile_ref[0, 2 * gz], tile_ref[0, 2 * gz + 1]
    kinds = jnp.where(lane < NY // 2, left_class, right_class)
    ice = (kinds > 0).astype(F32)
    friction = jnp.exp(logf[...]) * (kinds == 2).astype(F32) * contact[...].astype(F32)
    marked = jnp.where(kinds > 0, jnp.maximum(friction, 1e-30), 0.0)
    flat[2, own_rows, :] = marked

    swap[1].wait()
    drive = -(friction * step[...])
    flat[0, own_rows, :] = drive * base[0, 0].astype(F32)
    flat[1, own_rows, :] = drive * base[0, 1].astype(F32)

    fields = [flat[i, own_rows, :] for i in range(3)]
    packed = jnp.zeros((NX, 128), F32)
    for i, field in enumerate(fields):
        packed = jnp.where((lane >= 16 * i) & (lane < 16 * i + 16), turned(field, 16 * i), packed)
        at = 48 + 16 * i
        packed = jnp.where((lane >= at) & (lane < at + 16), turned(field, at - 112), packed)
    flat_pack[...] = packed

    def spread(dx):
        if dx == 0:
            return pl.ds(WIDE, NX), pl.ds(0, NX), pl.ds(WIDE, NX)
        if dx < 0:
            return pl.ds(WIDE, WIDE), pl.ds(0, WIDE), pl.ds(WIDE + NX, WIDE)
        return pl.ds(NX, WIDE), pl.ds(NX - WIDE, WIDE), pl.ds(0, WIDE)

    def to_neighbours(block, packs, lands, send, recv):
        copies = []
        for i, (dx, dy) in enumerate(DIRS):
            src, src_pack, dst = spread(dx)
            if dy == 0:
                pair = (block.at[:, src, :], block.at[:, dst, :])
            elif dy < 0:
                pair = (packs[0].at[src_pack, :], lands[1].at[dst, :])
            else:
                pair = (packs[1].at[src_pack, :], lands[0].at[dst, :])
            copies.append(
                pltpu.make_async_remote_copy(
                    *pair,
                    send.at[i],
                    recv.at[i],
                    device_id=device(dx, dy),
                    device_id_type=MESH,
                )
            )
        return copies

    def start_all(copies):
        for (dx, dy), copy in zip(DIRS, copies):
            pl.when(there(dx, dy))(copy.start)

    def arrived(copies):
        for (dx, dy), copy in zip(DIRS, copies):
            pl.when(there(-dx, -dy))(copy.wait_recv)

    def sent(copies):
        for (dx, dy), copy in zip(DIRS, copies):
            pl.when(there(dx, dy))(copy.wait_send)

    flat_copies = to_neighbours(flat, (flat_pack, flat_pack), (flat_l, flat_r), b_send, b_recv)
    start_all(flat_copies)

    local[0].wait()
    swap[0].wait()

    def pack_rows(i, _):
        rows = pl.ds(pl.multiple_of(i * 16, 16), 16)
        here = pl.ds(pl.multiple_of(WIDE + i * 16, 16), 16)
        spot = lanes_of((16, 128))
        low = jnp.zeros((16, 128), F32)
        high = jnp.zeros((16, 128), F32)
        for layer in range(NZ):
            e = visc[layer, here, :].astype(F32)
            inside = (spot >= 16 * layer) & (spot < 16 * layer + 16)
            low = jnp.where(inside, turned(e, 16 * layer), low)
            high = jnp.where(inside, turned(e, 16 * layer + 16), high)
        pack_l[rows, :] = low.astype(BF16)
        pack_r[rows, :] = high.astype(BF16)
        return 0

    lax.fori_loop(0, NX // 16, pack_rows, 0)
    visc_copies = to_neighbours(visc, (pack_l, pack_r), (edge_l, edge_r), a_send, a_recv)
    start_all(visc_copies)

    arrived(flat_copies)
    arrived(visc_copies)

    def spread_rows(i, _):
        for half, (place, out) in enumerate(((triple_low, vlow), (triple_high, vhigh))):
            rows = pl.ds(pl.multiple_of(half * ROWS + i * 16, 16), 16)
            ends_l, ends_r = edge_l[rows, :].astype(F32), edge_r[rows, :].astype(F32)
            for layer in range(NZ):
                own = visc[layer, rows, :].astype(F32)
                lefts, rights = (ends_l, 16 * layer), (ends_r, 16 * layer)
                for j, tile in enumerate(place((own, own), (lefts, lefts), (rights, rights))):
                    out[j, pl.ds(i * 16 * NZ + layer, 16, stride=NZ), :] = tile
        return 0

    lax.fori_loop(0, ROWS // 16, spread_rows, 0)

    def eight(i):
        return pl.ds(pl.multiple_of(i * NZ, NZ), NZ)

    t_buf[0] = jnp.zeros((NZ, LANES), F32)
    u_buf[0] = jnp.zeros((NZ, LANES), F32)

    def join_row(q, _):
        low = [vlow[j, eight(q), :] for j in range(3)]
        high = [vhigh[j, eight(ROWS - 1 - q), :] for j in range(3)]
        t_buf[q + 1] = joined_tiles(low, high)
        return 0

    lax.fori_loop(0, ROWS, join_row, 0)

    def close(buf):
        buf[ROWS + 1] = pltpu.roll(buf[ROWS], LANES // 2, 1)

    close(t_buf)

    def assemble(own, which, ends_l, ends_r, spots_l, spots_r, outs):
        def body(i, _):
            for half, (place, out) in enumerate(((triple_low, outs[0]), (triple_high, outs[1]))):
                rows = pl.ds(pl.multiple_of(half * ROWS + i * 8, 8), 8)
                l, r = ends_l[rows, :], ends_r[rows, :]
                pieces = [own[k, rows, :] for k in which]
                tiles = place(pieces, [(l, s) for s in spots_l], [(r, s) for s in spots_r])
                for j, tile in enumerate(tiles):
                    out[j, pl.ds(pl.multiple_of(i * 8, 8), 8), :] = tile
            return 0

        lax.fori_loop(0, ROWS // 8, body, 0)

    def flat_row(low, high, q):
        one = [low[j, pl.ds(q, 1), :] for j in range(3)]
        two = [high[j, pl.ds(ROWS - 1 - q, 1), :] for j in range(3)]
        return jnp.broadcast_to(joined_tiles(one, two), (NZ, LANES))

    assemble(flat, (2, 2), flat_l, flat_r, (80, 80), (32, 32), (clow, chigh))
    assemble(flat, (0, 1), flat_l, flat_r, (48, 64), (0, 16), (flow, fhigh))

    level = lax.broadcasted_iota(jnp.int32, (NZ, LANES), 0)

    def faces(q, _):
        here = t_buf[q + 1]

        def side(beside):
            return jnp.where(beside > 0, 0.5 * (here + beside), here)

        def column(beside):
            return (0.5 * ASPECT) * (here + beside)

        marks = flat_row(clow, chigh, q)
        parts = [
            side(t_buf[q]),
            side(t_buf[q + 2]),
            side(pltpu.roll(here, 1, 1)),
            side(pltpu.roll(here, LANES - 1, 1)),
            jnp.where(level > 0, column(pltpu.roll(here, 1, 0)), 0.0),
            jnp.where(level < NZ - 1, column(pltpu.roll(here, NZ - 1, 0)), 0.0),
        ]
        total = parts[0] + parts[1] + parts[2] + parts[3] + parts[4] + parts[5]
        total = total + jnp.where(level == 0, marks, 0.0)
        inverse = jnp.where(marks > 0, 1.0 / jnp.where(marks > 0, total, 1.0), 0.0)
        for j, part in enumerate(parts):
            gs[j, q] = part * inverse
        inverse = SCALE * inverse
        inv[q] = inverse
        u_buf[q + 1] = jnp.where(level == 0, inverse * flat_row(flow, fhigh, q), 0.0)
        return 0

    lax.fori_loop(0, ROWS, faces, 0)
    close(u_buf)

    def apply(src, dst, centre, shift, first):
        def chunk(i, _):
            for k in range(CHUNK):
                q = i * CHUNK + k
                here = src[q + 1]
                new = (
                    gs[0, q] * src[q]
                    + gs[1, q] * src[q + 2]
                    + gs[2, q] * pltpu.roll(here, 1, 1)
                    + gs[3, q] * pltpu.roll(here, LANES - 1, 1)
                    + gs[4, q] * pltpu.roll(here, 1, 0)
                    + gs[5, q] * pltpu.roll(here, NZ - 1, 0)
                    + shift * (here if centre is src else centre[q + 1])
                )
                dst[q + 1] = new
            return 0

        lax.fori_loop(lax.div(first, CHUNK), ROWS // CHUNK, chunk, 0)
        close(dst)

    def pick(values, i):
        out = jnp.float32(values[0])
        for k in range(1, len(values)):
            out = jnp.where(i == k, jnp.float32(values[k]), out)
        return out

    def solve():
        apply(u_buf, t_buf, u_buf, jnp.float32(LINEAR), jnp.int32(2))

        def factor(i, _):
            apply(t_buf, u_buf, t_buf, pick(PS, i), 2 * i + 3)
            apply(u_buf, t_buf, t_buf, pick(QS, i), 2 * i + 4)
            return 0

        lax.fori_loop(0, len(PS), factor, 0)

    def columns(reduce):
        def body(i, _):
            row = reduce(t_buf[WIDE + 1 + i])
            for j in range(3):
                dlow[j, pl.ds(i, 1), :] = row[:, 128 * j : 128 * j + 128]
                dhigh[j, pl.ds(NX // 2 - 1 - i, 1), :] = row[:, 128 * j + 256 : 128 * j + 384]
            return 0

        lax.fori_loop(0, NX // 2, body, 0)
        spot = lanes_of((NX // 2, NY))
        low, high = [dlow[j] for j in range(3)], [dhigh[j] for j in range(3)]
        top = (
            jnp.where(spot < 112, turned(low[0], -16), turned(low[1], -16)),
            jnp.where(spot < 80, turned(low[1], -48), turned(low[2], -48)),
        )
        bottom = (
            jnp.where(spot < 48, turned(high[0], -80), turned(high[1], -80)),
            jnp.where(spot < 16, turned(high[1], -112), turned(high[2], -112)),
        )
        return top, bottom

    solve()
    top, bottom = columns(lambda row: jnp.sum(row, axis=0, keepdims=True))
    for k in range(2):
        depth[k, 0 : NX // 2, :] = top[k]
        depth[k, NX // 2 : NX, :] = bottom[k]
    weight = ice * obs[...]
    packed = jnp.zeros((NX, 128), F32)
    for k in range(2):
        field = weight * depth[k]
        rhs[k, own_rows, :] = field
        packed = jnp.where((lane >= 16 * k) & (lane < 16 * k + 16), turned(field, 16 * k), packed)
        at = 32 + 16 * k
        packed = jnp.where((lane >= at) & (lane < at + 16), turned(field, at - 112), packed)
    rhs_pack[...] = packed

    rhs_copies = to_neighbours(rhs, (rhs_pack, rhs_pack), (rhs_l, rhs_r), c_send, c_recv)
    start_all(rhs_copies)
    depth_out = pltpu.make_async_copy(depth, depth_ref.at[:, :, own_cols], local_sem.at[6])
    depth_out.start()
    depth_over = pltpu.make_async_remote_copy(
        depth,
        depth_ref.at[:, :, own_cols],
        swap_send.at[2],
        swap_recv.at[2],
        device_id=partner,
        device_id_type=MESH,
    )
    depth_over.start()

    arrived(rhs_copies)
    assemble(rhs, (0, 1), rhs_l, rhs_r, (32, 48), (0, 16), (flow, fhigh))

    def start_row(q, _):
        u_buf[q + 1] = inv[q] * flat_row(flow, fhigh, q)
        return 0

    lax.fori_loop(0, ROWS, start_row, 0)
    close(u_buf)
    solve()
    top, bottom = columns(lambda row: row[0:1, :])
    for half, pair in enumerate((top, bottom)):
        part = slice(half * NX // 2, (half + 1) * NX // 2)
        product = base[0, 0, part].astype(F32) * pair[0] + base[0, 1, part].astype(F32) * pair[1]
        hess[part, :] = -friction[part] * product
    hess_out = pltpu.make_async_copy(hess, hess_ref, local_sem.at[7])
    hess_out.start()

    for copies in (flat_copies, visc_copies, rhs_copies):
        sent(copies)
    depth_out.wait()
    depth_over.wait()
    hess_out.wait()


def solution(mesh):
    gx_n, gy_n = mesh.shape["gx"], mesh.shape["gy"]

    def step(viscosity, velocity, log_friction, step_dir, obs_weight, tile_mask, contact):
        any_space = pl.BlockSpec(memory_space=pl.ANY)
        vmem, dma = pltpu.VMEM, pltpu.SemaphoreType.DMA
        nd = len(DIRS)
        return pl.pallas_call(
            functools.partial(kernel, gx_n, gy_n),
            out_shape=(
                jax.ShapeDtypeStruct((2, NX, 2 * NY), F32),
                jax.ShapeDtypeStruct((NX, NY), F32),
            ),
            in_specs=[any_space] * 6 + [pl.BlockSpec(memory_space=pltpu.SMEM)],
            out_specs=(any_space, any_space),
            scratch_shapes=[
                vmem((NZ, XT, NY), BF16),
                vmem((XT, 128), BF16),
                vmem((XT, 128), BF16),
                vmem((NX, 128), BF16),
                vmem((NX, 128), BF16),
                vmem((2, 2, NX, NY), BF16),
                vmem((NX, NY), F32),
                vmem((NX, NY), F32),
                vmem((NX, NY), F32),
                vmem((NX, NY), jnp.int32),
                vmem((3, XT, NY), F32),
                vmem((NX, 128), F32),
                vmem((XT, 128), F32),
                vmem((XT, 128), F32),
                vmem((2, XT, NY), F32),
                vmem((NX, 128), F32),
                vmem((XT, 128), F32),
                vmem((XT, 128), F32),
                vmem((2, NX, NY), F32),
                vmem((NX, NY), F32),
                vmem((3, ROWS * NZ, 128), F32),
                vmem((3, ROWS * NZ, 128), F32),
                vmem((3, ROWS, 128), F32),
                vmem((3, ROWS, 128), F32),
                vmem((3, ROWS, 128), F32),
                vmem((3, ROWS, 128), F32),
                vmem((3, NX // 2, 128), F32),
                vmem((3, NX // 2, 128), F32),
                vmem((6, ROWS, NZ, LANES), F32),
                vmem((ROWS, NZ, LANES), F32),
                vmem((ROWS + 2, NZ, LANES), F32),
                vmem((ROWS + 2, NZ, LANES), F32),
                dma((8,)),
                dma((3,)),
                dma((3,)),
                dma((nd,)),
                dma((nd,)),
                dma((nd,)),
                dma((nd,)),
                dma((nd,)),
                dma((nd,)),
            ],
            compiler_params=pltpu.CompilerParams(
                collective_id=0, has_side_effects=True, vmem_limit_bytes=40 * 1024 * 1024
            ),
        )(viscosity, velocity, log_friction, step_dir, obs_weight, contact, tile_mask)

    in_specs = (
        P("gz", "gx", "gy"),
        P(None, "gz", "gx", "gy"),
        P("gx", "gy"),
        P("gx", "gy"),
        P("gx", "gy"),
        P("gx", "gy"),
        P("gx", "gy"),
    )
    out_specs = (P(None, "gx", "gy"), P("gx", ("gy", "gz")))
    return jax.shard_map(step, mesh=mesh, in_specs=in_specs, out_specs=out_specs, check_vma=False)
```

```python
import functools
import math

import jax
import jax.numpy as jnp
from jax import lax
from jax.experimental import pallas as pl
from jax.experimental.pallas import tpu as pltpu
from jax.sharding import PartitionSpec as P

MESH = pl.DeviceIdType.MESH
F32 = jnp.float32
BF16 = jnp.bfloat16

SWEEP = 8
ASPECT = 16.0
LOWER = 0.1
UPPER = 2.0
CENTRE = (UPPER + LOWER) / 2.0
HALF = (UPPER - LOWER) / 2.0
SIGMA = CENTRE / HALF

DELTA = CENTRE - 1.0
LINEAR = DELTA + CENTRE
ORDER = (3, 6, 1, 4, 5, 2, 7)
ANGLES = [math.pi * j / SWEEP for j in ORDER]
PS = [2.0 * DELTA - 2.0 * CENTRE * math.cos(t) for t in ANGLES]
QS = [
    DELTA * DELTA - 2.0 * CENTRE * DELTA * math.cos(t) + CENTRE * CENTRE - (HALF * math.sin(t)) ** 2
    for t in ANGLES
]
TOP = math.cosh(SWEEP * math.acosh(SIGMA))
SCALE = 2.0 ** (2 * SWEEP - 2) / (TOP * TOP) / HALF ** (2 * SWEEP)

WIDE = 16
NX, NY, NZ = 64, 128, 8
ROWS = NX // 2 + WIDE
XT = NX + 2 * WIDE
FINE = 5
BLOCKS = (NY + 2 * WIDE) // FINE
CHUNK = 8
DIRS = [(dx, dy) for dx in (-1, 0, 1) for dy in (-1, 0, 1) if (dx, dy) != (0, 0)]


def lanes_of(shape):
    return lax.broadcasted_iota(jnp.int32, shape, len(shape) - 1)


def turned(value, by):
    by %= 128
    return value if by == 0 else pltpu.roll(value, by, value.ndim - 1)


def chooser(rows, fine, spot):
    k = lax.broadcasted_iota(jnp.int32, (rows, 128), 0)
    n = lanes_of((rows, 128))
    y = FINE * (n % BLOCKS) + fine
    return (k == spot(n // 64, (n // BLOCKS) % 2, y)).astype(F32).astype(BF16)


def spot_single(half, component, y):
    edge = jnp.where(y < WIDE, 128 + 80 + y, 128 + 32 + y - WIDE - NY)
    k = 256 * half + jnp.where((y >= WIDE) & (y < WIDE + NY), y - WIDE, edge)
    return jnp.where((y >= 0) & (y < NY + 2 * WIDE), k, -1)


def spot_pair(half, component, y):
    edge = 256 + 16 * component + jnp.where(y < WIDE, 48 + y, y - WIDE - NY)
    return 384 * half + jnp.where((y >= WIDE) & (y < WIDE + NY), 128 * component + y - WIDE, edge)


def returner(half, component):
    k = lax.broadcasted_iota(jnp.int32, (FINE * 128, NY), 0)
    y = lanes_of((FINE * 128, NY)) + WIDE
    source = (y % FINE) * 128 + 64 * half + BLOCKS * component + y // FINE
    return (k == source).astype(F32).astype(BF16)


def mirror(n):
    k = lax.broadcasted_iota(jnp.int32, (n, n), 0)
    return (k + lanes_of((n, n)) == n - 1).astype(F32).astype(BF16)


def thirds(value):
    high = value.astype(BF16)
    rest = value - high.astype(F32)
    middle = rest.astype(BF16)
    return high, middle, (rest - middle.astype(F32)).astype(BF16)


def dot(a, b):
    return jnp.dot(a, b, preferred_element_type=F32)


def exact_dot(value, matrix):
    n = value.shape[0]
    out = dot(jnp.concatenate(thirds(value), axis=0), matrix)
    return out[:n] + out[n : 2 * n] + out[2 * n :]


def kernel(
    gx_n,
    gy_n,
    visc_ref,
    vel_ref,
    logf_ref,
    step_ref,
    obs_ref,
    contact_ref,
    tile_ref,
    depth_ref,
    hess_ref,
    visc,
    edge_l,
    edge_r,
    pack_l,
    pack_r,
    base,
    logf,
    step,
    obs,
    contact,
    flat,
    flat_pack,
    flat_l,
    flat_r,
    rhs,
    rhs_pack,
    rhs_l,
    rhs_r,
    depth,
    hess,
    left,
    e_buf,
    spread_f,
    spread_c,
    dlow,
    dhigh,
    single,
    pair,
    back,
    gs,
    inv,
    ext,
    u_buf,
    t_buf,
    local_sem,
    swap_send,
    swap_recv,
    a_send,
    a_recv,
    b_send,
    b_recv,
    c_send,
    c_recv,
):
    gx, gy, gz = lax.axis_index("gx"), lax.axis_index("gy"), lax.axis_index("gz")
    yb = 2 * gy + gz
    y_n = 2 * gy_n

    def there(dx, dy):
        nx, ny = gx + dx, yb + dy
        return (nx >= 0) & (nx < gx_n) & (ny >= 0) & (ny < y_n)

    def device(dx, dy):
        ny = yb + dy
        return (gx + dx, lax.div(ny, 2), lax.rem(ny, 2))

    own_cols = pl.ds(pl.multiple_of(gz * NY, NY), NY)
    other_cols = pl.ds(pl.multiple_of((1 - gz) * NY, NY), NY)
    own_rows = pl.ds(WIDE, NX)
    layers = visc_ref.shape[0]
    mine = pl.ds(gz * layers, layers)
    partner = (gx, gy, 1 - gz)

    local = [
        pltpu.make_async_copy(visc_ref.at[:, :, own_cols], visc.at[mine, own_rows], local_sem.at[0]),
        pltpu.make_async_copy(vel_ref.at[:, 0, :, own_cols], base.at[gz], local_sem.at[1]),
        pltpu.make_async_copy(logf_ref.at[:, own_cols], logf, local_sem.at[2]),
        pltpu.make_async_copy(step_ref.at[:, own_cols], step, local_sem.at[3]),
        pltpu.make_async_copy(contact_ref.at[:, own_cols], contact, local_sem.at[4]),
        pltpu.make_async_copy(obs_ref.at[:, own_cols], obs, local_sem.at[5]),
    ]
    for copy in local:
        copy.start()

    barrier = pltpu.get_barrier_semaphore()
    met = 0
    for d in DIRS:
        here = there(*d)
        met = met + here.astype(jnp.int32)

        @pl.when(here)
        def _():
            pl.semaphore_signal(barrier, inc=1, device_id=device(*d), device_id_type=MESH)

    @pl.when(gx == 0)
    def _():
        visc[:, 0:WIDE, :] = jnp.zeros((NZ, WIDE, NY), BF16)
        flat[:, 0:WIDE, :] = jnp.zeros((3, WIDE, NY), F32)
        rhs[:, 0:WIDE, :] = jnp.zeros((2, WIDE, NY), F32)

    @pl.when(gx == gx_n - 1)
    def _():
        visc[:, XT - WIDE : XT, :] = jnp.zeros((NZ, WIDE, NY), BF16)
        flat[:, XT - WIDE : XT, :] = jnp.zeros((3, WIDE, NY), F32)
        rhs[:, XT - WIDE : XT, :] = jnp.zeros((2, WIDE, NY), F32)

    for dy, ends in ((-1, (edge_l, flat_l, rhs_l)), (1, (edge_r, flat_r, rhs_r))):
        for dx, first, count in ((-1, 0, WIDE), (0, WIDE, NX), (1, WIDE + NX, WIDE)):

            @pl.when(jnp.logical_not(there(dx, dy)))
            def _():
                for end in ends:
                    end[first : first + count, :] = jnp.zeros((count, 128), end.dtype)

    for fine in range(FINE):
        lot = slice(128 * fine, 128 * fine + 128)
        single[:, lot] = chooser(512, fine, spot_single)
        pair[:, lot] = chooser(768, fine, spot_pair)
    single[:, 128 * FINE : 128 * (FINE + 1)] = chooser(512, -1, spot_single)
    single[:, 128 * (FINE + 1) : 128 * (FINE + 2)] = chooser(512, FINE, spot_single)
    for half in range(2):
        for component in range(2):
            at = 128 * (2 * half + component)
            back[:, at : at + 128] = returner(half, component)

    pl.semaphore_wait(barrier, met)

    swap = [
        pltpu.make_async_remote_copy(
            visc_ref.at[:, :, other_cols],
            visc.at[mine, own_rows],
            swap_send.at[0],
            swap_recv.at[0],
            device_id=partner,
            device_id_type=MESH,
        ),
        pltpu.make_async_remote_copy(
            vel_ref.at[:, 0, :, other_cols],
            base.at[gz],
            swap_send.at[1],
            swap_recv.at[1],
            device_id=partner,
            device_id_type=MESH,
        ),
    ]
    for copy in swap:
        copy.start()

    for copy in local[1:]:
        copy.wait()

    lane = lanes_of((NX, NY))
    left_class, right_class = tile_ref[0, 2 * gz], tile_ref[0, 2 * gz + 1]
    kinds = jnp.where(lane < NY // 2, left_class, right_class)
    ice = (kinds > 0).astype(F32)
    friction = jnp.exp(logf[...]) * (kinds == 2).astype(F32) * contact[...].astype(F32)
    marked = jnp.where(kinds > 0, jnp.maximum(friction, 1e-30), 0.0)
    flat[2, own_rows, :] = marked

    swap[1].wait()
    drive = -(friction * step[...])
    flat[0, own_rows, :] = drive * base[0, 0].astype(F32)
    flat[1, own_rows, :] = drive * base[0, 1].astype(F32)

    fields = [flat[i, own_rows, :] for i in range(3)]
    packed = jnp.zeros((NX, 128), F32)
    for i, field in enumerate(fields):
        packed = jnp.where((lane >= 16 * i) & (lane < 16 * i + 16), turned(field, 16 * i), packed)
        at = 48 + 16 * i
        packed = jnp.where((lane >= at) & (lane < at + 16), turned(field, at - 112), packed)
    flat_pack[...] = packed

    def spread(dx):
        if dx == 0:
            return pl.ds(WIDE, NX), pl.ds(0, NX), pl.ds(WIDE, NX)
        if dx < 0:
            return pl.ds(WIDE, WIDE), pl.ds(0, WIDE), pl.ds(WIDE + NX, WIDE)
        return pl.ds(NX, WIDE), pl.ds(NX - WIDE, WIDE), pl.ds(0, WIDE)

    def to_neighbours(block, packs, lands, send, recv):
        copies = []
        for i, (dx, dy) in enumerate(DIRS):
            src, src_pack, dst = spread(dx)
            if dy == 0:
                pair = (block.at[:, src, :], block.at[:, dst, :])
            elif dy < 0:
                pair = (packs[0].at[src_pack, :], lands[1].at[dst, :])
            else:
                pair = (packs[1].at[src_pack, :], lands[0].at[dst, :])
            copies.append(
                pltpu.make_async_remote_copy(
                    *pair,
                    send.at[i],
                    recv.at[i],
                    device_id=device(dx, dy),
                    device_id_type=MESH,
                )
            )
        return copies

    def start_all(copies):
        for (dx, dy), copy in zip(DIRS, copies):
            pl.when(there(dx, dy))(copy.start)

    def arrived(copies):
        for (dx, dy), copy in zip(DIRS, copies):
            pl.when(there(-dx, -dy))(copy.wait_recv)

    def sent(copies):
        for (dx, dy), copy in zip(DIRS, copies):
            pl.when(there(dx, dy))(copy.wait_send)

    flat_copies = to_neighbours(flat, (flat_pack, flat_pack), (flat_l, flat_r), b_send, b_recv)
    start_all(flat_copies)

    local[0].wait()
    swap[0].wait()

    def pack_rows(i, _):
        rows = pl.ds(pl.multiple_of(i * 16, 16), 16)
        here = pl.ds(pl.multiple_of(WIDE + i * 16, 16), 16)
        spot = lanes_of((16, 128))
        low = jnp.zeros((16, 128), F32)
        high = jnp.zeros((16, 128), F32)
        for layer in range(NZ):
            e = visc[layer, here, :].astype(F32)
            inside = (spot >= 16 * layer) & (spot < 16 * layer + 16)
            low = jnp.where(inside, turned(e, 16 * layer), low)
            high = jnp.where(inside, turned(e, 16 * layer + 16), high)
        pack_l[rows, :] = low.astype(BF16)
        pack_r[rows, :] = high.astype(BF16)
        return 0

    lax.fori_loop(0, NX // 16, pack_rows, 0)
    visc_copies = to_neighbours(visc, (pack_l, pack_r), (edge_l, edge_r), a_send, a_recv)
    start_all(visc_copies)

    arrived(flat_copies)
    arrived(visc_copies)

    low_rows, high_rows = slice(0, ROWS), slice(ROWS, XT)
    flipped = mirror(ROWS)

    spot = lanes_of((ROWS, 128))
    turned_rows = []
    for half, rows in enumerate((low_rows, high_rows)):
        ends_l, ends_r = edge_l[rows, :].astype(F32), edge_r[rows, :].astype(F32)
        for layer in range(NZ):
            edge = jnp.where(spot < 64, turned(ends_r, 32 - 16 * layer), turned(ends_l, 80 - 16 * layer))
            edge = edge.astype(BF16)
            own = visc[layer, rows, :]
            if half == 1:
                both = dot(flipped, jnp.concatenate([own, edge], axis=1)).astype(BF16)
                own, edge = both[:, :128], both[:, 128:]
            here = slice(ROWS * layer, ROWS * layer + ROWS)
            left[here, 256 * half : 256 * half + 128] = own
            left[here, 256 * half + 128 : 256 * half + 256] = edge

    tiles = FINE + 2
    for fine in range(tiles):
        placed = 0.5 * dot(left[...], single[:, 128 * fine : 128 * fine + 128])
        for layer in range(NZ):
            e_buf[pl.ds(tiles * NZ + fine * NZ + layer, ROWS, stride=tiles * NZ), :] = placed[
                ROWS * layer : ROWS * layer + ROWS
            ]
    e_buf[0 : tiles * NZ, :] = jnp.zeros((tiles * NZ, 128), F32)

    def e_tile(row, fine):
        return pl.ds(pl.multiple_of((row * tiles + fine) * NZ, NZ), NZ)

    for fine in range(FINE):
        e_buf[e_tile(ROWS + 1, fine), :] = pltpu.roll(e_buf[e_tile(ROWS, fine), :], 64, 1)

    def both_halves(pieces):
        low, high = pieces(low_rows), thirds(pieces(high_rows))
        width = low.shape[1]
        high = dot(flipped, jnp.concatenate(high, axis=1))
        return jnp.concatenate([low, high[:, :width] + high[:, width : 2 * width] + high[:, 2 * width :]], axis=1)

    def edges(rows, ends_l, ends_r):
        return jnp.where(spot < 48, ends_r[rows, :], ends_l[rows, :])

    def put(out, value):
        for fine in range(FINE):
            out[fine] = value[:, 128 * fine : 128 * fine + 128]

    marks_placed = exact_dot(
        both_halves(lambda rows: jnp.concatenate([flat[2, rows, :], edges(rows, flat_l, flat_r)], axis=1)),
        single[:, : 128 * FINE],
    )
    put(spread_c, marks_placed)

    def spread_pair(own, ends_l, ends_r):
        placed = exact_dot(
            both_halves(
                lambda rows: jnp.concatenate([own[0, rows, :], own[1, rows, :], edges(rows, ends_l, ends_r)], axis=1)
            ),
            pair[...],
        )
        put(spread_f, placed)

    spread_pair(flat, flat_l, flat_r)

    level = lax.broadcasted_iota(jnp.int32, (NZ, 128), 0)

    def flat_tile(field, q, fine):
        return jnp.broadcast_to(field[fine, pl.ds(q, 1), :], (NZ, 128))

    def faces(q, _):
        for fine in range(FINE):
            here = e_buf[e_tile(q + 1, fine), :]

            def side(beside):
                return here + jnp.where(beside > 0, beside, here)

            def column(beside):
                return ASPECT * (here + beside)

            marks = flat_tile(spread_c, q, fine)
            parts = [
                side(e_buf[e_tile(q, fine), :]),
                side(e_buf[e_tile(q + 2, fine), :]),
                side(e_buf[e_tile(q + 1, fine - 1 if fine else FINE), :]),
                side(e_buf[e_tile(q + 1, fine + 1 if fine < FINE - 1 else FINE + 1), :]),
                jnp.where(level > 0, column(pltpu.roll(here, 1, 0)), 0.0),
                jnp.where(level < NZ - 1, column(pltpu.roll(here, NZ - 1, 0)), 0.0),
            ]
            total = parts[0] + parts[1] + parts[2] + parts[3] + parts[4] + parts[5]
            total = total + jnp.where(level == 0, marks, 0.0)
            inverse = jnp.where(marks > 0, 1.0 / jnp.where(marks > 0, total, 1.0), 0.0)
            for j, part in enumerate(parts):
                gs[q, fine, j] = part * inverse
            inverse = SCALE * inverse
            inv[q, fine] = inverse
            u_buf[q + 1, fine] = jnp.where(level == 0, inverse * flat_tile(spread_f, q, fine), 0.0)
        return 0

    lax.fori_loop(0, ROWS, faces, 0)
    for fine in range(FINE):
        u_buf[0, fine] = jnp.zeros((NZ, 128), F32)
        t_buf[0, fine] = jnp.zeros((NZ, 128), F32)
        t_buf[ROWS, fine] = jnp.zeros((NZ, 128), F32)

    def begin(buf):
        for fine in range(FINE):
            buf[ROWS + 1, fine] = pltpu.roll(buf[ROWS, fine], 64, 1)
        for k in range(CHUNK):
            row = ROWS - CHUNK + k + 1
            ext[k, 0] = pltpu.roll(buf[row, FINE - 1], 1, 1)
            ext[k, 1] = pltpu.roll(buf[row, 0], 127, 1)

    def apply(src, dst, centre, shift, first):
        n = lax.div(ROWS - first + CHUNK - 1, CHUNK)

        def chunk(i, _):
            q0 = ROWS - CHUNK * (i + 1)
            more = i + 1 < n
            ahead = jnp.maximum(q0 - CHUNK, 0)
            across = [(ext[k, 0], ext[k, 1]) for k in range(CHUNK)]
            later = []
            for k in range(CHUNK):
                row, again = ahead + k + 1, ROWS - CHUNK + k + 1
                up = jnp.where(more, src[row, FINE - 1], dst[again, FINE - 1])
                down = jnp.where(more, src[row, 0], dst[again, 0])
                later.append((pltpu.roll(up, 1, 1), pltpu.roll(down, 127, 1)))
            closing = [pltpu.roll(dst[ROWS, fine], 64, 1) for fine in range(FINE)]
            for k in range(CHUNK):
                q = q0 + k
                here = [src[q + 1, fine] for fine in range(FINE)]
                for fine in range(FINE):
                    before = here[fine - 1] if fine else across[k][0]
                    after = here[fine + 1] if fine < FINE - 1 else across[k][1]
                    new = (
                        (gs[q, fine, 0] * src[q, fine] + gs[q, fine, 1] * src[q + 2, fine])
                        + (gs[q, fine, 2] * before + gs[q, fine, 3] * after)
                        + (
                            gs[q, fine, 4] * pltpu.roll(here[fine], 1, 0)
                            + gs[q, fine, 5] * pltpu.roll(here[fine], NZ - 1, 0)
                        )
                    )
                    dst[q + 1, fine] = new + shift * (here[fine] if centre is src else centre[q + 1, fine])
            for k in range(CHUNK):
                ext[k, 0], ext[k, 1] = later[k]
            for fine in range(FINE):
                dst[ROWS + 1, fine] = closing[fine]
            return 0

        lax.fori_loop(0, n, chunk, 0)

    def pick(values, i):
        out = jnp.float32(values[0])
        for k in range(1, len(values)):
            out = jnp.where(i == k, jnp.float32(values[k]), out)
        return out

    def solve():
        begin(u_buf)
        apply(u_buf, t_buf, u_buf, jnp.float32(LINEAR), jnp.int32(2))

        def factor(i, _):
            apply(t_buf, u_buf, t_buf, pick(PS, i), 2 * i + 3)
            apply(u_buf, t_buf, t_buf, pick(QS, i), 2 * i + 4)
            return 0

        lax.fori_loop(0, len(PS), factor, 0)

    def columns(reduce):
        def body(i, _):
            for k in range(4):
                q = 4 * i + k
                for fine in range(FINE):
                    row = reduce(t_buf[WIDE + 1 + q, fine])
                    dlow[fine, pl.ds(q, 1), :] = row
                    dhigh[fine, pl.ds(NX // 2 - 1 - q, 1), :] = row
            return 0

        lax.fori_loop(0, NX // 8, body, 0)
        low = exact_dot(jnp.concatenate([dlow[fine] for fine in range(FINE)], axis=1), back[:, :256])
        high = exact_dot(jnp.concatenate([dhigh[fine] for fine in range(FINE)], axis=1), back[:, 256:])
        return (low[:, :128], low[:, 128:]), (high[:, :128], high[:, 128:])

    solve()
    top, bottom = columns(lambda row: jnp.sum(row, axis=0, keepdims=True))
    for k in range(2):
        depth[k, 0 : NX // 2, :] = top[k]
        depth[k, NX // 2 : NX, :] = bottom[k]
    weight = ice * obs[...]
    packed = jnp.zeros((NX, 128), F32)
    for k in range(2):
        field = weight * depth[k]
        rhs[k, own_rows, :] = field
        packed = jnp.where((lane >= 16 * k) & (lane < 16 * k + 16), turned(field, 16 * k), packed)
        at = 48 + 16 * k
        packed = jnp.where((lane >= at) & (lane < at + 16), turned(field, at - 112), packed)
    rhs_pack[...] = packed

    rhs_copies = to_neighbours(rhs, (rhs_pack, rhs_pack), (rhs_l, rhs_r), c_send, c_recv)
    start_all(rhs_copies)
    depth_out = pltpu.make_async_copy(depth, depth_ref.at[:, :, own_cols], local_sem.at[6])
    depth_out.start()
    depth_over = pltpu.make_async_remote_copy(
        depth,
        depth_ref.at[:, :, own_cols],
        swap_send.at[2],
        swap_recv.at[2],
        device_id=partner,
        device_id_type=MESH,
    )
    depth_over.start()

    arrived(rhs_copies)
    spread_pair(rhs, rhs_l, rhs_r)

    def start_rows(i, _):
        for k in range(4):
            q = 4 * i + k
            for fine in range(FINE):
                u_buf[q + 1, fine] = inv[q, fine] * flat_tile(spread_f, q, fine)
        return 0

    lax.fori_loop(0, ROWS // 4, start_rows, 0)
    solve()
    top, bottom = columns(lambda row: row[0:1, :])
    for half, pair in enumerate((top, bottom)):
        part = slice(half * NX // 2, (half + 1) * NX // 2)
        product = base[0, 0, part].astype(F32) * pair[0] + base[0, 1, part].astype(F32) * pair[1]
        hess[part, :] = -friction[part] * product
    hess_out = pltpu.make_async_copy(hess, hess_ref, local_sem.at[7])
    hess_out.start()

    for copies in (flat_copies, visc_copies, rhs_copies):
        sent(copies)
    depth_out.wait()
    depth_over.wait()
    hess_out.wait()


def solution(mesh):
    gx_n, gy_n = mesh.shape["gx"], mesh.shape["gy"]

    def step(viscosity, velocity, log_friction, step_dir, obs_weight, tile_mask, contact):
        any_space = pl.BlockSpec(memory_space=pl.ANY)
        vmem, dma = pltpu.VMEM, pltpu.SemaphoreType.DMA
        nd = len(DIRS)
        return pl.pallas_call(
            functools.partial(kernel, gx_n, gy_n),
            out_shape=(
                jax.ShapeDtypeStruct((2, NX, 2 * NY), F32),
                jax.ShapeDtypeStruct((NX, NY), F32),
            ),
            in_specs=[any_space] * 6 + [pl.BlockSpec(memory_space=pltpu.SMEM)],
            out_specs=(any_space, any_space),
            scratch_shapes=[
                vmem((NZ, XT, NY), BF16),
                vmem((XT, 128), BF16),
                vmem((XT, 128), BF16),
                vmem((NX, 128), BF16),
                vmem((NX, 128), BF16),
                vmem((2, 2, NX, NY), BF16),
                vmem((NX, NY), F32),
                vmem((NX, NY), F32),
                vmem((NX, NY), F32),
                vmem((NX, NY), jnp.int32),
                vmem((3, XT, NY), F32),
                vmem((NX, 128), F32),
                vmem((XT, 128), F32),
                vmem((XT, 128), F32),
                vmem((2, XT, NY), F32),
                vmem((NX, 128), F32),
                vmem((XT, 128), F32),
                vmem((XT, 128), F32),
                vmem((2, NX, NY), F32),
                vmem((NX, NY), F32),
                vmem((ROWS * NZ, 512), BF16),
                vmem(((ROWS + 2) * (FINE + 2) * NZ, 128), F32),
                vmem((FINE, ROWS, 128), F32),
                vmem((FINE, ROWS, 128), F32),
                vmem((FINE, NX // 2, 128), F32),
                vmem((FINE, NX // 2, 128), F32),
                vmem((512, (FINE + 2) * 128), BF16),
                vmem((768, FINE * 128), BF16),
                vmem((FINE * 128, 512), BF16),
                vmem((ROWS, FINE, 6, NZ, 128), F32),
                vmem((ROWS, FINE, NZ, 128), F32),
                vmem((CHUNK, 2, NZ, 128), F32),
                vmem((ROWS + 2, FINE, NZ, 128), F32),
                vmem((ROWS + 2, FINE, NZ, 128), F32),
                dma((8,)),
                dma((3,)),
                dma((3,)),
                dma((nd,)),
                dma((nd,)),
                dma((nd,)),
                dma((nd,)),
                dma((nd,)),
                dma((nd,)),
            ],
            compiler_params=pltpu.CompilerParams(
                collective_id=0, has_side_effects=True, vmem_limit_bytes=67043328
            ),
        )(viscosity, velocity, log_friction, step_dir, obs_weight, contact, tile_mask)

    in_specs = (
        P("gz", "gx", "gy"),
        P(None, "gz", "gx", "gy"),
        P("gx", "gy"),
        P("gx", "gy"),
        P("gx", "gy"),
        P("gx", "gy"),
        P("gx", "gy"),
    )
    out_specs = (P(None, "gx", "gy"), P("gx", ("gy", "gz")))
    return jax.shard_map(step, mesh=mesh, in_specs=in_specs, out_specs=out_specs, check_vma=False)
```

```python
import functools
import math

import jax
import jax.numpy as jnp
from jax import lax
from jax.experimental import pallas as pl
from jax.experimental.pallas import tpu as pltpu
from jax.sharding import PartitionSpec as P

MESH = pl.DeviceIdType.MESH
F32 = jnp.float32
BF16 = jnp.bfloat16

SWEEP = 8
ASPECT = 16.0
LOWER = 0.1
UPPER = 2.0
CENTRE = (UPPER + LOWER) / 2.0
HALF = (UPPER - LOWER) / 2.0
SIGMA = CENTRE / HALF

DELTA = CENTRE - 1.0
LINEAR = DELTA + CENTRE
ORDER = (3, 6, 1, 4, 5, 2, 7)
ANGLES = [math.pi * j / SWEEP for j in ORDER]
PS = [2.0 * DELTA - 2.0 * CENTRE * math.cos(t) for t in ANGLES]
QS = [
    DELTA * DELTA - 2.0 * CENTRE * DELTA * math.cos(t) + CENTRE * CENTRE - (HALF * math.sin(t)) ** 2
    for t in ANGLES
]
TOP = math.cosh(SWEEP * math.acosh(SIGMA))
SCALE = 2.0 ** (2 * SWEEP - 2) / (TOP * TOP) / HALF ** (2 * SWEEP)

WIDE = 16
NX, NY, NZ = 64, 128, 8
XT, YT = NX + 2 * WIDE, NY + 2 * WIDE
LOTS = 4
ROWS = XT // LOTS
BLOCKS = 128 // LOTS
FINE = YT // BLOCKS
DIRS = [(dx, dy) for dx in (-1, 0, 1) for dy in (-1, 0, 1) if (dx, dy) != (0, 0)]
R_AT, L_AT = 32, 80
ROW_ORDER = [ROWS - 1, *range(8), *range(ROWS - 2, 15, -1), *range(8, 16)]
LATE = range(12, 16)


def lanes_of(shape):
    return lax.broadcasted_iota(jnp.int32, shape, len(shape) - 1)


def turned(value, by):
    by %= 128
    return value if by == 0 else pltpu.roll(value, by, value.ndim - 1)


def one_in(rows, target):
    return (lax.broadcasted_iota(jnp.int32, (rows, 128), 0) == target).astype(F32).astype(BF16)


def chooser(fine):
    n = lanes_of((1, 128))
    y = FINE * (n % BLOCKS) + fine
    edge = jnp.where(y < WIDE, 128 + L_AT + y, 128 + R_AT + y - WIDE - NY)
    k = 256 * (n // BLOCKS) + jnp.where((y >= WIDE) & (y < WIDE + NY), y - WIDE, edge)
    return one_in(256 * LOTS, jnp.where((y >= 0) & (y < YT), k, -1))


def returner(lot):
    y = lanes_of((1, 128)) + WIDE
    return one_in(FINE * 128, (y % FINE) * 128 + BLOCKS * lot + y // FINE)


def thirds(value):
    high = value.astype(BF16)
    rest = value - high.astype(F32)
    middle = rest.astype(BF16)
    return high, middle, (rest - middle.astype(F32)).astype(BF16)


def dot(a, b):
    return jnp.dot(a, b, preferred_element_type=F32)


def exact_dot(value, matrix):
    n = value.shape[0]
    out = dot(jnp.concatenate(thirds(value), axis=0), matrix)
    return out[:n] + out[n : 2 * n] + out[2 * n :]


def kernel(
    gx_n,
    gy_n,
    visc_ref,
    vel_ref,
    logf_ref,
    step_ref,
    obs_ref,
    contact_ref,
    tile_ref,
    depth_ref,
    hess_ref,
    visc,
    edge_l,
    edge_r,
    pack_l,
    pack_r,
    base,
    logf,
    step,
    obs,
    contact,
    flat,
    flat_pack,
    flat_l,
    flat_r,
    rhs,
    rhs_pack,
    rhs_l,
    rhs_r,
    depth,
    hess,
    mult,
    left,
    e_buf,
    spread,
    sums,
    place,
    back,
    gs,
    inv,
    u_ext,
    t_ext,
    u_buf,
    t_buf,
    classes,
    local_sem,
    swap_send,
    swap_recv,
    a_send,
    a_recv,
    b_send,
    b_recv,
    c_send,
    c_recv,
):
    gx, gy, gz = lax.axis_index("gx"), lax.axis_index("gy"), lax.axis_index("gz")
    yb = 2 * gy + gz
    y_n = 2 * gy_n

    def there(dx, dy):
        nx, ny = gx + dx, yb + dy
        return (nx >= 0) & (nx < gx_n) & (ny >= 0) & (ny < y_n)

    def device(dx, dy):
        ny = yb + dy
        return (gx + dx, lax.div(ny, 2), lax.rem(ny, 2))

    own_cols = pl.ds(pl.multiple_of(gz * NY, NY), NY)
    other_cols = pl.ds(pl.multiple_of((1 - gz) * NY, NY), NY)
    own_rows = pl.ds(WIDE, NX)
    layers = visc_ref.shape[0]
    mine = pl.ds(gz * layers, layers)
    partner = (gx, gy, 1 - gz)

    local = [
        pltpu.make_async_copy(visc_ref.at[:, :, own_cols], visc.at[mine, own_rows], local_sem.at[0]),
        pltpu.make_async_copy(vel_ref.at[:, 0, :, own_cols], base.at[gz], local_sem.at[1]),
        pltpu.make_async_copy(logf_ref.at[:, own_cols], logf, local_sem.at[2]),
        pltpu.make_async_copy(step_ref.at[:, own_cols], step, local_sem.at[3]),
        pltpu.make_async_copy(contact_ref.at[:, own_cols], contact, local_sem.at[4]),
        pltpu.make_async_copy(obs_ref.at[:, own_cols], obs, local_sem.at[5]),
        pltpu.make_async_copy(tile_ref, classes, local_sem.at[6]),
    ]
    for copy in local:
        copy.start()

    barrier = pltpu.get_barrier_semaphore()
    met = 0
    for d in DIRS:
        here = there(*d)
        met = met + here.astype(jnp.int32)

        @pl.when(here)
        def _():
            pl.semaphore_signal(barrier, inc=1, device_id=device(*d), device_id_type=MESH)

    @pl.when(gx == 0)
    def _():
        visc[:, 0:WIDE, :] = jnp.zeros((NZ, WIDE, NY), BF16)
        flat[:, 0:WIDE, :] = jnp.zeros((3, WIDE, NY), F32)
        rhs[:, 0:WIDE, :] = jnp.zeros((2, WIDE, NY), F32)

    @pl.when(gx == gx_n - 1)
    def _():
        visc[:, XT - WIDE : XT, :] = jnp.zeros((NZ, WIDE, NY), BF16)
        flat[:, XT - WIDE : XT, :] = jnp.zeros((3, WIDE, NY), F32)
        rhs[:, XT - WIDE : XT, :] = jnp.zeros((2, WIDE, NY), F32)

    for dy, ends in ((-1, (edge_l, flat_l, rhs_l)), (1, (edge_r, flat_r, rhs_r))):
        for dx, first, count in ((-1, 0, WIDE), (0, WIDE, NX), (1, WIDE + NX, WIDE)):

            @pl.when(jnp.logical_not(there(dx, dy)))
            def _():
                for end in ends[:2]:
                    end[first : first + count, :] = jnp.zeros((count, 128), end.dtype)
                ends[2][:, first : first + count, :] = jnp.zeros((2, count, 128), F32)

    for tile, fine in enumerate((*range(FINE), -1, FINE)):
        place[:, 128 * tile : 128 * tile + 128] = chooser(fine)
    for lot in range(LOTS):
        back[:, 128 * lot : 128 * lot + 128] = returner(lot)

    pl.semaphore_wait(barrier, met)

    swap = [
        pltpu.make_async_remote_copy(
            visc_ref.at[:, :, other_cols],
            visc.at[mine, own_rows],
            swap_send.at[0],
            swap_recv.at[0],
            device_id=partner,
            device_id_type=MESH,
        ),
        pltpu.make_async_remote_copy(
            vel_ref.at[:, 0, :, other_cols],
            base.at[gz],
            swap_send.at[1],
            swap_recv.at[1],
            device_id=partner,
            device_id_type=MESH,
        ),
    ]
    for copy in swap:
        copy.start()

    for copy in local[1:]:
        copy.wait()

    lane = lanes_of((NX, NY))
    left_class, right_class = classes[0, 2 * gz], classes[0, 2 * gz + 1]
    kinds = jnp.where(lane < NY // 2, left_class, right_class)
    ice = (kinds > 0).astype(F32)
    friction = jnp.exp(logf[...]) * (kinds == 2).astype(F32) * contact[...].astype(F32)
    marked = jnp.where(kinds > 0, jnp.maximum(friction, 1e-30), 0.0)
    flat[2, own_rows, :] = marked

    swap[1].wait()
    drive = -(friction * step[...])
    flat[0, own_rows, :] = drive * base[0, 0].astype(F32)
    flat[1, own_rows, :] = drive * base[0, 1].astype(F32)

    def with_edges(packed, field, shift):
        for at, first in ((R_AT - shift, 0), (L_AT - shift, NY - WIDE)):
            packed = jnp.where((lane >= at) & (lane < at + WIDE), turned(field, at - first), packed)
        return packed

    packed = jnp.zeros((NX, 128), F32)
    for i in range(3):
        packed = with_edges(packed, flat[i, own_rows, :], 32 - 16 * i)
    flat_pack[...] = packed

    def extent(dx):
        if dx == 0:
            return pl.ds(WIDE, NX), pl.ds(0, NX), pl.ds(WIDE, NX)
        if dx < 0:
            return pl.ds(WIDE, WIDE), pl.ds(0, WIDE), pl.ds(WIDE + NX, WIDE)
        return pl.ds(NX, WIDE), pl.ds(NX - WIDE, WIDE), pl.ds(0, WIDE)

    def to_neighbours(block, packs, lands, send, recv):
        copies = []
        for i, (dx, dy) in enumerate(DIRS):
            src, src_pack, dst = extent(dx)
            if dy == 0:
                pair = (block.at[:, src, :], block.at[:, dst, :])
            elif dy < 0:
                pair = (packs[0].at[src_pack, :], lands[1].at[dst, :])
            else:
                pair = (packs[1].at[src_pack, :], lands[0].at[dst, :])
            copies.append(
                pltpu.make_async_remote_copy(
                    *pair,
                    send.at[i],
                    recv.at[i],
                    device_id=device(dx, dy),
                    device_id_type=MESH,
                )
            )
        return copies

    def start_all(copies):
        for (dx, dy), copy in zip(DIRS, copies):
            pl.when(there(dx, dy))(copy.start)

    def arrived(copies):
        for (dx, dy), copy in zip(DIRS, copies):
            pl.when(there(-dx, -dy))(copy.wait_recv)

    def sent(copies):
        for (dx, dy), copy in zip(DIRS, copies):
            pl.when(there(dx, dy))(copy.wait_send)

    flat_copies = to_neighbours(flat, (flat_pack, flat_pack), (flat_l, flat_r), b_send, b_recv)
    start_all(flat_copies)

    local[0].wait()
    swap[0].wait()

    def pack_rows(i, _):
        rows = pl.ds(pl.multiple_of(i * 16, 16), 16)
        here = pl.ds(pl.multiple_of(WIDE + i * 16, 16), 16)
        spot = lanes_of((16, 128))
        low = jnp.zeros((16, 128), F32)
        high = jnp.zeros((16, 128), F32)
        for layer in range(NZ):
            e = visc[layer, here, :].astype(F32)
            inside = (spot >= 16 * layer) & (spot < 16 * layer + 16)
            low = jnp.where(inside, turned(e, 16 * layer), low)
            high = jnp.where(inside, turned(e, 16 * layer + 16), high)
        pack_l[rows, :] = low.astype(BF16)
        pack_r[rows, :] = high.astype(BF16)
        return 0

    lax.fori_loop(0, NX // 16, pack_rows, 0)
    visc_copies = to_neighbours(visc, (pack_l, pack_r), (edge_l, edge_r), a_send, a_recv)
    start_all(visc_copies)

    arrived(flat_copies)
    arrived(visc_copies)

    spot = lanes_of((XT, 128))

    def in_lots(own, edge):
        return jnp.concatenate(
            [part[ROWS * lot : ROWS * lot + ROWS] for lot in range(LOTS) for part in (own, edge)], axis=1
        )

    ends_l, ends_r = edge_l[...].astype(F32), edge_r[...].astype(F32)
    for layer in range(NZ):
        edge = jnp.where(spot < 64, turned(ends_r, R_AT - 16 * layer), turned(ends_l, L_AT - 16 * layer))
        left[ROWS * layer : ROWS * layer + ROWS, :] = in_lots(visc[layer].astype(F32), edge)

    tiles = FINE + 2
    rows_in = left[...].astype(BF16)
    for tile in range(tiles):
        placed = 0.5 * dot(rows_in, place[:, 128 * tile : 128 * tile + 128])
        for layer in range(NZ):
            e_buf[pl.ds(tiles * NZ + tile * NZ + layer, ROWS, stride=tiles * NZ), :] = placed[
                ROWS * layer : ROWS * layer + ROWS
            ]

    def e_tile(row, tile):
        return pl.ds(pl.multiple_of((row * tiles + tile) * NZ, NZ), NZ)

    for fine in range(FINE):
        e_buf[e_tile(0, fine), :] = pltpu.roll(e_buf[e_tile(ROWS, fine), :], BLOCKS, 1)
        e_buf[e_tile(ROWS + 1, fine), :] = pltpu.roll(e_buf[e_tile(1, fine), :], 128 - BLOCKS, 1)

    def put(i, placed):
        for fine in range(FINE):
            spread[i, fine] = placed[:, 128 * fine : 128 * fine + 128]

    ends = jnp.where(spot < 48, flat_r[...], flat_l[...])
    flat_rows = jnp.concatenate([in_lots(flat[i], turned(ends, 32 - 16 * i)) for i in range(3)], axis=0)
    placed = exact_dot(flat_rows, place[:, : 128 * FINE])
    for i in range(3):
        put(i, placed[ROWS * i : ROWS * i + ROWS])

    level = lax.broadcasted_iota(jnp.int32, (NZ, 128), 0)

    def flat_tile(i, q, fine):
        return jnp.broadcast_to(spread[i, fine, pl.ds(q, 1), :], (NZ, 128))

    def faces(q, _):
        for fine in range(FINE):
            here = e_buf[e_tile(q + 1, fine), :]

            def side(beside):
                return here + jnp.where(beside > 0, beside, here)

            def column(beside):
                return ASPECT * (here + beside)

            marks = flat_tile(2, q, fine)
            parts = [
                side(e_buf[e_tile(q, fine), :]),
                side(e_buf[e_tile(q + 2, fine), :]),
                side(e_buf[e_tile(q + 1, fine - 1 if fine else FINE), :]),
                side(e_buf[e_tile(q + 1, fine + 1 if fine < FINE - 1 else FINE + 1), :]),
                jnp.where(level > 0, column(pltpu.roll(here, 1, 0)), 0.0),
                jnp.where(level < NZ - 1, column(pltpu.roll(here, NZ - 1, 0)), 0.0),
            ]
            total = parts[0] + parts[1] + parts[2] + parts[3] + parts[4] + parts[5]
            total = total + jnp.where(level == 0, marks, 0.0)
            inverse = jnp.where(marks > 0, 1.0 / jnp.where(marks > 0, total, 1.0), 0.0)
            for j, part in enumerate(parts):
                gs[q, fine, j] = part * inverse
            inv[q, fine] = SCALE * inverse
        return 0

    lax.fori_loop(0, ROWS, faces, 0)

    def across(buf, row):
        return pltpu.roll(buf[row, FINE - 1], 1, 1), pltpu.roll(buf[row, 0], 127, 1)

    def apply(src, src_ext, dst, dst_ext, centre, shift):
        found = {q: across(src, q + 1) for q in ROW_ORDER if q in LATE}
        for q in ROW_ORDER:
            here = [src[q + 1, fine] for fine in range(FINE)]
            sides = found[q] if q in LATE else (src_ext[q, 0], src_ext[q, 1])
            row = []
            for fine in range(FINE):
                before = here[fine - 1] if fine else sides[0]
                after = here[fine + 1] if fine < FINE - 1 else sides[1]
                new = (
                    (gs[q, fine, 0] * src[q, fine] + gs[q, fine, 1] * src[q + 2, fine])
                    + (gs[q, fine, 2] * before + gs[q, fine, 3] * after)
                    + (
                        gs[q, fine, 4] * pltpu.roll(here[fine], 1, 0)
                        + gs[q, fine, 5] * pltpu.roll(here[fine], NZ - 1, 0)
                    )
                )
                new = new + shift * (here[fine] if centre is src else centre[q + 1, fine])
                dst[q + 1, fine] = new
                row.append(new)
            if q not in LATE:
                dst_ext[q, 0], dst_ext[q, 1] = pltpu.roll(row[FINE - 1], 1, 1), pltpu.roll(row[0], 127, 1)
            if q == ROWS - 1:
                for fine in range(FINE):
                    dst[0, fine] = pltpu.roll(row[fine], BLOCKS, 1)
            if q == 0:
                for fine in range(FINE):
                    dst[ROWS + 1, fine] = pltpu.roll(row[fine], 128 - BLOCKS, 1)

    def pick(values, i):
        out = jnp.float32(values[0])
        for k in range(1, len(values)):
            out = jnp.where(i == k, jnp.float32(values[k]), out)
        return out

    def solve(i, floor_only):
        def start_rows(j, _):
            for m in range(4):
                q = 4 * j + m
                for fine in range(FINE):
                    value = inv[q, fine] * flat_tile(i, q, fine)
                    u_buf[q + 1, fine] = jnp.where((level == 0) | jnp.logical_not(floor_only), value, 0.0)
            return 0

        lax.fori_loop(0, ROWS // 4, start_rows, 0)
        for fine in range(FINE):
            u_buf[0, fine] = pltpu.roll(u_buf[ROWS, fine], BLOCKS, 1)
            u_buf[ROWS + 1, fine] = pltpu.roll(u_buf[1, fine], 128 - BLOCKS, 1)
        for q in range(ROWS):
            if q not in LATE:
                u_ext[q, 0], u_ext[q, 1] = across(u_buf, q + 1)

        apply(u_buf, u_ext, t_buf, t_ext, u_buf, jnp.float32(LINEAR))

        def factor(j, _):
            apply(t_buf, t_ext, u_buf, u_ext, t_buf, pick(PS, j))
            apply(u_buf, u_ext, t_buf, t_ext, t_buf, pick(QS, j))
            return 0

        lax.fori_loop(0, len(PS), factor, 0)

    def own_columns():
        out = exact_dot(jnp.concatenate([sums[fine] for fine in range(FINE)], axis=1), back[...])
        cut = [slice(WIDE, ROWS), slice(0, ROWS), slice(0, ROWS), slice(0, ROWS - WIDE)]
        return jnp.concatenate([out[rows, 128 * lot : 128 * lot + 128] for lot, rows in enumerate(cut)], axis=0)

    def fold(reduce):
        for q in range(ROWS):
            for fine in range(FINE):
                sums[fine, q : q + 1, :] = reduce(t_buf[q + 1, fine])

    weight = ice * obs[...]

    def rhs_copies(c):
        packs = rhs_pack.at[c]
        return to_neighbours(
            rhs.at[pl.ds(c, 1)], (packs, packs), (rhs_l.at[c], rhs_r.at[c]), c_send.at[c], c_recv.at[c]
        )

    def depth_copies(c):
        here = pltpu.make_async_copy(depth.at[c], depth_ref.at[c, :, own_cols], local_sem.at[8 + c])
        there_too = pltpu.make_async_remote_copy(
            depth.at[c],
            depth_ref.at[c, :, own_cols],
            swap_send.at[2 + c],
            swap_recv.at[2 + c],
            device_id=partner,
            device_id_type=MESH,
        )
        return here, there_too

    def phase(p, _):
        c = lax.rem(p, 2)
        forward = p < 2

        @pl.when(jnp.logical_not(forward))
        def _():
            arrived(rhs_copies(c))
            edge = jnp.where(spot < 64, rhs_r[c], rhs_l[c])
            put(c, exact_dot(in_lots(rhs[c], edge), place[:, : 128 * FINE]))

        solve(c, forward)

        @pl.when(forward)
        def _():
            fold(lambda tile: jnp.sum(tile, axis=0, keepdims=True))
            field = own_columns()
            depth[c] = field
            field = weight * field
            rhs[c, own_rows, :] = field
            rhs_pack[c] = with_edges(jnp.zeros((NX, 128), F32), field, 0)
            start_all(rhs_copies(c))
            for copy in depth_copies(c):
                copy.start()

        @pl.when(jnp.logical_not(forward))
        def _():
            fold(lambda tile: tile[0:1, :])
            mult[c] = own_columns()

        return 0

    lax.fori_loop(0, 4, phase, 0)

    hess[...] = -friction * (base[0, 0].astype(F32) * mult[0] + base[0, 1].astype(F32) * mult[1])
    hess_out = pltpu.make_async_copy(hess, hess_ref, local_sem.at[7])
    hess_out.start()

    for copies in (flat_copies, visc_copies, rhs_copies(0), rhs_copies(1)):
        sent(copies)
    for c in range(2):
        for copy in depth_copies(c):
            copy.wait()
    hess_out.wait()


def solution(mesh):
    gx_n, gy_n = mesh.shape["gx"], mesh.shape["gy"]

    def step(viscosity, velocity, log_friction, step_dir, obs_weight, tile_mask, contact):
        any_space = pl.BlockSpec(memory_space=pl.ANY)
        vmem, dma = pltpu.VMEM, pltpu.SemaphoreType.DMA
        nd = len(DIRS)
        return pl.pallas_call(
            functools.partial(kernel, gx_n, gy_n),
            out_shape=(
                jax.ShapeDtypeStruct((2, NX, 2 * NY), F32),
                jax.ShapeDtypeStruct((NX, NY), F32),
            ),
            in_specs=[any_space] * 7,
            out_specs=(any_space, any_space),
            scratch_shapes=[
                vmem((NZ, XT, NY), BF16),
                vmem((XT, 128), BF16),
                vmem((XT, 128), BF16),
                vmem((NX, 128), BF16),
                vmem((NX, 128), BF16),
                vmem((2, 2, NX, NY), BF16),
                vmem((NX, NY), F32),
                vmem((NX, NY), F32),
                vmem((NX, NY), F32),
                vmem((NX, NY), jnp.int32),
                vmem((3, XT, NY), F32),
                vmem((NX, 128), F32),
                vmem((XT, 128), F32),
                vmem((XT, 128), F32),
                vmem((2, XT, NY), F32),
                vmem((2, NX, 128), F32),
                vmem((2, XT, 128), F32),
                vmem((2, XT, 128), F32),
                vmem((2, NX, NY), F32),
                vmem((NX, NY), F32),
                vmem((2, NX, NY), F32),
                vmem((ROWS * NZ, 256 * LOTS), F32),
                vmem(((ROWS + 2) * (FINE + 2) * NZ, 128), F32),
                vmem((3, FINE, ROWS, 128), F32),
                vmem((FINE, ROWS, 128), F32),
                vmem((256 * LOTS, (FINE + 2) * 128), BF16),
                vmem((FINE * 128, 128 * LOTS), BF16),
                vmem((ROWS, FINE, 6, NZ, 128), F32),
                vmem((ROWS, FINE, NZ, 128), F32),
                vmem((ROWS, 2, NZ, 128), F32),
                vmem((ROWS, 2, NZ, 128), F32),
                vmem((ROWS + 2, FINE, NZ, 128), F32),
                vmem((ROWS + 2, FINE, NZ, 128), F32),
                pltpu.SMEM((1, 4), jnp.int32),
                dma((10,)),
                dma((4,)),
                dma((4,)),
                dma((nd,)),
                dma((nd,)),
                dma((nd,)),
                dma((nd,)),
                dma((2, nd)),
                dma((2, nd)),
            ],
            compiler_params=pltpu.CompilerParams(
                collective_id=0, has_side_effects=True, vmem_limit_bytes=67043328
            ),
        )(viscosity, velocity, log_friction, step_dir, obs_weight, contact, tile_mask)

    in_specs = (
        P("gz", "gx", "gy"),
        P(None, "gz", "gx", "gy"),
        P("gx", "gy"),
        P("gx", "gy"),
        P("gx", "gy"),
        P("gx", "gy"),
        P("gx", "gy"),
    )
    out_specs = (P(None, "gx", "gy"), P("gx", ("gy", "gz")))
    return jax.shard_map(step, mesh=mesh, in_specs=in_specs, out_specs=out_specs, check_vma=False)
```

```python
import functools
import math

import jax
import jax.numpy as jnp
from jax import lax
from jax.experimental import pallas as pl
from jax.experimental.pallas import tpu as pltpu
from jax.sharding import PartitionSpec as P

MESH = pl.DeviceIdType.MESH
F32 = jnp.float32
BF16 = jnp.bfloat16

SWEEP = 8
ASPECT = 16.0
LOWER = 0.1
UPPER = 2.0
CENTRE = (UPPER + LOWER) / 2.0
HALF = (UPPER - LOWER) / 2.0
SIGMA = CENTRE / HALF

DELTA = CENTRE - 1.0
LINEAR = DELTA + CENTRE
ORDER = (3, 6, 1, 4, 5, 2, 7)
ANGLES = [math.pi * j / SWEEP for j in ORDER]
PS = [2.0 * DELTA - 2.0 * CENTRE * math.cos(t) for t in ANGLES]
QS = [
    DELTA * DELTA - 2.0 * CENTRE * DELTA * math.cos(t) + CENTRE * CENTRE - (HALF * math.sin(t)) ** 2
    for t in ANGLES
]
TOP = math.cosh(SWEEP * math.acosh(SIGMA))
SCALE = 2.0 ** (2 * SWEEP - 2) / (TOP * TOP) / HALF ** (2 * SWEEP)

WIDE = 16
NX, NY, NZ = 64, 128, 8
XT, YT = NX + 2 * WIDE, NY + 2 * WIDE
LOTS = 4
ROWS = XT // LOTS
BLOCKS = 128 // LOTS
FINE = YT // BLOCKS
DIRS = [(-1, -1), (-1, 1), (1, -1), (1, 1), (-1, 0), (1, 0), (0, -1), (0, 1)]
R_AT, L_AT = 32, 80
ROW_ORDER = [ROWS - 1, *range(8), *range(ROWS - 2, 15, -1), *range(8, 16)]
LATE = range(12, 16)


def lanes_of(shape):
    return lax.broadcasted_iota(jnp.int32, shape, len(shape) - 1)


def turned(value, by):
    by %= 128
    return value if by == 0 else pltpu.roll(value, by, value.ndim - 1)


def one_in(rows, target):
    return (lax.broadcasted_iota(jnp.int32, (rows, 128), 0) == target).astype(F32).astype(BF16)


def chooser(fine):
    n = lanes_of((1, 128))
    y = FINE * (n % BLOCKS) + fine
    edge = jnp.where(y < WIDE, 128 + L_AT + y, 128 + R_AT + y - WIDE - NY)
    k = 256 * (n // BLOCKS) + jnp.where((y >= WIDE) & (y < WIDE + NY), y - WIDE, edge)
    return one_in(256 * LOTS, jnp.where((y >= 0) & (y < YT), k, -1))


def returner(lot):
    y = lanes_of((1, 128)) + WIDE
    return one_in(FINE * 128, (y % FINE) * 128 + BLOCKS * lot + y // FINE)


def thirds(value):
    high = value.astype(BF16)
    rest = value - high.astype(F32)
    middle = rest.astype(BF16)
    return high, middle, (rest - middle.astype(F32)).astype(BF16)


def dot(a, b):
    return jnp.dot(a, b, preferred_element_type=F32)


def exact_dot(value, matrix):
    n = value.shape[0]
    out = dot(jnp.concatenate(thirds(value), axis=0), matrix)
    return out[:n] + out[n : 2 * n] + out[2 * n :]


def kernel(
    gx_n,
    gy_n,
    visc_ref,
    vel_ref,
    logf_ref,
    step_ref,
    obs_ref,
    contact_ref,
    tile_ref,
    depth_ref,
    hess_ref,
    visc,
    edge_l,
    edge_r,
    pack_l,
    pack_r,
    base,
    logf,
    step,
    obs,
    contact,
    flat,
    flat_pack,
    flat_l,
    flat_r,
    rhs,
    rhs_pack,
    rhs_l,
    rhs_r,
    depth,
    hess,
    mult,
    left,
    e_buf,
    spread,
    sums,
    place,
    back,
    gs,
    inv,
    u_ext,
    t_ext,
    u_buf,
    t_buf,
    classes,
    local_sem,
    swap_send,
    swap_recv,
    a_send,
    a_recv,
    b_send,
    b_recv,
    c_send,
    c_recv,
):
    gx, gy, gz = lax.axis_index("gx"), lax.axis_index("gy"), lax.axis_index("gz")
    yb = 2 * gy + gz
    y_n = 2 * gy_n

    def there(dx, dy):
        nx, ny = gx + dx, yb + dy
        return (nx >= 0) & (nx < gx_n) & (ny >= 0) & (ny < y_n)

    def device(dx, dy):
        ny = yb + dy
        return (gx + dx, lax.div(ny, 2), lax.rem(ny, 2))

    own_cols = pl.ds(pl.multiple_of(gz * NY, NY), NY)
    other_cols = pl.ds(pl.multiple_of((1 - gz) * NY, NY), NY)
    own_rows = pl.ds(WIDE, NX)
    layers = visc_ref.shape[0]
    mine = pl.ds(gz * layers, layers)
    partner = (gx, gy, 1 - gz)

    local = [
        pltpu.make_async_copy(visc_ref.at[:, :, own_cols], visc.at[mine, own_rows], local_sem.at[0]),
        pltpu.make_async_copy(vel_ref.at[:, 0, :, own_cols], base.at[gz], local_sem.at[1]),
        pltpu.make_async_copy(logf_ref.at[:, own_cols], logf, local_sem.at[2]),
        pltpu.make_async_copy(step_ref.at[:, own_cols], step, local_sem.at[3]),
        pltpu.make_async_copy(contact_ref.at[:, own_cols], contact, local_sem.at[4]),
        pltpu.make_async_copy(obs_ref.at[:, own_cols], obs, local_sem.at[5]),
        pltpu.make_async_copy(tile_ref, classes, local_sem.at[6]),
    ]
    for copy in local:
        copy.start()

    barrier = pltpu.get_barrier_semaphore()
    met = 0
    for d in DIRS:
        here = there(*d)
        met = met + here.astype(jnp.int32)

        @pl.when(here)
        def _():
            pl.semaphore_signal(barrier, inc=1, device_id=device(*d), device_id_type=MESH)

    @pl.when(gx == 0)
    def _():
        visc[:, 0:WIDE, :] = jnp.zeros((NZ, WIDE, NY), BF16)
        flat[:, 0:WIDE, :] = jnp.zeros((3, WIDE, NY), F32)
        rhs[:, 0:WIDE, :] = jnp.zeros((2, WIDE, NY), F32)

    @pl.when(gx == gx_n - 1)
    def _():
        visc[:, XT - WIDE : XT, :] = jnp.zeros((NZ, WIDE, NY), BF16)
        flat[:, XT - WIDE : XT, :] = jnp.zeros((3, WIDE, NY), F32)
        rhs[:, XT - WIDE : XT, :] = jnp.zeros((2, WIDE, NY), F32)

    for dy, ends in ((-1, (edge_l, flat_l, rhs_l)), (1, (edge_r, flat_r, rhs_r))):
        for dx, first, count in ((-1, 0, WIDE), (0, WIDE, NX), (1, WIDE + NX, WIDE)):

            @pl.when(jnp.logical_not(there(dx, dy)))
            def _():
                for end in ends[:2]:
                    end[first : first + count, :] = jnp.zeros((count, 128), end.dtype)
                ends[2][:, first : first + count, :] = jnp.zeros((2, count, 128), F32)

    for tile, fine in enumerate((*range(FINE), -1, FINE)):
        place[:, 128 * tile : 128 * tile + 128] = chooser(fine)
    for lot in range(LOTS):
        back[:, 128 * lot : 128 * lot + 128] = returner(lot)

    for copy in local[1:]:
        copy.wait()

    lane = lanes_of((NX, NY))
    left_class, right_class = classes[0, 2 * gz], classes[0, 2 * gz + 1]
    kinds = jnp.where(lane < NY // 2, left_class, right_class)
    ice = (kinds > 0).astype(F32)
    friction = jnp.exp(logf[...]) * (kinds == 2).astype(F32) * contact[...].astype(F32)
    marked = jnp.where(kinds > 0, jnp.maximum(friction, 1e-30), 0.0)
    flat[2, own_rows, :] = marked
    drive = -(friction * step[...])

    pl.semaphore_wait(barrier, met)

    swap = [
        pltpu.make_async_remote_copy(
            visc_ref.at[:, :, other_cols],
            visc.at[mine, own_rows],
            swap_send.at[0],
            swap_recv.at[0],
            device_id=partner,
            device_id_type=MESH,
        ),
        pltpu.make_async_remote_copy(
            vel_ref.at[:, 0, :, other_cols],
            base.at[gz],
            swap_send.at[1],
            swap_recv.at[1],
            device_id=partner,
            device_id_type=MESH,
        ),
    ]
    for copy in swap:
        copy.start()

    def with_edges(packed, field, shift):
        for at, first in ((R_AT - shift, 0), (L_AT - shift, NY - WIDE)):
            packed = jnp.where((lane >= at) & (lane < at + WIDE), turned(field, at - first), packed)
        return packed

    def extent(dx):
        if dx == 0:
            return pl.ds(WIDE, NX), pl.ds(0, NX), pl.ds(WIDE, NX)
        if dx < 0:
            return pl.ds(WIDE, WIDE), pl.ds(0, WIDE), pl.ds(WIDE + NX, WIDE)
        return pl.ds(NX, WIDE), pl.ds(NX - WIDE, WIDE), pl.ds(0, WIDE)

    def to_neighbours(block, packs, lands, send, recv):
        copies = []
        for i, (dx, dy) in enumerate(DIRS):
            src, src_pack, dst = extent(dx)
            if dy == 0:
                pair = (block.at[:, src, :], block.at[:, dst, :])
            elif dy < 0:
                pair = (packs[0].at[src_pack, :], lands[1].at[dst, :])
            else:
                pair = (packs[1].at[src_pack, :], lands[0].at[dst, :])
            copies.append(
                pltpu.make_async_remote_copy(
                    *pair,
                    send.at[i],
                    recv.at[i],
                    device_id=device(dx, dy),
                    device_id_type=MESH,
                )
            )
        return copies

    def start_all(copies):
        for (dx, dy), copy in zip(DIRS, copies):
            pl.when(there(dx, dy))(copy.start)

    def arrived(copies):
        for (dx, dy), copy in zip(DIRS, copies):
            pl.when(there(-dx, -dy))(copy.wait_recv)

    def sent(copies):
        for (dx, dy), copy in zip(DIRS, copies):
            pl.when(there(dx, dy))(copy.wait_send)

    local[0].wait()
    swap[0].wait()

    low = jnp.zeros((NX, 128), F32)
    high = jnp.zeros((NX, 128), F32)
    for layer in range(NZ):
        e = visc[layer, own_rows, :].astype(F32)
        inside = (lane >= 16 * layer) & (lane < 16 * layer + 16)
        low = jnp.where(inside, turned(e, 16 * layer), low)
        high = jnp.where(inside, turned(e, 16 * layer + 16), high)
    pack_l[...] = low.astype(BF16)
    pack_r[...] = high.astype(BF16)
    visc_copies = to_neighbours(visc, (pack_l, pack_r), (edge_l, edge_r), a_send, a_recv)
    start_all(visc_copies)

    swap[1].wait()
    flat[0, own_rows, :] = drive * base[0, 0].astype(F32)
    flat[1, own_rows, :] = drive * base[0, 1].astype(F32)
    packed = jnp.zeros((NX, 128), F32)
    for i in range(3):
        packed = with_edges(packed, flat[i, own_rows, :], 32 - 16 * i)
    flat_pack[...] = packed
    flat_copies = to_neighbours(flat, (flat_pack, flat_pack), (flat_l, flat_r), b_send, b_recv)
    start_all(flat_copies)

    arrived(visc_copies)

    spot = lanes_of((XT, 128))

    def in_lots(own, edge):
        return jnp.concatenate(
            [part[ROWS * lot : ROWS * lot + ROWS] for lot in range(LOTS) for part in (own, edge)], axis=1
        )

    ends_l, ends_r = edge_l[...].astype(F32), edge_r[...].astype(F32)
    for layer in range(NZ):
        edge = jnp.where(spot < 64, turned(ends_r, R_AT - 16 * layer), turned(ends_l, L_AT - 16 * layer))
        left[ROWS * layer : ROWS * layer + ROWS, :] = in_lots(visc[layer].astype(F32), edge)

    tiles = FINE + 2
    rows_in = left[...].astype(BF16)
    for tile in range(tiles):
        placed = 0.5 * dot(rows_in, place[:, 128 * tile : 128 * tile + 128])
        for layer in range(NZ):
            e_buf[pl.ds(tiles * NZ + tile * NZ + layer, ROWS, stride=tiles * NZ), :] = placed[
                ROWS * layer : ROWS * layer + ROWS
            ]

    def e_tile(row, tile):
        return pl.ds(pl.multiple_of((row * tiles + tile) * NZ, NZ), NZ)

    for fine in range(FINE):
        e_buf[e_tile(0, fine), :] = pltpu.roll(e_buf[e_tile(ROWS, fine), :], BLOCKS, 1)
        e_buf[e_tile(ROWS + 1, fine), :] = pltpu.roll(e_buf[e_tile(1, fine), :], 128 - BLOCKS, 1)

    def put(i, placed):
        for fine in range(FINE):
            spread[i, fine] = placed[:, 128 * fine : 128 * fine + 128]

    arrived(flat_copies)
    ends = jnp.where(spot < 48, flat_r[...], flat_l[...])
    flat_rows = jnp.concatenate([in_lots(flat[i], turned(ends, 32 - 16 * i)) for i in range(3)], axis=0)
    placed = exact_dot(flat_rows, place[:, : 128 * FINE])
    for i in range(3):
        put(i, placed[ROWS * i : ROWS * i + ROWS])

    level = lax.broadcasted_iota(jnp.int32, (NZ, 128), 0)

    def flat_tile(i, q, fine):
        return jnp.broadcast_to(spread[i, fine, pl.ds(q, 1), :], (NZ, 128))

    def faces(i, _):
        for k in range(2 * FINE):
            q, fine = 2 * i + k // FINE, k % FINE
            here = e_buf[e_tile(q + 1, fine), :]

            def side(beside):
                return here + jnp.where(beside > 0, beside, here)

            def column(beside):
                return ASPECT * (here + beside)

            marks = flat_tile(2, q, fine)
            parts = [
                side(e_buf[e_tile(q, fine), :]),
                side(e_buf[e_tile(q + 2, fine), :]),
                side(e_buf[e_tile(q + 1, fine - 1 if fine else FINE), :]),
                side(e_buf[e_tile(q + 1, fine + 1 if fine < FINE - 1 else FINE + 1), :]),
                jnp.where(level > 0, column(pltpu.roll(here, 1, 0)), 0.0),
                jnp.where(level < NZ - 1, column(pltpu.roll(here, NZ - 1, 0)), 0.0),
            ]
            total = parts[0] + parts[1] + parts[2] + parts[3] + parts[4] + parts[5]
            total = total + jnp.where(level == 0, marks, 0.0)
            inverse = jnp.where(marks > 0, 1.0 / jnp.where(marks > 0, total, 1.0), 0.0)
            for j, part in enumerate(parts):
                gs[q, fine, j] = part * inverse
            inv[q, fine] = SCALE * inverse
        return 0

    lax.fori_loop(0, ROWS // 2, faces, 0)

    def across(buf, row):
        return pltpu.roll(buf[row, FINE - 1], 1, 1), pltpu.roll(buf[row, 0], 127, 1)

    def apply(src, src_ext, dst, dst_ext, centre, shift):
        found = {q: across(src, q + 1) for q in ROW_ORDER if q in LATE and src_ext is not None}
        for q in ROW_ORDER:
            here = [src[q + 1, fine] for fine in range(FINE)]
            if src_ext is None:
                sides = across(src, q + 1)
            else:
                sides = found[q] if q in LATE else (src_ext[q, 0], src_ext[q, 1])
            row = []
            for fine in range(FINE):
                before = here[fine - 1] if fine else sides[0]
                after = here[fine + 1] if fine < FINE - 1 else sides[1]
                new = (
                    (gs[q, fine, 0] * src[q, fine] + gs[q, fine, 1] * src[q + 2, fine])
                    + (gs[q, fine, 2] * before + gs[q, fine, 3] * after)
                    + (
                        gs[q, fine, 4] * pltpu.roll(here[fine], 1, 0)
                        + gs[q, fine, 5] * pltpu.roll(here[fine], NZ - 1, 0)
                    )
                )
                new = new + shift * (here[fine] if centre is src else centre[q + 1, fine])
                dst[q + 1, fine] = new
                row.append(new)
            if q not in LATE:
                dst_ext[q, 0], dst_ext[q, 1] = pltpu.roll(row[FINE - 1], 1, 1), pltpu.roll(row[0], 127, 1)
            if q == ROWS - 1:
                for fine in range(FINE):
                    dst[0, fine] = pltpu.roll(row[fine], BLOCKS, 1)
            if q == 0:
                for fine in range(FINE):
                    dst[ROWS + 1, fine] = pltpu.roll(row[fine], 128 - BLOCKS, 1)

    def pick(values, i):
        out = jnp.float32(values[0])
        for k in range(1, len(values)):
            out = jnp.where(i == k, jnp.float32(values[k]), out)
        return out

    def solve(i, floor_only):
        def start_rows(j, _):
            for m in range(4):
                q = 4 * j + m
                for fine in range(FINE):
                    value = inv[q, fine] * flat_tile(i, q, fine)
                    u_buf[q + 1, fine] = jnp.where((level == 0) | jnp.logical_not(floor_only), value, 0.0)
            return 0

        lax.fori_loop(0, ROWS // 4, start_rows, 0)
        for fine in range(FINE):
            u_buf[0, fine] = pltpu.roll(u_buf[ROWS, fine], BLOCKS, 1)
            u_buf[ROWS + 1, fine] = pltpu.roll(u_buf[1, fine], 128 - BLOCKS, 1)

        apply(u_buf, None, t_buf, t_ext, u_buf, jnp.float32(LINEAR))

        def factor(j, _):
            apply(t_buf, t_ext, u_buf, u_ext, t_buf, pick(PS, j))
            apply(u_buf, u_ext, t_buf, t_ext, t_buf, pick(QS, j))
            return 0

        lax.fori_loop(0, len(PS), factor, 0)

    def own_columns():
        out = exact_dot(jnp.concatenate([sums[fine] for fine in range(FINE)], axis=1), back[...])
        cut = [slice(WIDE, ROWS), slice(0, ROWS), slice(0, ROWS), slice(0, ROWS - WIDE)]
        return jnp.concatenate([out[rows, 128 * lot : 128 * lot + 128] for lot, rows in enumerate(cut)], axis=0)

    def fold(reduce):
        for q in range(ROWS):
            for fine in range(FINE):
                sums[fine, q : q + 1, :] = reduce(t_buf[q + 1, fine])

    weight = ice * obs[...]

    def rhs_copies(c):
        packs = rhs_pack.at[c]
        return to_neighbours(
            rhs.at[pl.ds(c, 1)], (packs, packs), (rhs_l.at[c], rhs_r.at[c]), c_send.at[c], c_recv.at[c]
        )

    def depth_copies(c):
        here = pltpu.make_async_copy(depth.at[c], depth_ref.at[c, :, own_cols], local_sem.at[8 + c])
        there_too = pltpu.make_async_remote_copy(
            depth.at[c],
            depth_ref.at[c, :, own_cols],
            swap_send.at[2 + c],
            swap_recv.at[2 + c],
            device_id=partner,
            device_id_type=MESH,
        )
        return here, there_too

    def phase(p, _):
        c = lax.rem(p, 2)
        forward = p < 2

        @pl.when(jnp.logical_not(forward))
        def _():
            arrived(rhs_copies(c))
            edge = jnp.where(spot < 64, rhs_r[c], rhs_l[c])
            put(c, exact_dot(in_lots(rhs[c], edge), place[:, : 128 * FINE]))

        solve(c, forward)

        @pl.when(forward)
        def _():
            fold(lambda tile: jnp.sum(tile, axis=0, keepdims=True))
            field = own_columns()
            depth[c] = field
            field = weight * field
            rhs[c, own_rows, :] = field
            rhs_pack[c] = with_edges(jnp.zeros((NX, 128), F32), field, 0)
            start_all(rhs_copies(c))
            for copy in depth_copies(c):
                copy.start()

        @pl.when(jnp.logical_not(forward))
        def _():
            fold(lambda tile: tile[0:1, :])
            mult[c] = own_columns()

        return 0

    lax.fori_loop(0, 4, phase, 0)

    hess[...] = -friction * (base[0, 0].astype(F32) * mult[0] + base[0, 1].astype(F32) * mult[1])
    hess_out = pltpu.make_async_copy(hess, hess_ref, local_sem.at[7])
    hess_out.start()

    for copies in (flat_copies, visc_copies, rhs_copies(0), rhs_copies(1)):
        sent(copies)
    for c in range(2):
        for copy in depth_copies(c):
            copy.wait()
    hess_out.wait()


def solution(mesh):
    gx_n, gy_n = mesh.shape["gx"], mesh.shape["gy"]

    def step(viscosity, velocity, log_friction, step_dir, obs_weight, tile_mask, contact):
        any_space = pl.BlockSpec(memory_space=pl.ANY)
        vmem, dma = pltpu.VMEM, pltpu.SemaphoreType.DMA
        nd = len(DIRS)
        return pl.pallas_call(
            functools.partial(kernel, gx_n, gy_n),
            out_shape=(
                jax.ShapeDtypeStruct((2, NX, 2 * NY), F32),
                jax.ShapeDtypeStruct((NX, NY), F32),
            ),
            in_specs=[any_space] * 7,
            out_specs=(any_space, any_space),
            scratch_shapes=[
                vmem((NZ, XT, NY), BF16),
                vmem((XT, 128), BF16),
                vmem((XT, 128), BF16),
                vmem((NX, 128), BF16),
                vmem((NX, 128), BF16),
                vmem((2, 2, NX, NY), BF16),
                vmem((NX, NY), F32),
                vmem((NX, NY), F32),
                vmem((NX, NY), F32),
                vmem((NX, NY), jnp.int32),
                vmem((3, XT, NY), F32),
                vmem((NX, 128), F32),
                vmem((XT, 128), F32),
                vmem((XT, 128), F32),
                vmem((2, XT, NY), F32),
                vmem((2, NX, 128), F32),
                vmem((2, XT, 128), F32),
                vmem((2, XT, 128), F32),
                vmem((2, NX, NY), F32),
                vmem((NX, NY), F32),
                vmem((2, NX, NY), F32),
                vmem((ROWS * NZ, 256 * LOTS), F32),
                vmem(((ROWS + 2) * (FINE + 2) * NZ, 128), F32),
                vmem((3, FINE, ROWS, 128), F32),
                vmem((FINE, ROWS, 128), F32),
                vmem((256 * LOTS, (FINE + 2) * 128), BF16),
                vmem((FINE * 128, 128 * LOTS), BF16),
                vmem((ROWS, FINE, 6, NZ, 128), F32),
                vmem((ROWS, FINE, NZ, 128), F32),
                vmem((ROWS, 2, NZ, 128), F32),
                vmem((ROWS, 2, NZ, 128), F32),
                vmem((ROWS + 2, FINE, NZ, 128), F32),
                vmem((ROWS + 2, FINE, NZ, 128), F32),
                pltpu.SMEM((1, 4), jnp.int32),
                dma((10,)),
                dma((4,)),
                dma((4,)),
                dma((nd,)),
                dma((nd,)),
                dma((nd,)),
                dma((nd,)),
                dma((2, nd)),
                dma((2, nd)),
            ],
            compiler_params=pltpu.CompilerParams(
                collective_id=0, has_side_effects=True, vmem_limit_bytes=67043328
            ),
        )(viscosity, velocity, log_friction, step_dir, obs_weight, contact, tile_mask)

    in_specs = (
        P("gz", "gx", "gy"),
        P(None, "gz", "gx", "gy"),
        P("gx", "gy"),
        P("gx", "gy"),
        P("gx", "gy"),
        P("gx", "gy"),
        P("gx", "gy"),
    )
    out_specs = (P(None, "gx", "gy"), P("gx", ("gy", "gz")))
    return jax.shard_map(step, mesh=mesh, in_specs=in_specs, out_specs=out_specs, check_vma=False)
```

```python
import functools
import math

import jax
import jax.numpy as jnp
from jax import lax
from jax.experimental import pallas as pl
from jax.experimental.pallas import tpu as pltpu
from jax.sharding import PartitionSpec as P

MESH = pl.DeviceIdType.MESH
F32 = jnp.float32
BF16 = jnp.bfloat16

SWEEP = 8
ASPECT = 16.0
LOWER = 0.1
UPPER = 2.0
CENTRE = (UPPER + LOWER) / 2.0
HALF = (UPPER - LOWER) / 2.0
SIGMA = CENTRE / HALF

DELTA = CENTRE - 1.0
LINEAR = DELTA + CENTRE
ORDER = (3, 6, 1, 4, 5, 2, 7)
ANGLES = [math.pi * j / SWEEP for j in ORDER]
PS = [2.0 * DELTA - 2.0 * CENTRE * math.cos(t) for t in ANGLES]
QS = [
    DELTA * DELTA - 2.0 * CENTRE * DELTA * math.cos(t) + CENTRE * CENTRE - (HALF * math.sin(t)) ** 2
    for t in ANGLES
]
TOP = math.cosh(SWEEP * math.acosh(SIGMA))
SCALE = 2.0 ** (2 * SWEEP - 2) / (TOP * TOP) / HALF ** (2 * SWEEP)

WIDE = 16
NX, NY, NZ = 64, 128, 8
XT, YT = NX + 2 * WIDE, NY + 2 * WIDE
LOTS = 4
ROWS = XT // LOTS
BLOCKS = 128 // LOTS
FINE = YT // BLOCKS
DIRS = [(-1, -1), (-1, 1), (1, -1), (1, 1), (-1, 0), (1, 0), (0, -1), (0, 1)]
R_AT, L_AT = 32, 80
ROW_ORDER = [ROWS - 1, *range(8), *range(ROWS - 2, 15, -1), *range(8, 16)]
LATE = range(12, 16)


def lanes_of(shape):
    return lax.broadcasted_iota(jnp.int32, shape, len(shape) - 1)


def turned(value, by):
    by %= 128
    return value if by == 0 else pltpu.roll(value, by, value.ndim - 1)


def one_in(rows, target):
    return (lax.broadcasted_iota(jnp.int32, (rows, 128), 0) == target).astype(F32).astype(BF16)


def chooser(fine):
    n = lanes_of((1, 128))
    y = FINE * (n % BLOCKS) + fine
    edge = jnp.where(y < WIDE, 128 + L_AT + y, 128 + R_AT + y - WIDE - NY)
    k = 256 * (n // BLOCKS) + jnp.where((y >= WIDE) & (y < WIDE + NY), y - WIDE, edge)
    return one_in(256 * LOTS, jnp.where((y >= 0) & (y < YT), k, -1))


def returner(lot):
    y = lanes_of((1, 128)) + WIDE
    return one_in(FINE * 128, (y % FINE) * 128 + BLOCKS * lot + y // FINE)


def thirds(value):
    high = value.astype(BF16)
    rest = value - high.astype(F32)
    middle = rest.astype(BF16)
    return high, middle, (rest - middle.astype(F32)).astype(BF16)


def dot(a, b):
    return jnp.dot(a, b, preferred_element_type=F32)


def exact_dot(value, matrix):
    n = value.shape[0]
    out = dot(jnp.concatenate(thirds(value), axis=0), matrix)
    return out[:n] + out[n : 2 * n] + out[2 * n :]


def kernel(
    gx_n,
    gy_n,
    visc_ref,
    vel_ref,
    logf_ref,
    step_ref,
    obs_ref,
    contact_ref,
    tile_ref,
    depth_ref,
    hess_ref,
    visc,
    edge_l,
    edge_r,
    pack_l,
    pack_r,
    base,
    logf,
    step,
    obs,
    contact,
    flat,
    flat_pack,
    flat_l,
    flat_r,
    rhs,
    rhs_pack,
    rhs_l,
    rhs_r,
    depth,
    hess,
    mult,
    left,
    e_buf,
    spread,
    sums,
    place,
    back,
    gs,
    inv,
    u_ext,
    t_ext,
    u_buf,
    t_buf,
    classes,
    local_sem,
    swap_send,
    swap_recv,
    a_send,
    a_recv,
    b_send,
    b_recv,
    c_send,
    c_recv,
):
    gx, gy, gz = lax.axis_index("gx"), lax.axis_index("gy"), lax.axis_index("gz")
    yb = 2 * gy + gz
    y_n = 2 * gy_n

    def there(dx, dy):
        nx, ny = gx + dx, yb + dy
        return (nx >= 0) & (nx < gx_n) & (ny >= 0) & (ny < y_n)

    def device(dx, dy):
        ny = yb + dy
        return (gx + dx, lax.div(ny, 2), lax.rem(ny, 2))

    own_cols = pl.ds(pl.multiple_of(gz * NY, NY), NY)
    other_cols = pl.ds(pl.multiple_of((1 - gz) * NY, NY), NY)
    own_rows = pl.ds(WIDE, NX)
    layers = visc_ref.shape[0]
    mine = pl.ds(gz * layers, layers)
    partner = (gx, gy, 1 - gz)

    local = [
        pltpu.make_async_copy(visc_ref.at[:, :, own_cols], visc.at[mine, own_rows], local_sem.at[0]),
        pltpu.make_async_copy(vel_ref.at[:, 0, :, own_cols], base.at[gz], local_sem.at[1]),
        pltpu.make_async_copy(logf_ref.at[:, own_cols], logf, local_sem.at[2]),
        pltpu.make_async_copy(step_ref.at[:, own_cols], step, local_sem.at[3]),
        pltpu.make_async_copy(contact_ref.at[:, own_cols], contact, local_sem.at[4]),
        pltpu.make_async_copy(obs_ref.at[:, own_cols], obs, local_sem.at[5]),
        pltpu.make_async_copy(tile_ref, classes, local_sem.at[6]),
    ]
    for copy in local:
        copy.start()

    barrier = pltpu.get_barrier_semaphore()
    met = 0
    for d in DIRS:
        here = there(*d)
        met = met + here.astype(jnp.int32)

        @pl.when(here)
        def _():
            pl.semaphore_signal(barrier, inc=1, device_id=device(*d), device_id_type=MESH)

    @pl.when(gx == 0)
    def _():
        visc[:, 0:WIDE, :] = jnp.zeros((NZ, WIDE, NY), BF16)
        flat[:, 0:WIDE, :] = jnp.zeros((3, WIDE, NY), F32)
        rhs[:, 0:WIDE, :] = jnp.zeros((2, WIDE, NY), F32)

    @pl.when(gx == gx_n - 1)
    def _():
        visc[:, XT - WIDE : XT, :] = jnp.zeros((NZ, WIDE, NY), BF16)
        flat[:, XT - WIDE : XT, :] = jnp.zeros((3, WIDE, NY), F32)
        rhs[:, XT - WIDE : XT, :] = jnp.zeros((2, WIDE, NY), F32)

    for dy, ends in ((-1, (edge_l, flat_l, rhs_l)), (1, (edge_r, flat_r, rhs_r))):
        for dx, first, count in ((-1, 0, WIDE), (0, WIDE, NX), (1, WIDE + NX, WIDE)):

            @pl.when(jnp.logical_not(there(dx, dy)))
            def _():
                for end in ends[:2]:
                    end[first : first + count, :] = jnp.zeros((count, 128), end.dtype)
                ends[2][:, first : first + count, :] = jnp.zeros((2, count, 128), F32)

    for tile, fine in enumerate((*range(FINE), -1, FINE)):
        place[:, 128 * tile : 128 * tile + 128] = chooser(fine)
    for lot in range(LOTS):
        back[:, 128 * lot : 128 * lot + 128] = returner(lot)

    for copy in local[1:]:
        copy.wait()

    lane = lanes_of((NX, NY))
    left_class, right_class = classes[0, 2 * gz], classes[0, 2 * gz + 1]
    kinds = jnp.where(lane < NY // 2, left_class, right_class)
    ice = (kinds > 0).astype(F32)
    friction = jnp.exp(logf[...]) * (kinds == 2).astype(F32) * contact[...].astype(F32)
    marked = jnp.where(kinds > 0, jnp.maximum(friction, 1e-30), 0.0)
    flat[2, own_rows, :] = marked
    drive = -(friction * step[...])

    pl.semaphore_wait(barrier, met)

    swap = [
        pltpu.make_async_remote_copy(
            visc_ref.at[:, :, other_cols],
            visc.at[mine, own_rows],
            swap_send.at[0],
            swap_recv.at[0],
            device_id=partner,
            device_id_type=MESH,
        ),
        pltpu.make_async_remote_copy(
            vel_ref.at[:, 0, :, other_cols],
            base.at[gz],
            swap_send.at[1],
            swap_recv.at[1],
            device_id=partner,
            device_id_type=MESH,
        ),
    ]
    for copy in swap:
        copy.start()

    def with_edges(packed, field, shift):
        for at, first in ((R_AT - shift, 0), (L_AT - shift, NY - WIDE)):
            packed = jnp.where((lane >= at) & (lane < at + WIDE), turned(field, at - first), packed)
        return packed

    def extent(dx):
        if dx == 0:
            return pl.ds(WIDE, NX), pl.ds(0, NX), pl.ds(WIDE, NX)
        if dx < 0:
            return pl.ds(WIDE, WIDE), pl.ds(0, WIDE), pl.ds(WIDE + NX, WIDE)
        return pl.ds(NX, WIDE), pl.ds(NX - WIDE, WIDE), pl.ds(0, WIDE)

    def to_neighbours(block, packs, lands, send, recv):
        copies = []
        for i, (dx, dy) in enumerate(DIRS):
            src, src_pack, dst = extent(dx)
            if dy == 0:
                pair = (block.at[:, src, :], block.at[:, dst, :])
            elif dy < 0:
                pair = (packs[0].at[src_pack, :], lands[1].at[dst, :])
            else:
                pair = (packs[1].at[src_pack, :], lands[0].at[dst, :])
            copies.append(
                pltpu.make_async_remote_copy(
                    *pair,
                    send.at[i],
                    recv.at[i],
                    device_id=device(dx, dy),
                    device_id_type=MESH,
                )
            )
        return copies

    def start_all(copies):
        for (dx, dy), copy in zip(DIRS, copies):
            pl.when(there(dx, dy))(copy.start)

    def arrived(copies):
        for (dx, dy), copy in zip(DIRS, copies):
            pl.when(there(-dx, -dy))(copy.wait_recv)

    def sent(copies):
        for (dx, dy), copy in zip(DIRS, copies):
            pl.when(there(dx, dy))(copy.wait_send)

    local[0].wait()
    swap[0].wait()

    low = jnp.zeros((NX, 128), F32)
    high = jnp.zeros((NX, 128), F32)
    for layer in range(NZ):
        e = visc[layer, own_rows, :].astype(F32)
        inside = (lane >= 16 * layer) & (lane < 16 * layer + 16)
        low = jnp.where(inside, turned(e, 16 * layer), low)
        high = jnp.where(inside, turned(e, 16 * layer + 16), high)
    pack_l[...] = low.astype(BF16)
    pack_r[...] = high.astype(BF16)
    visc_copies = to_neighbours(visc, (pack_l, pack_r), (edge_l, edge_r), a_send, a_recv)
    start_all(visc_copies)

    swap[1].wait()
    flat[0, own_rows, :] = drive * base[0, 0].astype(F32)
    flat[1, own_rows, :] = drive * base[0, 1].astype(F32)
    packed = jnp.zeros((NX, 128), F32)
    for i in range(3):
        packed = with_edges(packed, flat[i, own_rows, :], 32 - 16 * i)
    flat_pack[...] = packed
    flat_copies = to_neighbours(flat, (flat_pack, flat_pack), (flat_l, flat_r), b_send, b_recv)
    start_all(flat_copies)

    arrived(visc_copies)

    spot = lanes_of((XT, 128))

    def in_lots(own, edge):
        return jnp.concatenate(
            [part[ROWS * lot : ROWS * lot + ROWS] for lot in range(LOTS) for part in (own, edge)], axis=1
        )

    ends_l, ends_r = edge_l[...].astype(F32), edge_r[...].astype(F32)
    for layer in range(NZ):
        edge = jnp.where(spot < 64, turned(ends_r, R_AT - 16 * layer), turned(ends_l, L_AT - 16 * layer))
        left[ROWS * layer : ROWS * layer + ROWS, :] = in_lots(visc[layer].astype(F32), edge)

    tiles = FINE + 2
    rows_in = left[...].astype(BF16)
    for tile in range(tiles):
        placed = 0.5 * dot(rows_in, place[:, 128 * tile : 128 * tile + 128])
        for layer in range(NZ):
            e_buf[pl.ds(tiles * NZ + tile * NZ + layer, ROWS, stride=tiles * NZ), :] = placed[
                ROWS * layer : ROWS * layer + ROWS
            ]

    def e_tile(row, tile):
        return pl.ds(pl.multiple_of((row * tiles + tile) * NZ, NZ), NZ)

    for fine in range(FINE):
        e_buf[e_tile(0, fine), :] = pltpu.roll(e_buf[e_tile(ROWS, fine), :], BLOCKS, 1)
        e_buf[e_tile(ROWS + 1, fine), :] = pltpu.roll(e_buf[e_tile(1, fine), :], 128 - BLOCKS, 1)

    def put(i, placed):
        for fine in range(FINE):
            spread[i, fine] = placed[:, 128 * fine : 128 * fine + 128]

    arrived(flat_copies)
    ends = jnp.where(spot < 48, flat_r[...], flat_l[...])
    flat_rows = jnp.concatenate([in_lots(flat[i], turned(ends, 32 - 16 * i)) for i in range(3)], axis=0)
    placed = exact_dot(flat_rows, place[:, : 128 * FINE])
    for i in range(3):
        put(i, placed[ROWS * i : ROWS * i + ROWS])

    level = lax.broadcasted_iota(jnp.int32, (NZ, 128), 0)

    def flat_tile(i, q, fine):
        return jnp.broadcast_to(spread[i, fine, pl.ds(q, 1), :], (NZ, 128))

    def faces(i, _):
        for k in range(2 * FINE):
            q, fine = 2 * i + k // FINE, k % FINE
            here = e_buf[e_tile(q + 1, fine), :]

            def side(beside):
                return here + jnp.where(beside > 0, beside, here)

            def column(beside):
                return ASPECT * (here + beside)

            marks = flat_tile(2, q, fine)
            parts = [
                side(e_buf[e_tile(q, fine), :]),
                side(e_buf[e_tile(q + 2, fine), :]),
                side(e_buf[e_tile(q + 1, fine - 1 if fine else FINE), :]),
                side(e_buf[e_tile(q + 1, fine + 1 if fine < FINE - 1 else FINE + 1), :]),
                jnp.where(level > 0, column(pltpu.roll(here, 1, 0)), 0.0),
                jnp.where(level < NZ - 1, column(pltpu.roll(here, NZ - 1, 0)), 0.0),
            ]
            total = parts[0] + parts[1] + parts[2] + parts[3] + parts[4] + parts[5]
            total = total + jnp.where(level == 0, marks, 0.0)
            inverse = jnp.where(marks > 0, 1.0 / jnp.where(marks > 0, total, 1.0), 0.0)
            for j, part in enumerate(parts):
                gs[q, fine, j] = part * inverse
            inv[q, fine] = SCALE * inverse
        return 0

    lax.fori_loop(0, ROWS // 2, faces, 0)

    def across(buf, row):
        return pltpu.roll(buf[row, FINE - 1], 1, 1), pltpu.roll(buf[row, 0], 127, 1)

    def apply(src, src_ext, dst, dst_ext, centre, shift):
        found = {q: across(src, q + 1) for q in ROW_ORDER if q in LATE and src_ext is not None}
        for q in ROW_ORDER:
            here = [src[q + 1, fine] for fine in range(FINE)]
            if src_ext is None:
                sides = across(src, q + 1)
            else:
                sides = found[q] if q in LATE else (src_ext[q, 0], src_ext[q, 1])
            row = []
            for fine in range(FINE):
                before = here[fine - 1] if fine else sides[0]
                after = here[fine + 1] if fine < FINE - 1 else sides[1]
                new = (
                    (gs[q, fine, 0] * src[q, fine] + gs[q, fine, 1] * src[q + 2, fine])
                    + (gs[q, fine, 2] * before + gs[q, fine, 3] * after)
                    + (
                        gs[q, fine, 4] * pltpu.roll(here[fine], 1, 0)
                        + gs[q, fine, 5] * pltpu.roll(here[fine], NZ - 1, 0)
                    )
                )
                new = new + shift * (here[fine] if centre is src else centre[q + 1, fine])
                dst[q + 1, fine] = new
                row.append(new)
            if q not in LATE:
                dst_ext[q, 0], dst_ext[q, 1] = pltpu.roll(row[FINE - 1], 1, 1), pltpu.roll(row[0], 127, 1)
            if q == ROWS - 1:
                for fine in range(FINE):
                    dst[0, fine] = pltpu.roll(row[fine], BLOCKS, 1)
            if q == 0:
                for fine in range(FINE):
                    dst[ROWS + 1, fine] = pltpu.roll(row[fine], 128 - BLOCKS, 1)

    def pick(values, i):
        out = jnp.float32(values[0])
        for k in range(1, len(values)):
            out = jnp.where(i == k, jnp.float32(values[k]), out)
        return out

    def solve(i, floor_only):
        def start_rows(j, _):
            for m in range(4):
                q = 4 * j + m
                for fine in range(FINE):
                    value = inv[q, fine] * flat_tile(i, q, fine)
                    u_buf[q + 1, fine] = jnp.where((level == 0) | jnp.logical_not(floor_only), value, 0.0)
            return 0

        lax.fori_loop(0, ROWS // 4, start_rows, 0)
        for fine in range(FINE):
            u_buf[0, fine] = pltpu.roll(u_buf[ROWS, fine], BLOCKS, 1)
            u_buf[ROWS + 1, fine] = pltpu.roll(u_buf[1, fine], 128 - BLOCKS, 1)

        apply(u_buf, None, t_buf, t_ext, u_buf, jnp.float32(LINEAR))

        def factor(j, _):
            apply(t_buf, t_ext, u_buf, u_ext, t_buf, pick(PS, j))
            apply(u_buf, u_ext, t_buf, t_ext, t_buf, pick(QS, j))
            return 0

        lax.fori_loop(0, len(PS), factor, 0)

    def own_columns():
        out = exact_dot(jnp.concatenate([sums[fine] for fine in range(FINE)], axis=1), back[...])
        cut = [slice(WIDE, ROWS), slice(0, ROWS), slice(0, ROWS), slice(0, ROWS - WIDE)]
        return jnp.concatenate([out[rows, 128 * lot : 128 * lot + 128] for lot, rows in enumerate(cut)], axis=0)

    def fold(reduce):
        for q in range(ROWS):
            for fine in range(FINE):
                sums[fine, q : q + 1, :] = reduce(t_buf[q + 1, fine])

    weight = ice * obs[...]

    def rhs_copies(c):
        packs = rhs_pack.at[c]
        return to_neighbours(
            rhs.at[pl.ds(c, 1)], (packs, packs), (rhs_l.at[c], rhs_r.at[c]), c_send.at[c], c_recv.at[c]
        )

    def depth_copies(c):
        here = pltpu.make_async_copy(depth.at[c], depth_ref.at[c, :, own_cols], local_sem.at[8 + c])
        there_too = pltpu.make_async_remote_copy(
            depth.at[c],
            depth_ref.at[c, :, own_cols],
            swap_send.at[2 + c],
            swap_recv.at[2 + c],
            device_id=partner,
            device_id_type=MESH,
        )
        return here, there_too

    def phase(p, _):
        c = lax.rem(p, 2)
        forward = p < 2

        @pl.when(jnp.logical_not(forward))
        def _():
            arrived(rhs_copies(c))
            edge = jnp.where(spot < 64, rhs_r[c], rhs_l[c])
            put(c, exact_dot(in_lots(rhs[c], edge), place[:, : 128 * FINE]))

        solve(c, forward)

        @pl.when(forward)
        def _():
            fold(lambda tile: jnp.sum(tile, axis=0, keepdims=True))
            field = own_columns()
            depth[c] = field
            field = weight * field
            rhs[c, own_rows, :] = field
            rhs_pack[c] = with_edges(jnp.zeros((NX, 128), F32), field, 0)
            start_all(rhs_copies(c))
            for copy in depth_copies(c):
                copy.start()

        @pl.when(jnp.logical_not(forward))
        def _():
            fold(lambda tile: tile[0:1, :])
            mult[c] = own_columns()

        return 0

    lax.fori_loop(0, 4, phase, 0)

    hess[...] = -friction * (base[0, 0].astype(F32) * mult[0] + base[0, 1].astype(F32) * mult[1])
    hess_out = pltpu.make_async_copy(hess, hess_ref, local_sem.at[7])
    hess_out.start()

    for copies in (flat_copies, visc_copies, rhs_copies(0), rhs_copies(1)):
        sent(copies)
    for c in range(2):
        for copy in depth_copies(c):
            copy.wait()
    hess_out.wait()


def solution(mesh):
    gx_n, gy_n = mesh.shape["gx"], mesh.shape["gy"]

    def step(viscosity, velocity, log_friction, step_dir, obs_weight, tile_mask, contact):
        any_space = pl.BlockSpec(memory_space=pl.ANY)
        vmem, dma = pltpu.VMEM, pltpu.SemaphoreType.DMA
        nd = len(DIRS)
        return pl.pallas_call(
            functools.partial(kernel, gx_n, gy_n),
            out_shape=(
                jax.ShapeDtypeStruct((2, NX, 2 * NY), F32),
                jax.ShapeDtypeStruct((NX, NY), F32),
            ),
            in_specs=[any_space] * 7,
            out_specs=(any_space, any_space),
            scratch_shapes=[
                vmem((NZ, XT, NY), BF16),
                vmem((XT, 128), BF16),
                vmem((XT, 128), BF16),
                vmem((NX, 128), BF16),
                vmem((NX, 128), BF16),
                vmem((2, 2, NX, NY), BF16),
                vmem((NX, NY), F32),
                vmem((NX, NY), F32),
                vmem((NX, NY), F32),
                vmem((NX, NY), jnp.int32),
                vmem((3, XT, NY), F32),
                vmem((NX, 128), F32),
                vmem((XT, 128), F32),
                vmem((XT, 128), F32),
                vmem((2, XT, NY), F32),
                vmem((2, NX, 128), F32),
                vmem((2, XT, 128), F32),
                vmem((2, XT, 128), F32),
                vmem((2, NX, NY), F32),
                vmem((NX, NY), F32),
                vmem((2, NX, NY), F32),
                vmem((ROWS * NZ, 256 * LOTS), F32),
                vmem(((ROWS + 2) * (FINE + 2) * NZ, 128), F32),
                vmem((3, FINE, ROWS, 128), F32),
                vmem((FINE, ROWS, 128), F32),
                vmem((256 * LOTS, (FINE + 2) * 128), BF16),
                vmem((FINE * 128, 128 * LOTS), BF16),
                vmem((ROWS, FINE, 6, NZ, 128), F32),
                vmem((ROWS, FINE, NZ, 128), F32),
                vmem((ROWS, 2, NZ, 128), F32),
                vmem((ROWS, 2, NZ, 128), F32),
                vmem((ROWS + 2, FINE, NZ, 128), F32),
                vmem((ROWS + 2, FINE, NZ, 128), F32),
                pltpu.SMEM((1, 4), jnp.int32),
                dma((10,)),
                dma((4,)),
                dma((4,)),
                dma((nd,)),
                dma((nd,)),
                dma((nd,)),
                dma((nd,)),
                dma((2, nd)),
                dma((2, nd)),
            ],
            compiler_params=pltpu.CompilerParams(
                collective_id=0, has_side_effects=True, vmem_limit_bytes=40 * 1024 * 1024
            ),
        )(
            *(
                pltpu.with_memory_space_constraint(x, pltpu.HBM)
                for x in (viscosity, velocity, log_friction, step_dir, obs_weight, contact, tile_mask)
            )
        )

    in_specs = (
        P("gz", "gx", "gy"),
        P(None, "gz", "gx", "gy"),
        P("gx", "gy"),
        P("gx", "gy"),
        P("gx", "gy"),
        P("gx", "gy"),
        P("gx", "gy"),
    )
    out_specs = (P(None, "gx", "gy"), P("gx", ("gy", "gz")))
    return jax.shard_map(step, mesh=mesh, in_specs=in_specs, out_specs=out_specs, check_vma=False)
```

```python
import functools
import math

import jax
import jax.numpy as jnp
from jax import lax
from jax.experimental import pallas as pl
from jax.experimental.pallas import tpu as pltpu
from jax.sharding import PartitionSpec as P

MESH = pl.DeviceIdType.MESH
F32 = jnp.float32
BF16 = jnp.bfloat16

SWEEP = 8
ASPECT = 16.0
LOWER = 0.1
UPPER = 2.0
CENTRE = (UPPER + LOWER) / 2.0
HALF = (UPPER - LOWER) / 2.0
SIGMA = CENTRE / HALF

DELTA = CENTRE - 1.0
LINEAR = DELTA + CENTRE
ORDER = (3, 6, 1, 4, 5, 2, 7)
ANGLES = [math.pi * j / SWEEP for j in ORDER]
PS = [2.0 * DELTA - 2.0 * CENTRE * math.cos(t) for t in ANGLES]
QS = [
    DELTA * DELTA - 2.0 * CENTRE * DELTA * math.cos(t) + CENTRE * CENTRE - (HALF * math.sin(t)) ** 2
    for t in ANGLES
]
TOP = math.cosh(SWEEP * math.acosh(SIGMA))
SCALE = 2.0 ** (2 * SWEEP - 2) / (TOP * TOP) / HALF ** (2 * SWEEP)

WIDE = 16
NX, NY, NZ = 64, 128, 8
XT, YT = NX + 2 * WIDE, NY + 2 * WIDE
LOTS = 4
ROWS = XT // LOTS
BLOCKS = 128 // LOTS
FINE = YT // BLOCKS
DIRS = [(-1, -1), (-1, 1), (1, -1), (1, 1), (-1, 0), (1, 0), (0, -1), (0, 1)]
R_AT, L_AT = 32, 80
ROW_ORDER = [ROWS - 1, *range(8), *range(ROWS - 2, 15, -1), *range(8, 16)]
LATE = range(12, 16)


def lanes_of(shape):
    return lax.broadcasted_iota(jnp.int32, shape, len(shape) - 1)


def turned(value, by):
    by %= 128
    return value if by == 0 else pltpu.roll(value, by, value.ndim - 1)


def one_in(rows, target):
    return (lax.broadcasted_iota(jnp.int32, (rows, 128), 0) == target).astype(F32).astype(BF16)


def chooser(fine):
    n = lanes_of((1, 128))
    y = FINE * (n % BLOCKS) + fine
    edge = jnp.where(y < WIDE, 128 + L_AT + y, 128 + R_AT + y - WIDE - NY)
    k = 256 * (n // BLOCKS) + jnp.where((y >= WIDE) & (y < WIDE + NY), y - WIDE, edge)
    return one_in(256 * LOTS, jnp.where((y >= 0) & (y < YT), k, -1))


def returner(lot):
    y = lanes_of((1, 128)) + WIDE
    return one_in(FINE * 128, (y % FINE) * 128 + BLOCKS * lot + y // FINE)


def thirds(value):
    high = value.astype(BF16)
    rest = value - high.astype(F32)
    middle = rest.astype(BF16)
    return high, middle, (rest - middle.astype(F32)).astype(BF16)


def dot(a, b):
    return jnp.dot(a, b, preferred_element_type=F32)


def exact_dot(value, matrix):
    n = value.shape[0]
    out = dot(jnp.concatenate(thirds(value), axis=0), matrix)
    return out[:n] + out[n : 2 * n] + out[2 * n :]


def kernel(
    gx_n,
    gy_n,
    visc_ref,
    vel_ref,
    logf_ref,
    step_ref,
    obs_ref,
    contact_ref,
    tile_ref,
    depth_ref,
    hess_ref,
    visc,
    edge_l,
    edge_r,
    pack_l,
    pack_r,
    base,
    logf,
    step,
    obs,
    contact,
    flat,
    flat_pack,
    flat_l,
    flat_r,
    rhs,
    rhs_pack,
    rhs_l,
    rhs_r,
    depth,
    mult,
    left,
    e_buf,
    spread,
    sums,
    place,
    back,
    gs,
    inv,
    u_ext,
    t_ext,
    u_buf,
    t_buf,
    classes,
    local_sem,
    swap_send,
    swap_recv,
    a_send,
    a_recv,
    b_send,
    b_recv,
    c_send,
    c_recv,
):
    gx, gy, gz = lax.axis_index("gx"), lax.axis_index("gy"), lax.axis_index("gz")
    yb = 2 * gy + gz
    y_n = 2 * gy_n

    def there(dx, dy):
        nx, ny = gx + dx, yb + dy
        return (nx >= 0) & (nx < gx_n) & (ny >= 0) & (ny < y_n)

    def device(dx, dy):
        ny = yb + dy
        return (gx + dx, lax.div(ny, 2), lax.rem(ny, 2))

    own_cols = pl.ds(pl.multiple_of(gz * NY, NY), NY)
    other_cols = pl.ds(pl.multiple_of((1 - gz) * NY, NY), NY)
    own_rows = pl.ds(WIDE, NX)
    layers = visc_ref.shape[0]
    mine = pl.ds(gz * layers, layers)
    partner = (gx, gy, 1 - gz)

    local = [
        pltpu.make_async_copy(visc_ref.at[:, :, own_cols], visc.at[mine, own_rows], local_sem.at[0]),
        pltpu.make_async_copy(vel_ref.at[:, 0, :, own_cols], base.at[gz], local_sem.at[1]),
        pltpu.make_async_copy(logf_ref.at[:, own_cols], logf, local_sem.at[2]),
        pltpu.make_async_copy(step_ref.at[:, own_cols], step, local_sem.at[3]),
        pltpu.make_async_copy(contact_ref.at[:, own_cols], contact, local_sem.at[4]),
        pltpu.make_async_copy(obs_ref.at[:, own_cols], obs, local_sem.at[5]),
        pltpu.make_async_copy(tile_ref, classes, local_sem.at[6]),
    ]
    for copy in local:
        copy.start()

    barrier = pltpu.get_barrier_semaphore()
    met = 0
    for d in DIRS:
        here = there(*d)
        met = met + here.astype(jnp.int32)

        @pl.when(here)
        def _():
            pl.semaphore_signal(barrier, inc=1, device_id=device(*d), device_id_type=MESH)

    @pl.when(gx == 0)
    def _():
        visc[:, 0:WIDE, :] = jnp.zeros((NZ, WIDE, NY), BF16)
        flat[:, 0:WIDE, :] = jnp.zeros((3, WIDE, NY), F32)
        rhs[:, 0:WIDE, :] = jnp.zeros((2, WIDE, NY), F32)

    @pl.when(gx == gx_n - 1)
    def _():
        visc[:, XT - WIDE : XT, :] = jnp.zeros((NZ, WIDE, NY), BF16)
        flat[:, XT - WIDE : XT, :] = jnp.zeros((3, WIDE, NY), F32)
        rhs[:, XT - WIDE : XT, :] = jnp.zeros((2, WIDE, NY), F32)

    for dy, ends in ((-1, (edge_l, flat_l, rhs_l)), (1, (edge_r, flat_r, rhs_r))):
        for dx, first, count in ((-1, 0, WIDE), (0, WIDE, NX), (1, WIDE + NX, WIDE)):

            @pl.when(jnp.logical_not(there(dx, dy)))
            def _():
                for end in ends[:2]:
                    end[first : first + count, :] = jnp.zeros((count, 128), end.dtype)
                ends[2][:, first : first + count, :] = jnp.zeros((2, count, 128), F32)

    for tile, fine in enumerate((*range(FINE), -1, FINE)):
        place[:, 128 * tile : 128 * tile + 128] = chooser(fine)
    for lot in range(LOTS):
        back[:, 128 * lot : 128 * lot + 128] = returner(lot)

    for copy in local[1:]:
        copy.wait()

    lane = lanes_of((NX, NY))
    left_class, right_class = classes[0, 2 * gz], classes[0, 2 * gz + 1]
    kinds = jnp.where(lane < NY // 2, left_class, right_class)
    ice = (kinds > 0).astype(F32)
    friction = jnp.exp(logf[...]) * (kinds == 2).astype(F32) * contact[...].astype(F32)
    marked = jnp.where(kinds > 0, jnp.maximum(friction, 1e-30), 0.0)
    flat[2, own_rows, :] = marked
    drive = -(friction * step[...])

    pl.semaphore_wait(barrier, met)

    swap = [
        pltpu.make_async_remote_copy(
            visc_ref.at[:, :, other_cols],
            visc.at[mine, own_rows],
            swap_send.at[0],
            swap_recv.at[0],
            device_id=partner,
            device_id_type=MESH,
        ),
        pltpu.make_async_remote_copy(
            vel_ref.at[:, 0, :, other_cols],
            base.at[gz],
            swap_send.at[1],
            swap_recv.at[1],
            device_id=partner,
            device_id_type=MESH,
        ),
    ]
    for copy in swap:
        copy.start()

    def with_edges(packed, field, shift):
        for at, first in ((R_AT - shift, 0), (L_AT - shift, NY - WIDE)):
            packed = jnp.where((lane >= at) & (lane < at + WIDE), turned(field, at - first), packed)
        return packed

    def extent(dx):
        if dx == 0:
            return pl.ds(WIDE, NX), pl.ds(0, NX), pl.ds(WIDE, NX)
        if dx < 0:
            return pl.ds(WIDE, WIDE), pl.ds(0, WIDE), pl.ds(WIDE + NX, WIDE)
        return pl.ds(NX, WIDE), pl.ds(NX - WIDE, WIDE), pl.ds(0, WIDE)

    def to_neighbours(block, packs, lands, send, recv):
        copies = []
        for i, (dx, dy) in enumerate(DIRS):
            src, src_pack, dst = extent(dx)
            if dy == 0:
                pair = (block.at[:, src, :], block.at[:, dst, :])
            elif dy < 0:
                pair = (packs[0].at[src_pack, :], lands[1].at[dst, :])
            else:
                pair = (packs[1].at[src_pack, :], lands[0].at[dst, :])
            copies.append(
                pltpu.make_async_remote_copy(
                    *pair,
                    send.at[i],
                    recv.at[i],
                    device_id=device(dx, dy),
                    device_id_type=MESH,
                )
            )
        return copies

    def start_all(copies):
        for (dx, dy), copy in zip(DIRS, copies):
            pl.when(there(dx, dy))(copy.start)

    def arrived(copies):
        for (dx, dy), copy in zip(DIRS, copies):
            pl.when(there(-dx, -dy))(copy.wait_recv)

    def sent(copies):
        for (dx, dy), copy in zip(DIRS, copies):
            pl.when(there(dx, dy))(copy.wait_send)

    local[0].wait()
    swap[0].wait()

    low = jnp.zeros((NX, 128), F32)
    high = jnp.zeros((NX, 128), F32)
    for layer in range(NZ):
        e = visc[layer, own_rows, :].astype(F32)
        inside = (lane >= 16 * layer) & (lane < 16 * layer + 16)
        low = jnp.where(inside, turned(e, 16 * layer), low)
        high = jnp.where(inside, turned(e, 16 * layer + 16), high)
    pack_l[...] = low.astype(BF16)
    pack_r[...] = high.astype(BF16)
    visc_copies = to_neighbours(visc, (pack_l, pack_r), (edge_l, edge_r), a_send, a_recv)
    start_all(visc_copies)

    swap[1].wait()
    flat[0, own_rows, :] = drive * base[0, 0].astype(F32)
    flat[1, own_rows, :] = drive * base[0, 1].astype(F32)
    packed = jnp.zeros((NX, 128), F32)
    for i in range(3):
        packed = with_edges(packed, flat[i, own_rows, :], 32 - 16 * i)
    flat_pack[...] = packed
    flat_copies = to_neighbours(flat, (flat_pack, flat_pack), (flat_l, flat_r), b_send, b_recv)
    start_all(flat_copies)

    arrived(visc_copies)

    spot = lanes_of((XT, 128))

    def in_lots(own, edge):
        return jnp.concatenate(
            [part[ROWS * lot : ROWS * lot + ROWS] for lot in range(LOTS) for part in (own, edge)], axis=1
        )

    ends_l, ends_r = edge_l[...].astype(F32), edge_r[...].astype(F32)
    for layer in range(NZ):
        edge = jnp.where(spot < 64, turned(ends_r, R_AT - 16 * layer), turned(ends_l, L_AT - 16 * layer))
        left[ROWS * layer : ROWS * layer + ROWS, :] = in_lots(visc[layer].astype(F32), edge)

    tiles = FINE + 2
    rows_in = left[...].astype(BF16)
    for tile in range(tiles):
        placed = 0.5 * dot(rows_in, place[:, 128 * tile : 128 * tile + 128])
        for layer in range(NZ):
            e_buf[pl.ds(tiles * NZ + tile * NZ + layer, ROWS, stride=tiles * NZ), :] = placed[
                ROWS * layer : ROWS * layer + ROWS
            ]

    def e_tile(row, tile):
        return pl.ds(pl.multiple_of((row * tiles + tile) * NZ, NZ), NZ)

    for fine in range(FINE):
        e_buf[e_tile(0, fine), :] = pltpu.roll(e_buf[e_tile(ROWS, fine), :], BLOCKS, 1)
        e_buf[e_tile(ROWS + 1, fine), :] = pltpu.roll(e_buf[e_tile(1, fine), :], 128 - BLOCKS, 1)

    def put(i, placed):
        for fine in range(FINE):
            spread[i, fine] = placed[:, 128 * fine : 128 * fine + 128]

    arrived(flat_copies)
    ends = jnp.where(spot < 48, flat_r[...], flat_l[...])
    flat_rows = jnp.concatenate([in_lots(flat[i], turned(ends, 32 - 16 * i)) for i in range(3)], axis=0)
    placed = exact_dot(flat_rows, place[:, : 128 * FINE])
    for i in range(3):
        put(i, placed[ROWS * i : ROWS * i + ROWS])

    level = lax.broadcasted_iota(jnp.int32, (NZ, 128), 0)

    def flat_tile(i, q, fine):
        return jnp.broadcast_to(spread[i, fine, pl.ds(q, 1), :], (NZ, 128))

    def faces(i, _):
        for k in range(2 * FINE):
            q, fine = 2 * i + k // FINE, k % FINE
            here = e_buf[e_tile(q + 1, fine), :]

            def side(beside):
                return here + jnp.where(beside > 0, beside, here)

            def column(beside):
                return ASPECT * (here + beside)

            marks = flat_tile(2, q, fine)
            parts = [
                side(e_buf[e_tile(q, fine), :]),
                side(e_buf[e_tile(q + 2, fine), :]),
                side(e_buf[e_tile(q + 1, fine - 1 if fine else FINE), :]),
                side(e_buf[e_tile(q + 1, fine + 1 if fine < FINE - 1 else FINE + 1), :]),
                jnp.where(level > 0, column(pltpu.roll(here, 1, 0)), 0.0),
                jnp.where(level < NZ - 1, column(pltpu.roll(here, NZ - 1, 0)), 0.0),
            ]
            total = parts[0] + parts[1] + parts[2] + parts[3] + parts[4] + parts[5]
            total = total + jnp.where(level == 0, marks, 0.0)
            inverse = jnp.where(marks > 0, 1.0 / jnp.where(marks > 0, total, 1.0), 0.0)
            for j, part in enumerate(parts):
                gs[q, fine, j] = part * inverse
            inv[q, fine] = SCALE * inverse
        return 0

    lax.fori_loop(0, ROWS // 2, faces, 0)

    def across(buf, row):
        return pltpu.roll(buf[row, FINE - 1], 1, 1), pltpu.roll(buf[row, 0], 127, 1)

    def apply(src, src_ext, dst, dst_ext, centre, shift):
        found = {q: across(src, q + 1) for q in ROW_ORDER if q in LATE and src_ext is not None}
        for q in ROW_ORDER:
            here = [src[q + 1, fine] for fine in range(FINE)]
            if src_ext is None:
                sides = across(src, q + 1)
            else:
                sides = found[q] if q in LATE else (src_ext[q, 0], src_ext[q, 1])
            row = []
            for fine in range(FINE):
                before = here[fine - 1] if fine else sides[0]
                after = here[fine + 1] if fine < FINE - 1 else sides[1]
                new = (
                    (gs[q, fine, 0] * src[q, fine] + gs[q, fine, 1] * src[q + 2, fine])
                    + (gs[q, fine, 2] * before + gs[q, fine, 3] * after)
                    + (
                        gs[q, fine, 4] * pltpu.roll(here[fine], 1, 0)
                        + gs[q, fine, 5] * pltpu.roll(here[fine], NZ - 1, 0)
                    )
                )
                new = new + shift * (here[fine] if centre is src else centre[q + 1, fine])
                dst[q + 1, fine] = new
                row.append(new)
            if q not in LATE:
                dst_ext[q, 0], dst_ext[q, 1] = pltpu.roll(row[FINE - 1], 1, 1), pltpu.roll(row[0], 127, 1)
            if q == ROWS - 1:
                for fine in range(FINE):
                    dst[0, fine] = pltpu.roll(row[fine], BLOCKS, 1)
            if q == 0:
                for fine in range(FINE):
                    dst[ROWS + 1, fine] = pltpu.roll(row[fine], 128 - BLOCKS, 1)

    def pick(values, i):
        out = jnp.float32(values[0])
        for k in range(1, len(values)):
            out = jnp.where(i == k, jnp.float32(values[k]), out)
        return out

    def solve(i, floor_only):
        def start_rows(j, _):
            for m in range(4):
                q = 4 * j + m
                for fine in range(FINE):
                    value = inv[q, fine] * flat_tile(i, q, fine)
                    u_buf[q + 1, fine] = jnp.where((level == 0) | jnp.logical_not(floor_only), value, 0.0)
            return 0

        lax.fori_loop(0, ROWS // 4, start_rows, 0)
        for fine in range(FINE):
            u_buf[0, fine] = pltpu.roll(u_buf[ROWS, fine], BLOCKS, 1)
            u_buf[ROWS + 1, fine] = pltpu.roll(u_buf[1, fine], 128 - BLOCKS, 1)

        apply(u_buf, None, t_buf, t_ext, u_buf, jnp.float32(LINEAR))

        def factor(j, _):
            apply(t_buf, t_ext, u_buf, u_ext, t_buf, pick(PS, j))
            apply(u_buf, u_ext, t_buf, t_ext, t_buf, pick(QS, j))
            return 0

        lax.fori_loop(0, len(PS), factor, 0)

    def own_columns():
        out = exact_dot(jnp.concatenate([sums[fine] for fine in range(FINE)], axis=1), back[...])
        cut = [slice(WIDE, ROWS), slice(0, ROWS), slice(0, ROWS), slice(0, ROWS - WIDE)]
        return jnp.concatenate([out[rows, 128 * lot : 128 * lot + 128] for lot, rows in enumerate(cut)], axis=0)

    def fold(reduce):
        for q in range(ROWS):
            for fine in range(FINE):
                sums[fine, q : q + 1, :] = reduce(t_buf[q + 1, fine])

    weight = ice * obs[...]

    def rhs_copies(c):
        packs = rhs_pack.at[c]
        return to_neighbours(
            rhs.at[pl.ds(c, 1)], (packs, packs), (rhs_l.at[c], rhs_r.at[c]), c_send.at[c], c_recv.at[c]
        )

    def depth_copies(c):
        here = pltpu.make_async_copy(depth.at[c], depth_ref.at[c, :, own_cols], local_sem.at[8 + c])
        there_too = pltpu.make_async_remote_copy(
            depth.at[c],
            depth_ref.at[c, :, own_cols],
            swap_send.at[2 + c],
            swap_recv.at[2 + c],
            device_id=partner,
            device_id_type=MESH,
        )
        return here, there_too

    def phase(p, _):
        c = lax.rem(p, 2)
        forward = p < 2

        @pl.when(jnp.logical_not(forward))
        def _():
            arrived(rhs_copies(c))
            edge = jnp.where(spot < 64, rhs_r[c], rhs_l[c])
            put(c, exact_dot(in_lots(rhs[c], edge), place[:, : 128 * FINE]))

        solve(c, forward)

        @pl.when(forward)
        def _():
            fold(lambda tile: jnp.sum(tile, axis=0, keepdims=True))
            field = own_columns()
            depth[c] = field
            field = weight * field
            rhs[c, own_rows, :] = field
            rhs_pack[c] = with_edges(jnp.zeros((NX, 128), F32), field, 0)
            start_all(rhs_copies(c))
            for copy in depth_copies(c):
                copy.start()

        @pl.when(jnp.logical_not(forward))
        def _():
            fold(lambda tile: tile[0:1, :])
            mult[c] = own_columns()

        return 0

    lax.fori_loop(0, 4, phase, 0)

    hess_ref[...] = -friction * (base[0, 0].astype(F32) * mult[0] + base[0, 1].astype(F32) * mult[1])

    for copies in (flat_copies, visc_copies, rhs_copies(0), rhs_copies(1)):
        sent(copies)
    for c in range(2):
        for copy in depth_copies(c):
            copy.wait()


def hand_over(depth_in, hess_in, depth_out, hess_out, sem):
    copies = [
        pltpu.make_async_copy(depth_in, depth_out, sem.at[0]),
        pltpu.make_async_copy(hess_in, hess_out, sem.at[1]),
    ]
    for copy in copies:
        copy.start()
    for copy in copies:
        copy.wait()


def solution(mesh):
    gx_n, gy_n = mesh.shape["gx"], mesh.shape["gy"]

    def step(viscosity, velocity, log_friction, step_dir, obs_weight, tile_mask, contact):
        any_space = pl.BlockSpec(memory_space=pl.ANY)
        vmem, dma = pltpu.VMEM, pltpu.SemaphoreType.DMA
        nd = len(DIRS)
        results = pl.pallas_call(
            functools.partial(kernel, gx_n, gy_n),
            out_shape=(
                jax.ShapeDtypeStruct((2, NX, 2 * NY), F32),
                jax.ShapeDtypeStruct((NX, NY), F32),
            ),
            in_specs=[any_space] * 7,
            out_specs=(any_space, pl.BlockSpec(memory_space=pltpu.VMEM)),
            scratch_shapes=[
                vmem((NZ, XT, NY), BF16),
                vmem((XT, 128), BF16),
                vmem((XT, 128), BF16),
                vmem((NX, 128), BF16),
                vmem((NX, 128), BF16),
                vmem((2, 2, NX, NY), BF16),
                vmem((NX, NY), F32),
                vmem((NX, NY), F32),
                vmem((NX, NY), F32),
                vmem((NX, NY), jnp.int32),
                vmem((3, XT, NY), F32),
                vmem((NX, 128), F32),
                vmem((XT, 128), F32),
                vmem((XT, 128), F32),
                vmem((2, XT, NY), F32),
                vmem((2, NX, 128), F32),
                vmem((2, XT, 128), F32),
                vmem((2, XT, 128), F32),
                vmem((2, NX, NY), F32),
                vmem((2, NX, NY), F32),
                vmem((ROWS * NZ, 256 * LOTS), F32),
                vmem(((ROWS + 2) * (FINE + 2) * NZ, 128), F32),
                vmem((3, FINE, ROWS, 128), F32),
                vmem((FINE, ROWS, 128), F32),
                vmem((256 * LOTS, (FINE + 2) * 128), BF16),
                vmem((FINE * 128, 128 * LOTS), BF16),
                vmem((ROWS, FINE, 6, NZ, 128), F32),
                vmem((ROWS, FINE, NZ, 128), F32),
                vmem((ROWS, 2, NZ, 128), F32),
                vmem((ROWS, 2, NZ, 128), F32),
                vmem((ROWS + 2, FINE, NZ, 128), F32),
                vmem((ROWS + 2, FINE, NZ, 128), F32),
                pltpu.SMEM((1, 4), jnp.int32),
                dma((10,)),
                dma((4,)),
                dma((4,)),
                dma((nd,)),
                dma((nd,)),
                dma((nd,)),
                dma((nd,)),
                dma((2, nd)),
                dma((2, nd)),
            ],
            compiler_params=pltpu.CompilerParams(
                collective_id=0, has_side_effects=True, vmem_limit_bytes=40 * 1024 * 1024
            ),
        )(
            *(
                pltpu.with_memory_space_constraint(x, pltpu.HBM)
                for x in (viscosity, velocity, log_friction, step_dir, obs_weight, contact, tile_mask)
            )
        )
        return pl.pallas_call(
            hand_over,
            out_shape=tuple(jax.ShapeDtypeStruct(x.shape, x.dtype) for x in results),
            in_specs=[any_space, any_space],
            out_specs=(any_space, any_space),
            scratch_shapes=[dma((2,))],
            compiler_params=pltpu.CompilerParams(vmem_limit_bytes=1024 * 1024),
        )(*results)

    in_specs = (
        P("gz", "gx", "gy"),
        P(None, "gz", "gx", "gy"),
        P("gx", "gy"),
        P("gx", "gy"),
        P("gx", "gy"),
        P("gx", "gy"),
        P("gx", "gy"),
    )
    out_specs = (P(None, "gx", "gy"), P("gx", ("gy", "gz")))
    return jax.shard_map(step, mesh=mesh, in_specs=in_specs, out_specs=out_specs, check_vma=False)
```

```python
import functools
import math

import jax
import jax.numpy as jnp
from jax import lax
from jax.experimental import pallas as pl
from jax.experimental.pallas import tpu as pltpu
from jax.sharding import PartitionSpec as P

MESH = pl.DeviceIdType.MESH
F32 = jnp.float32
BF16 = jnp.bfloat16

SWEEP = 8
ASPECT = 16.0
LOWER = 0.1
UPPER = 2.0
CENTRE = (UPPER + LOWER) / 2.0
HALF = (UPPER - LOWER) / 2.0
SIGMA = CENTRE / HALF

DELTA = CENTRE - 1.0
LINEAR = DELTA + CENTRE
ORDER = (3, 6, 1, 4, 5, 2, 7)
ANGLES = [math.pi * j / SWEEP for j in ORDER]
PS = [2.0 * DELTA - 2.0 * CENTRE * math.cos(t) for t in ANGLES]
QS = [
    DELTA * DELTA - 2.0 * CENTRE * DELTA * math.cos(t) + CENTRE * CENTRE - (HALF * math.sin(t)) ** 2
    for t in ANGLES
]
TOP = math.cosh(SWEEP * math.acosh(SIGMA))
SCALE = 2.0 ** (2 * SWEEP - 2) / (TOP * TOP) / HALF ** (2 * SWEEP)

WIDE = 16
NX, NY, NZ = 64, 128, 8
XT, YT = NX + 2 * WIDE, NY + 2 * WIDE
LOTS = 4
ROWS = XT // LOTS
BLOCKS = 128 // LOTS
FINE = YT // BLOCKS
DIRS = [(-1, -1), (-1, 1), (1, -1), (1, 1), (-1, 0), (1, 0), (0, -1), (0, 1)]
R_AT, L_AT = 32, 80
ROW_ORDER = [ROWS - 1, *range(8), *range(ROWS - 2, 15, -1), *range(8, 16)]
LATE = range(12, 16)


def lanes_of(shape):
    return lax.broadcasted_iota(jnp.int32, shape, len(shape) - 1)


def turned(value, by):
    by %= 128
    return value if by == 0 else pltpu.roll(value, by, value.ndim - 1)


def one_in(rows, target):
    return (lax.broadcasted_iota(jnp.int32, (rows, 128), 0) == target).astype(F32).astype(BF16)


def chooser(fine):
    n = lanes_of((1, 128))
    y = FINE * (n % BLOCKS) + fine
    edge = jnp.where(y < WIDE, 128 + L_AT + y, 128 + R_AT + y - WIDE - NY)
    k = 256 * (n // BLOCKS) + jnp.where((y >= WIDE) & (y < WIDE + NY), y - WIDE, edge)
    return one_in(256 * LOTS, jnp.where((y >= 0) & (y < YT), k, -1))


def returner(lot):
    y = lanes_of((1, 128)) + WIDE
    return one_in(FINE * 128, (y % FINE) * 128 + BLOCKS * lot + y // FINE)


def thirds(value):
    high = value.astype(BF16)
    rest = value - high.astype(F32)
    middle = rest.astype(BF16)
    return high, middle, (rest - middle.astype(F32)).astype(BF16)


def dot(a, b):
    return jnp.dot(a, b, preferred_element_type=F32)


def exact_dot(value, matrix):
    n = value.shape[0]
    out = dot(jnp.concatenate(thirds(value), axis=0), matrix)
    return out[:n] + out[n : 2 * n] + out[2 * n :]


def kernel(
    gx_n,
    gy_n,
    visc_ref,
    vel_ref,
    logf_ref,
    step_ref,
    obs_ref,
    contact_ref,
    tile_ref,
    depth_ref,
    hess_ref,
    visc,
    edge_l,
    edge_r,
    pack_l,
    pack_r,
    base,
    logf,
    step,
    obs,
    contact,
    flat,
    flat_pack,
    flat_l,
    flat_r,
    rhs,
    rhs_pack,
    rhs_l,
    rhs_r,
    depth,
    mult,
    left,
    e_buf,
    spread,
    sums,
    place,
    back,
    gs,
    inv,
    u_ext,
    t_ext,
    u_buf,
    t_buf,
    classes,
    local_sem,
    swap_send,
    swap_recv,
    a_send,
    a_recv,
    b_send,
    b_recv,
    c_send,
    c_recv,
):
    gx, gy, gz = lax.axis_index("gx"), lax.axis_index("gy"), lax.axis_index("gz")
    yb = 2 * gy + gz
    y_n = 2 * gy_n

    def there(dx, dy):
        nx, ny = gx + dx, yb + dy
        return (nx >= 0) & (nx < gx_n) & (ny >= 0) & (ny < y_n)

    def device(dx, dy):
        ny = yb + dy
        return (gx + dx, lax.div(ny, 2), lax.rem(ny, 2))

    own_cols = pl.ds(pl.multiple_of(gz * NY, NY), NY)
    other_cols = pl.ds(pl.multiple_of((1 - gz) * NY, NY), NY)
    own_rows = pl.ds(WIDE, NX)
    layers = visc_ref.shape[0]
    mine = pl.ds(gz * layers, layers)
    partner = (gx, gy, 1 - gz)

    local = [
        pltpu.make_async_copy(visc_ref.at[:, :, own_cols], visc.at[mine, own_rows], local_sem.at[0]),
        pltpu.make_async_copy(vel_ref.at[:, 0, :, own_cols], base.at[gz], local_sem.at[1]),
        pltpu.make_async_copy(logf_ref.at[:, own_cols], logf, local_sem.at[2]),
        pltpu.make_async_copy(step_ref.at[:, own_cols], step, local_sem.at[3]),
        pltpu.make_async_copy(contact_ref.at[:, own_cols], contact, local_sem.at[4]),
        pltpu.make_async_copy(obs_ref.at[:, own_cols], obs, local_sem.at[5]),
        pltpu.make_async_copy(tile_ref, classes, local_sem.at[6]),
    ]
    for copy in local:
        copy.start()

    barrier = pltpu.get_barrier_semaphore()
    met = 0
    for d in DIRS:
        here = there(*d)
        met = met + here.astype(jnp.int32)

        @pl.when(here)
        def _():
            pl.semaphore_signal(barrier, inc=1, device_id=device(*d), device_id_type=MESH)

    @pl.when(gx == 0)
    def _():
        visc[:, 0:WIDE, :] = jnp.zeros((NZ, WIDE, NY), BF16)
        flat[:, 0:WIDE, :] = jnp.zeros((3, WIDE, NY), F32)
        rhs[:, 0:WIDE, :] = jnp.zeros((2, WIDE, NY), F32)

    @pl.when(gx == gx_n - 1)
    def _():
        visc[:, XT - WIDE : XT, :] = jnp.zeros((NZ, WIDE, NY), BF16)
        flat[:, XT - WIDE : XT, :] = jnp.zeros((3, WIDE, NY), F32)
        rhs[:, XT - WIDE : XT, :] = jnp.zeros((2, WIDE, NY), F32)

    for dy, ends in ((-1, (edge_l, flat_l, rhs_l)), (1, (edge_r, flat_r, rhs_r))):
        for dx, first, count in ((-1, 0, WIDE), (0, WIDE, NX), (1, WIDE + NX, WIDE)):

            @pl.when(jnp.logical_not(there(dx, dy)))
            def _():
                for end in ends[:2]:
                    end[first : first + count, :] = jnp.zeros((count, 128), end.dtype)
                ends[2][:, first : first + count, :] = jnp.zeros((2, count, 128), F32)

    for tile, fine in enumerate((*range(FINE), -1, FINE)):
        place[:, 128 * tile : 128 * tile + 128] = chooser(fine)
    for lot in range(LOTS):
        back[:, 128 * lot : 128 * lot + 128] = returner(lot)

    for copy in local[1:]:
        copy.wait()

    lane = lanes_of((NX, NY))
    left_class, right_class = classes[0, 2 * gz], classes[0, 2 * gz + 1]
    kinds = jnp.where(lane < NY // 2, left_class, right_class)
    ice = (kinds > 0).astype(F32)
    friction = jnp.exp(logf[...]) * (kinds == 2).astype(F32) * contact[...].astype(F32)
    marked = jnp.where(kinds > 0, jnp.maximum(friction, 1e-30), 0.0)
    flat[2, own_rows, :] = marked
    drive = -(friction * step[...])

    pl.semaphore_wait(barrier, met)

    swap = [
        pltpu.make_async_remote_copy(
            visc_ref.at[:, :, other_cols],
            visc.at[mine, own_rows],
            swap_send.at[0],
            swap_recv.at[0],
            device_id=partner,
            device_id_type=MESH,
        ),
        pltpu.make_async_remote_copy(
            vel_ref.at[:, 0, :, other_cols],
            base.at[gz],
            swap_send.at[1],
            swap_recv.at[1],
            device_id=partner,
            device_id_type=MESH,
        ),
    ]
    for copy in swap:
        copy.start()

    def with_edges(packed, field, shift):
        for at, first in ((R_AT - shift, 0), (L_AT - shift, NY - WIDE)):
            packed = jnp.where((lane >= at) & (lane < at + WIDE), turned(field, at - first), packed)
        return packed

    def extent(dx):
        if dx == 0:
            return pl.ds(WIDE, NX), pl.ds(0, NX), pl.ds(WIDE, NX)
        if dx < 0:
            return pl.ds(WIDE, WIDE), pl.ds(0, WIDE), pl.ds(WIDE + NX, WIDE)
        return pl.ds(NX, WIDE), pl.ds(NX - WIDE, WIDE), pl.ds(0, WIDE)

    def to_neighbours(block, packs, lands, send, recv):
        copies = []
        for i, (dx, dy) in enumerate(DIRS):
            src, src_pack, dst = extent(dx)
            if dy == 0:
                pair = (block.at[:, src, :], block.at[:, dst, :])
            elif dy < 0:
                pair = (packs[0].at[src_pack, :], lands[1].at[dst, :])
            else:
                pair = (packs[1].at[src_pack, :], lands[0].at[dst, :])
            copies.append(
                pltpu.make_async_remote_copy(
                    *pair,
                    send.at[i],
                    recv.at[i],
                    device_id=device(dx, dy),
                    device_id_type=MESH,
                )
            )
        return copies

    def start_all(copies):
        for (dx, dy), copy in zip(DIRS, copies):
            pl.when(there(dx, dy))(copy.start)

    def arrived(copies):
        for (dx, dy), copy in zip(DIRS, copies):
            pl.when(there(-dx, -dy))(copy.wait_recv)

    def sent(copies):
        for (dx, dy), copy in zip(DIRS, copies):
            pl.when(there(dx, dy))(copy.wait_send)

    local[0].wait()
    swap[0].wait()

    low = jnp.zeros((NX, 128), F32)
    high = jnp.zeros((NX, 128), F32)
    for layer in range(NZ):
        e = visc[layer, own_rows, :].astype(F32)
        inside = (lane >= 16 * layer) & (lane < 16 * layer + 16)
        low = jnp.where(inside, turned(e, 16 * layer), low)
        high = jnp.where(inside, turned(e, 16 * layer + 16), high)
    pack_l[...] = low.astype(BF16)
    pack_r[...] = high.astype(BF16)
    visc_copies = to_neighbours(visc, (pack_l, pack_r), (edge_l, edge_r), a_send, a_recv)
    start_all(visc_copies)

    swap[1].wait()
    flat[0, own_rows, :] = drive * base[0, 0].astype(F32)
    flat[1, own_rows, :] = drive * base[0, 1].astype(F32)
    packed = jnp.zeros((NX, 128), F32)
    for i in range(3):
        packed = with_edges(packed, flat[i, own_rows, :], 32 - 16 * i)
    flat_pack[...] = packed
    flat_copies = to_neighbours(flat, (flat_pack, flat_pack), (flat_l, flat_r), b_send, b_recv)
    start_all(flat_copies)

    whole = [lot for lot in range(LOTS) if ROWS * lot >= WIDE and ROWS * (lot + 1) <= WIDE + NX]
    for layer in range(NZ):
        for lot in whole:
            left[ROWS * layer : ROWS * layer + ROWS, 256 * lot : 256 * lot + 128] = visc[
                layer, WIDE : WIDE + NX, :
            ].astype(F32)[ROWS * lot - WIDE : ROWS * lot - WIDE + ROWS]

    arrived(visc_copies)

    spot = lanes_of((XT, 128))

    def in_lots(own, edge):
        return jnp.concatenate(
            [part[ROWS * lot : ROWS * lot + ROWS] for lot in range(LOTS) for part in (own, edge)], axis=1
        )

    ends_l, ends_r = edge_l[...].astype(F32), edge_r[...].astype(F32)
    for layer in range(NZ):
        edge = jnp.where(spot < 64, turned(ends_r, R_AT - 16 * layer), turned(ends_l, L_AT - 16 * layer))
        own = visc[layer].astype(F32)
        for lot in range(LOTS):
            rows, here = slice(ROWS * lot, ROWS * lot + ROWS), slice(ROWS * layer, ROWS * layer + ROWS)
            if lot not in whole:
                left[here, 256 * lot : 256 * lot + 128] = own[rows]
            left[here, 256 * lot + 128 : 256 * lot + 256] = edge[rows]

    tiles = FINE + 2
    rows_in = left[...].astype(BF16)
    for tile in range(tiles):
        placed = 0.5 * dot(rows_in, place[:, 128 * tile : 128 * tile + 128])
        for layer in range(NZ):
            e_buf[pl.ds(tiles * NZ + tile * NZ + layer, ROWS, stride=tiles * NZ), :] = placed[
                ROWS * layer : ROWS * layer + ROWS
            ]

    def e_tile(row, tile):
        return pl.ds(pl.multiple_of((row * tiles + tile) * NZ, NZ), NZ)

    for fine in range(FINE):
        e_buf[e_tile(0, fine), :] = pltpu.roll(e_buf[e_tile(ROWS, fine), :], BLOCKS, 1)
        e_buf[e_tile(ROWS + 1, fine), :] = pltpu.roll(e_buf[e_tile(1, fine), :], 128 - BLOCKS, 1)

    def put(i, placed):
        for fine in range(FINE):
            spread[i, fine] = placed[:, 128 * fine : 128 * fine + 128]

    arrived(flat_copies)
    ends = jnp.where(spot < 48, flat_r[...], flat_l[...])
    flat_rows = jnp.concatenate([in_lots(flat[i], turned(ends, 32 - 16 * i)) for i in range(3)], axis=0)
    placed = exact_dot(flat_rows, place[:, : 128 * FINE])
    for i in range(3):
        put(i, placed[ROWS * i : ROWS * i + ROWS])

    level = lax.broadcasted_iota(jnp.int32, (NZ, 128), 0)

    def flat_tile(i, q, fine):
        return jnp.broadcast_to(spread[i, fine, pl.ds(q, 1), :], (NZ, 128))

    def faces(i, _):
        for k in range(3 * FINE):
            q, fine = 3 * i + k // FINE, k % FINE
            here = e_buf[e_tile(q + 1, fine), :]

            def side(beside):
                return here + jnp.where(beside > 0, beside, here)

            def column(beside):
                return ASPECT * (here + beside)

            marks = flat_tile(2, q, fine)
            parts = [
                side(e_buf[e_tile(q, fine), :]),
                side(e_buf[e_tile(q + 2, fine), :]),
                side(e_buf[e_tile(q + 1, fine - 1 if fine else FINE), :]),
                side(e_buf[e_tile(q + 1, fine + 1 if fine < FINE - 1 else FINE + 1), :]),
                jnp.where(level > 0, column(pltpu.roll(here, 1, 0)), 0.0),
                jnp.where(level < NZ - 1, column(pltpu.roll(here, NZ - 1, 0)), 0.0),
            ]
            total = parts[0] + parts[1] + parts[2] + parts[3] + parts[4] + parts[5]
            total = total + jnp.where(level == 0, marks, 0.0)
            inverse = jnp.where(marks > 0, 1.0 / jnp.where(marks > 0, total, 1.0), 0.0)
            for j, part in enumerate(parts):
                gs[q, fine, j] = part * inverse
            inv[q, fine] = SCALE * inverse
        return 0

    lax.fori_loop(0, ROWS // 3, faces, 0)

    def across(buf, row):
        return pltpu.roll(buf[row, FINE - 1], 1, 1), pltpu.roll(buf[row, 0], 127, 1)

    def apply(src, src_ext, dst, dst_ext, centre, shift):
        found = {q: across(src, q + 1) for q in ROW_ORDER if q in LATE and src_ext is not None}
        for q in ROW_ORDER:
            here = [src[q + 1, fine] for fine in range(FINE)]
            if src_ext is None:
                sides = across(src, q + 1)
            else:
                sides = found[q] if q in LATE else (src_ext[q, 0], src_ext[q, 1])
            row = []
            for fine in range(FINE):
                before = here[fine - 1] if fine else sides[0]
                after = here[fine + 1] if fine < FINE - 1 else sides[1]
                new = (
                    (gs[q, fine, 0] * src[q, fine] + gs[q, fine, 1] * src[q + 2, fine])
                    + (gs[q, fine, 2] * before + gs[q, fine, 3] * after)
                    + (
                        gs[q, fine, 4] * pltpu.roll(here[fine], 1, 0)
                        + gs[q, fine, 5] * pltpu.roll(here[fine], NZ - 1, 0)
                    )
                )
                new = new + shift * (here[fine] if centre is src else centre[q + 1, fine])
                dst[q + 1, fine] = new
                row.append(new)
            if q not in LATE:
                dst_ext[q, 0], dst_ext[q, 1] = pltpu.roll(row[FINE - 1], 1, 1), pltpu.roll(row[0], 127, 1)
            if q == ROWS - 1:
                for fine in range(FINE):
                    dst[0, fine] = pltpu.roll(row[fine], BLOCKS, 1)
            if q == 0:
                for fine in range(FINE):
                    dst[ROWS + 1, fine] = pltpu.roll(row[fine], 128 - BLOCKS, 1)

    def pick(values, i):
        out = jnp.float32(values[0])
        for k in range(1, len(values)):
            out = jnp.where(i == k, jnp.float32(values[k]), out)
        return out

    def solve(i, floor_only):
        def start_rows(j, _):
            for m in range(12):
                q = 12 * j + m
                for fine in range(FINE):
                    value = inv[q, fine] * flat_tile(i, q, fine)
                    u_buf[q + 1, fine] = jnp.where((level == 0) | jnp.logical_not(floor_only), value, 0.0)
            return 0

        lax.fori_loop(0, ROWS // 12, start_rows, 0)
        for fine in range(FINE):
            u_buf[0, fine] = pltpu.roll(u_buf[ROWS, fine], BLOCKS, 1)
            u_buf[ROWS + 1, fine] = pltpu.roll(u_buf[1, fine], 128 - BLOCKS, 1)

        apply(u_buf, None, t_buf, t_ext, u_buf, jnp.float32(LINEAR))

        def factor(j, _):
            apply(t_buf, t_ext, u_buf, u_ext, t_buf, pick(PS, j))
            apply(u_buf, u_ext, t_buf, t_ext, t_buf, pick(QS, j))
            return 0

        lax.fori_loop(0, len(PS), factor, 0)

    def own_columns():
        out = exact_dot(jnp.concatenate([sums[fine] for fine in range(FINE)], axis=1), back[...])
        cut = [slice(WIDE, ROWS), slice(0, ROWS), slice(0, ROWS), slice(0, ROWS - WIDE)]
        return jnp.concatenate([out[rows, 128 * lot : 128 * lot + 128] for lot, rows in enumerate(cut)], axis=0)

    def fold(reduce):
        for q in range(ROWS):
            for fine in range(FINE):
                sums[fine, q : q + 1, :] = reduce(t_buf[q + 1, fine])

    weight = ice * obs[...]

    def rhs_copies(c):
        packs = rhs_pack.at[c]
        return to_neighbours(
            rhs.at[pl.ds(c, 1)], (packs, packs), (rhs_l.at[c], rhs_r.at[c]), c_send.at[c], c_recv.at[c]
        )

    def depth_copies(c):
        here = pltpu.make_async_copy(depth.at[c], depth_ref.at[c, :, own_cols], local_sem.at[8 + c])
        there_too = pltpu.make_async_remote_copy(
            depth.at[c],
            depth_ref.at[c, :, own_cols],
            swap_send.at[2 + c],
            swap_recv.at[2 + c],
            device_id=partner,
            device_id_type=MESH,
        )
        return here, there_too

    def phase(p, _):
        c = lax.rem(p, 2)
        forward = p < 2

        @pl.when(jnp.logical_not(forward))
        def _():
            arrived(rhs_copies(c))
            edge = jnp.where(spot < 64, rhs_r[c], rhs_l[c])
            put(c, exact_dot(in_lots(rhs[c], edge), place[:, : 128 * FINE]))

        solve(c, forward)

        @pl.when(forward)
        def _():
            fold(lambda tile: jnp.sum(tile, axis=0, keepdims=True))
            field = own_columns()
            depth[c] = field
            field = weight * field
            rhs[c, own_rows, :] = field
            rhs_pack[c] = with_edges(jnp.zeros((NX, 128), F32), field, 0)
            start_all(rhs_copies(c))
            for copy in depth_copies(c):
                copy.start()

        @pl.when(jnp.logical_not(forward))
        def _():
            fold(lambda tile: tile[0:1, :])
            mult[c] = own_columns()

        return 0

    lax.fori_loop(0, 4, phase, 0)

    hess_ref[...] = -friction * (base[0, 0].astype(F32) * mult[0] + base[0, 1].astype(F32) * mult[1])

    for copies in (flat_copies, visc_copies, rhs_copies(0), rhs_copies(1)):
        sent(copies)
    for c in range(2):
        for copy in depth_copies(c):
            copy.wait()


def hand_over(depth_in, hess_in, depth_out, hess_out, sem):
    copies = [
        pltpu.make_async_copy(depth_in, depth_out, sem.at[0]),
        pltpu.make_async_copy(hess_in, hess_out, sem.at[1]),
    ]
    for copy in copies:
        copy.start()
    for copy in copies:
        copy.wait()


def solution(mesh):
    gx_n, gy_n = mesh.shape["gx"], mesh.shape["gy"]

    def step(viscosity, velocity, log_friction, step_dir, obs_weight, tile_mask, contact):
        any_space = pl.BlockSpec(memory_space=pl.ANY)
        vmem, dma = pltpu.VMEM, pltpu.SemaphoreType.DMA
        nd = len(DIRS)
        results = pl.pallas_call(
            functools.partial(kernel, gx_n, gy_n),
            out_shape=(
                jax.ShapeDtypeStruct((2, NX, 2 * NY), F32),
                jax.ShapeDtypeStruct((NX, NY), F32),
            ),
            in_specs=[any_space] * 7,
            out_specs=(any_space, pl.BlockSpec(memory_space=pltpu.VMEM)),
            scratch_shapes=[
                vmem((NZ, XT, NY), BF16),
                vmem((XT, 128), BF16),
                vmem((XT, 128), BF16),
                vmem((NX, 128), BF16),
                vmem((NX, 128), BF16),
                vmem((2, 2, NX, NY), BF16),
                vmem((NX, NY), F32),
                vmem((NX, NY), F32),
                vmem((NX, NY), F32),
                vmem((NX, NY), jnp.int32),
                vmem((3, XT, NY), F32),
                vmem((NX, 128), F32),
                vmem((XT, 128), F32),
                vmem((XT, 128), F32),
                vmem((2, XT, NY), F32),
                vmem((2, NX, 128), F32),
                vmem((2, XT, 128), F32),
                vmem((2, XT, 128), F32),
                vmem((2, NX, NY), F32),
                vmem((2, NX, NY), F32),
                vmem((ROWS * NZ, 256 * LOTS), F32),
                vmem(((ROWS + 2) * (FINE + 2) * NZ, 128), F32),
                vmem((3, FINE, ROWS, 128), F32),
                vmem((FINE, ROWS, 128), F32),
                vmem((256 * LOTS, (FINE + 2) * 128), BF16),
                vmem((FINE * 128, 128 * LOTS), BF16),
                vmem((ROWS, FINE, 6, NZ, 128), F32),
                vmem((ROWS, FINE, NZ, 128), F32),
                vmem((ROWS, 2, NZ, 128), F32),
                vmem((ROWS, 2, NZ, 128), F32),
                vmem((ROWS + 2, FINE, NZ, 128), F32),
                vmem((ROWS + 2, FINE, NZ, 128), F32),
                pltpu.SMEM((1, 4), jnp.int32),
                dma((10,)),
                dma((4,)),
                dma((4,)),
                dma((nd,)),
                dma((nd,)),
                dma((nd,)),
                dma((nd,)),
                dma((2, nd)),
                dma((2, nd)),
            ],
            compiler_params=pltpu.CompilerParams(
                collective_id=0, has_side_effects=True, vmem_limit_bytes=40 * 1024 * 1024
            ),
        )(
            *(
                pltpu.with_memory_space_constraint(x, pltpu.HBM)
                for x in (viscosity, velocity, log_friction, step_dir, obs_weight, contact, tile_mask)
            )
        )
        return pl.pallas_call(
            hand_over,
            out_shape=tuple(jax.ShapeDtypeStruct(x.shape, x.dtype) for x in results),
            in_specs=[any_space, any_space],
            out_specs=(any_space, any_space),
            scratch_shapes=[dma((2,))],
            compiler_params=pltpu.CompilerParams(vmem_limit_bytes=1024 * 1024),
        )(*results)

    in_specs = (
        P("gz", "gx", "gy"),
        P(None, "gz", "gx", "gy"),
        P("gx", "gy"),
        P("gx", "gy"),
        P("gx", "gy"),
        P("gx", "gy"),
        P("gx", "gy"),
    )
    out_specs = (P(None, "gx", "gy"), P("gx", ("gy", "gz")))
    return jax.shard_map(step, mesh=mesh, in_specs=in_specs, out_specs=out_specs, check_vma=False)
```

```python
import functools
import math

import jax
import jax.numpy as jnp
from jax import lax
from jax.experimental import pallas as pl
from jax.experimental.pallas import tpu as pltpu
from jax.sharding import PartitionSpec as P

MESH = pl.DeviceIdType.MESH
F32 = jnp.float32
BF16 = jnp.bfloat16

SWEEP = 8
ASPECT = 16.0
LOWER = 0.1
UPPER = 2.0
CENTRE = (UPPER + LOWER) / 2.0
HALF = (UPPER - LOWER) / 2.0
SIGMA = CENTRE / HALF

DELTA = CENTRE - 1.0
LINEAR = DELTA + CENTRE
ORDER = (3, 6, 1, 4, 5, 2, 7)
ANGLES = [math.pi * j / SWEEP for j in ORDER]
PS = [2.0 * DELTA - 2.0 * CENTRE * math.cos(t) for t in ANGLES]
QS = [
    DELTA * DELTA - 2.0 * CENTRE * DELTA * math.cos(t) + CENTRE * CENTRE - (HALF * math.sin(t)) ** 2
    for t in ANGLES
]
TOP = math.cosh(SWEEP * math.acosh(SIGMA))
SCALE = 2.0 ** (2 * SWEEP - 2) / (TOP * TOP) / HALF ** (2 * SWEEP)

WIDE = 16
NX, NY, NZ = 64, 128, 8
XT, YT = NX + 2 * WIDE, NY + 2 * WIDE
LOTS = 4
ROWS = XT // LOTS
BLOCKS = 128 // LOTS
FINE = YT // BLOCKS
DIRS = [(-1, -1), (-1, 1), (1, -1), (1, 1), (-1, 0), (1, 0), (0, -1), (0, 1)]
R_AT, L_AT = 32, 80
ROW_ORDER = [ROWS - 1, *range(8), *range(ROWS - 2, 15, -1), *range(8, 16)]
LATE = range(12, 16)


def lanes_of(shape):
    return lax.broadcasted_iota(jnp.int32, shape, len(shape) - 1)


def turned(value, by):
    by %= 128
    return value if by == 0 else pltpu.roll(value, by, value.ndim - 1)


def one_in(rows, target):
    return (lax.broadcasted_iota(jnp.int32, (rows, 128), 0) == target).astype(F32).astype(BF16)


def chooser(fine):
    n = lanes_of((1, 128))
    y = FINE * (n % BLOCKS) + fine
    edge = jnp.where(y < WIDE, 128 + L_AT + y, 128 + R_AT + y - WIDE - NY)
    k = 256 * (n // BLOCKS) + jnp.where((y >= WIDE) & (y < WIDE + NY), y - WIDE, edge)
    return one_in(256 * LOTS, jnp.where((y >= 0) & (y < YT), k, -1))


def returner(lot):
    y = lanes_of((1, 128)) + WIDE
    return one_in(FINE * 128, (y % FINE) * 128 + BLOCKS * lot + y // FINE)


def thirds(value):
    high = value.astype(BF16)
    rest = value - high.astype(F32)
    middle = rest.astype(BF16)
    return high, middle, (rest - middle.astype(F32)).astype(BF16)


def dot(a, b):
    return jnp.dot(a, b, preferred_element_type=F32)


def exact_dot(value, matrix):
    n = value.shape[0]
    out = dot(jnp.concatenate(thirds(value), axis=0), matrix)
    return out[:n] + out[n : 2 * n] + out[2 * n :]


def kernel(
    gx_n,
    gy_n,
    visc_ref,
    vel_ref,
    logf_ref,
    step_ref,
    obs_ref,
    contact_ref,
    tile_ref,
    depth_ref,
    hess_ref,
    visc,
    edge_l,
    edge_r,
    pack_l,
    pack_r,
    base,
    logf,
    step,
    obs,
    contact,
    flat,
    flat_pack,
    flat_l,
    flat_r,
    rhs,
    rhs_pack,
    rhs_l,
    rhs_r,
    depth,
    mult,
    left,
    e_buf,
    spread,
    sums,
    place,
    back,
    gs,
    inv,
    u_ext,
    t_ext,
    u_buf,
    t_buf,
    classes,
    local_sem,
    swap_send,
    swap_recv,
    a_send,
    a_recv,
    b_send,
    b_recv,
    c_send,
    c_recv,
):
    gx, gy, gz = lax.axis_index("gx"), lax.axis_index("gy"), lax.axis_index("gz")
    yb = 2 * gy + gz
    y_n = 2 * gy_n

    def there(dx, dy):
        nx, ny = gx + dx, yb + dy
        return (nx >= 0) & (nx < gx_n) & (ny >= 0) & (ny < y_n)

    def device(dx, dy):
        ny = yb + dy
        return (gx + dx, lax.div(ny, 2), lax.rem(ny, 2))

    own_cols = pl.ds(pl.multiple_of(gz * NY, NY), NY)
    other_cols = pl.ds(pl.multiple_of((1 - gz) * NY, NY), NY)
    own_rows = pl.ds(WIDE, NX)
    layers = visc_ref.shape[0]
    mine = pl.ds(gz * layers, layers)
    partner = (gx, gy, 1 - gz)

    local = [
        pltpu.make_async_copy(visc_ref.at[:, :, own_cols], visc.at[mine, own_rows], local_sem.at[0]),
        pltpu.make_async_copy(vel_ref.at[:, 0, :, own_cols], base.at[gz], local_sem.at[1]),
        pltpu.make_async_copy(logf_ref.at[:, own_cols], logf, local_sem.at[2]),
        pltpu.make_async_copy(step_ref.at[:, own_cols], step, local_sem.at[3]),
        pltpu.make_async_copy(contact_ref.at[:, own_cols], contact, local_sem.at[4]),
        pltpu.make_async_copy(obs_ref.at[:, own_cols], obs, local_sem.at[5]),
        pltpu.make_async_copy(tile_ref, classes, local_sem.at[6]),
    ]
    for copy in local:
        copy.start()

    barrier = pltpu.get_barrier_semaphore()
    met = 0
    for d in DIRS:
        here = there(*d)
        met = met + here.astype(jnp.int32)

        @pl.when(here)
        def _():
            pl.semaphore_signal(barrier, inc=1, device_id=device(*d), device_id_type=MESH)

    @pl.when(gx == 0)
    def _():
        visc[:, 0:WIDE, :] = jnp.zeros((NZ, WIDE, NY), BF16)
        flat[:, 0:WIDE, :] = jnp.zeros((3, WIDE, NY), F32)
        rhs[:, 0:WIDE, :] = jnp.zeros((2, WIDE, NY), F32)

    @pl.when(gx == gx_n - 1)
    def _():
        visc[:, XT - WIDE : XT, :] = jnp.zeros((NZ, WIDE, NY), BF16)
        flat[:, XT - WIDE : XT, :] = jnp.zeros((3, WIDE, NY), F32)
        rhs[:, XT - WIDE : XT, :] = jnp.zeros((2, WIDE, NY), F32)

    for dy, ends in ((-1, (edge_l, flat_l, rhs_l)), (1, (edge_r, flat_r, rhs_r))):
        for dx, first, count in ((-1, 0, WIDE), (0, WIDE, NX), (1, WIDE + NX, WIDE)):

            @pl.when(jnp.logical_not(there(dx, dy)))
            def _():
                for end in ends[:2]:
                    end[first : first + count, :] = jnp.zeros((count, 128), end.dtype)
                ends[2][:, first : first + count, :] = jnp.zeros((2, count, 128), F32)

    for tile, fine in enumerate((*range(FINE), -1, FINE)):
        place[:, 128 * tile : 128 * tile + 128] = chooser(fine)
    for lot in range(LOTS):
        back[:, 128 * lot : 128 * lot + 128] = returner(lot)

    for copy in local[1:]:
        copy.wait()

    lane = lanes_of((NX, NY))
    left_class, right_class = classes[0, 2 * gz], classes[0, 2 * gz + 1]
    kinds = jnp.where(lane < NY // 2, left_class, right_class)
    ice = (kinds > 0).astype(F32)
    friction = jnp.exp(logf[...]) * (kinds == 2).astype(F32) * contact[...].astype(F32)
    marked = jnp.where(kinds > 0, jnp.maximum(friction, 1e-30), 0.0)
    flat[2, own_rows, :] = marked
    drive = -(friction * step[...])

    pl.semaphore_wait(barrier, met)

    swap = [
        pltpu.make_async_remote_copy(
            visc_ref.at[:, :, other_cols],
            visc.at[mine, own_rows],
            swap_send.at[0],
            swap_recv.at[0],
            device_id=partner,
            device_id_type=MESH,
        ),
        pltpu.make_async_remote_copy(
            vel_ref.at[:, 0, :, other_cols],
            base.at[gz],
            swap_send.at[1],
            swap_recv.at[1],
            device_id=partner,
            device_id_type=MESH,
        ),
    ]
    for copy in swap:
        copy.start()

    def with_edges(packed, field, shift):
        for at, first in ((R_AT - shift, 0), (L_AT - shift, NY - WIDE)):
            packed = jnp.where((lane >= at) & (lane < at + WIDE), turned(field, at - first), packed)
        return packed

    def extent(dx):
        if dx == 0:
            return pl.ds(WIDE, NX), pl.ds(0, NX), pl.ds(WIDE, NX)
        if dx < 0:
            return pl.ds(WIDE, WIDE), pl.ds(0, WIDE), pl.ds(WIDE + NX, WIDE)
        return pl.ds(NX, WIDE), pl.ds(NX - WIDE, WIDE), pl.ds(0, WIDE)

    def to_neighbours(block, packs, lands, send, recv):
        copies = []
        for i, (dx, dy) in enumerate(DIRS):
            src, src_pack, dst = extent(dx)
            if dy == 0:
                pair = (block.at[:, src, :], block.at[:, dst, :])
            elif dy < 0:
                pair = (packs[0].at[src_pack, :], lands[1].at[dst, :])
            else:
                pair = (packs[1].at[src_pack, :], lands[0].at[dst, :])
            copies.append(
                pltpu.make_async_remote_copy(
                    *pair,
                    send.at[i],
                    recv.at[i],
                    device_id=device(dx, dy),
                    device_id_type=MESH,
                )
            )
        return copies

    def start_all(copies):
        for (dx, dy), copy in zip(DIRS, copies):
            pl.when(there(dx, dy))(copy.start)

    def arrived(copies):
        for (dx, dy), copy in zip(DIRS, copies):
            pl.when(there(-dx, -dy))(copy.wait_recv)

    def sent(copies):
        for (dx, dy), copy in zip(DIRS, copies):
            pl.when(there(dx, dy))(copy.wait_send)

    local[0].wait()
    swap[0].wait()

    low = jnp.zeros((NX, 128), F32)
    high = jnp.zeros((NX, 128), F32)
    for layer in range(NZ):
        e = visc[layer, own_rows, :].astype(F32)
        inside = (lane >= 16 * layer) & (lane < 16 * layer + 16)
        low = jnp.where(inside, turned(e, 16 * layer), low)
        high = jnp.where(inside, turned(e, 16 * layer + 16), high)
    pack_l[...] = low.astype(BF16)
    pack_r[...] = high.astype(BF16)
    visc_copies = to_neighbours(visc, (pack_l, pack_r), (edge_l, edge_r), a_send, a_recv)
    start_all(visc_copies)

    swap[1].wait()
    flat[0, own_rows, :] = drive * base[0, 0].astype(F32)
    flat[1, own_rows, :] = drive * base[0, 1].astype(F32)
    packed = jnp.zeros((NX, 128), F32)
    for i in range(3):
        packed = with_edges(packed, flat[i, own_rows, :], 32 - 16 * i)
    flat_pack[...] = packed
    flat_copies = to_neighbours(flat, (flat_pack, flat_pack), (flat_l, flat_r), b_send, b_recv)
    start_all(flat_copies)

    whole = [lot for lot in range(LOTS) if ROWS * lot >= WIDE and ROWS * (lot + 1) <= WIDE + NX]
    for layer in range(NZ):
        for lot in whole:
            left[ROWS * layer : ROWS * layer + ROWS, 256 * lot : 256 * lot + 128] = visc[
                layer, WIDE : WIDE + NX, :
            ].astype(F32)[ROWS * lot - WIDE : ROWS * lot - WIDE + ROWS]

    arrived(visc_copies)

    spot = lanes_of((XT, 128))

    def in_lots(own, edge):
        return jnp.concatenate(
            [part[ROWS * lot : ROWS * lot + ROWS] for lot in range(LOTS) for part in (own, edge)], axis=1
        )

    ends_l, ends_r = edge_l[...].astype(F32), edge_r[...].astype(F32)
    for layer in range(NZ):
        edge = jnp.where(spot < 64, turned(ends_r, R_AT - 16 * layer), turned(ends_l, L_AT - 16 * layer))
        own = visc[layer].astype(F32)
        for lot in range(LOTS):
            rows, here = slice(ROWS * lot, ROWS * lot + ROWS), slice(ROWS * layer, ROWS * layer + ROWS)
            if lot not in whole:
                left[here, 256 * lot : 256 * lot + 128] = own[rows]
            left[here, 256 * lot + 128 : 256 * lot + 256] = edge[rows]

    tiles = FINE + 2
    rows_in = left[...].astype(BF16)
    for tile in range(tiles):
        placed = 0.5 * dot(rows_in, place[:, 128 * tile : 128 * tile + 128])
        for layer in range(NZ):
            e_buf[pl.ds(tiles * NZ + tile * NZ + layer, ROWS, stride=tiles * NZ), :] = placed[
                ROWS * layer : ROWS * layer + ROWS
            ]

    def e_tile(row, tile):
        return pl.ds(pl.multiple_of((row * tiles + tile) * NZ, NZ), NZ)

    for fine in range(FINE):
        e_buf[e_tile(0, fine), :] = pltpu.roll(e_buf[e_tile(ROWS, fine), :], BLOCKS, 1)
        e_buf[e_tile(ROWS + 1, fine), :] = pltpu.roll(e_buf[e_tile(1, fine), :], 128 - BLOCKS, 1)

    def put(i, placed):
        for fine in range(FINE):
            spread[i, fine] = placed[:, 128 * fine : 128 * fine + 128]

    arrived(flat_copies)
    ends = jnp.where(spot < 48, flat_r[...], flat_l[...])
    flat_rows = jnp.concatenate([in_lots(flat[i], turned(ends, 32 - 16 * i)) for i in range(3)], axis=0)
    placed = exact_dot(flat_rows, place[:, : 128 * FINE])
    for i in range(3):
        put(i, placed[ROWS * i : ROWS * i + ROWS])

    level = lax.broadcasted_iota(jnp.int32, (NZ, 128), 0)

    def flat_tile(i, q, fine):
        return jnp.broadcast_to(spread[i, fine, pl.ds(q, 1), :], (NZ, 128))

    def faces(i, _):
        for k in range(4 * FINE):
            q, fine = 4 * i + k // FINE, k % FINE
            here = e_buf[e_tile(q + 1, fine), :]

            def side(beside):
                return here + jnp.where(beside > 0, beside, here)

            def column(beside):
                return ASPECT * (here + beside)

            marks = flat_tile(2, q, fine)
            parts = [
                side(e_buf[e_tile(q, fine), :]),
                side(e_buf[e_tile(q + 2, fine), :]),
                side(e_buf[e_tile(q + 1, fine - 1 if fine else FINE), :]),
                side(e_buf[e_tile(q + 1, fine + 1 if fine < FINE - 1 else FINE + 1), :]),
                jnp.where(level > 0, column(pltpu.roll(here, 1, 0)), 0.0),
                jnp.where(level < NZ - 1, column(pltpu.roll(here, NZ - 1, 0)), 0.0),
            ]
            total = parts[0] + parts[1] + parts[2] + parts[3] + parts[4] + parts[5]
            total = total + jnp.where(level == 0, marks, 0.0)
            inverse = jnp.where(marks > 0, 1.0 / jnp.where(marks > 0, total, 1.0), 0.0)
            for j, part in enumerate(parts):
                gs[q, fine, j] = part * inverse
            inv[q, fine] = SCALE * inverse
        return 0

    lax.fori_loop(0, ROWS // 4, faces, 0)

    def across(buf, row):
        return pltpu.roll(buf[row, FINE - 1], 1, 1), pltpu.roll(buf[row, 0], 127, 1)

    def apply(src, src_ext, dst, dst_ext, centre, shift):
        found = {q: across(src, q + 1) for q in ROW_ORDER if q in LATE and src_ext is not None}
        for q in ROW_ORDER:
            here = [src[q + 1, fine] for fine in range(FINE)]
            if src_ext is None:
                sides = across(src, q + 1)
            else:
                sides = found[q] if q in LATE else (src_ext[q, 0], src_ext[q, 1])
            row = []
            for fine in range(FINE):
                before = here[fine - 1] if fine else sides[0]
                after = here[fine + 1] if fine < FINE - 1 else sides[1]
                new = (
                    (gs[q, fine, 0] * src[q, fine] + gs[q, fine, 1] * src[q + 2, fine])
                    + (gs[q, fine, 2] * before + gs[q, fine, 3] * after)
                    + (
                        gs[q, fine, 4] * pltpu.roll(here[fine], 1, 0)
                        + gs[q, fine, 5] * pltpu.roll(here[fine], NZ - 1, 0)
                    )
                )
                new = new + shift * (here[fine] if centre is src else centre[q + 1, fine])
                dst[q + 1, fine] = new
                row.append(new)
            if q not in LATE:
                dst_ext[q, 0], dst_ext[q, 1] = pltpu.roll(row[FINE - 1], 1, 1), pltpu.roll(row[0], 127, 1)
            if q == ROWS - 1:
                for fine in range(FINE):
                    dst[0, fine] = pltpu.roll(row[fine], BLOCKS, 1)
            if q == 0:
                for fine in range(FINE):
                    dst[ROWS + 1, fine] = pltpu.roll(row[fine], 128 - BLOCKS, 1)

    def pick(values, i):
        out = jnp.float32(values[0])
        for k in range(1, len(values)):
            out = jnp.where(i == k, jnp.float32(values[k]), out)
        return out

    def solve(i, floor_only):
        def start_rows(j, _):
            for m in range(24):
                q = 24 * j + m
                for fine in range(FINE):
                    value = inv[q, fine] * flat_tile(i, q, fine)
                    u_buf[q + 1, fine] = jnp.where((level == 0) | jnp.logical_not(floor_only), value, 0.0)
            return 0

        lax.fori_loop(0, ROWS // 24, start_rows, 0)
        for fine in range(FINE):
            u_buf[0, fine] = pltpu.roll(u_buf[ROWS, fine], BLOCKS, 1)
            u_buf[ROWS + 1, fine] = pltpu.roll(u_buf[1, fine], 128 - BLOCKS, 1)

        apply(u_buf, None, t_buf, t_ext, u_buf, jnp.float32(LINEAR))

        def factor(j, _):
            apply(t_buf, t_ext, u_buf, u_ext, t_buf, pick(PS, j))
            apply(u_buf, u_ext, t_buf, t_ext, t_buf, pick(QS, j))
            return 0

        lax.fori_loop(0, len(PS), factor, 0)

    def own_columns():
        out = exact_dot(jnp.concatenate([sums[fine] for fine in range(FINE)], axis=1), back[...])
        cut = [slice(WIDE, ROWS), slice(0, ROWS), slice(0, ROWS), slice(0, ROWS - WIDE)]
        return jnp.concatenate([out[rows, 128 * lot : 128 * lot + 128] for lot, rows in enumerate(cut)], axis=0)

    def fold(reduce):
        for q in range(ROWS):
            for fine in range(FINE):
                sums[fine, q : q + 1, :] = reduce(t_buf[q + 1, fine])

    weight = ice * obs[...]

    def rhs_copies(c):
        packs = rhs_pack.at[c]
        return to_neighbours(
            rhs.at[pl.ds(c, 1)], (packs, packs), (rhs_l.at[c], rhs_r.at[c]), c_send.at[c], c_recv.at[c]
        )

    def depth_copies(c):
        here = pltpu.make_async_copy(depth.at[c], depth_ref.at[c, :, own_cols], local_sem.at[8 + c])
        there_too = pltpu.make_async_remote_copy(
            depth.at[c],
            depth_ref.at[c, :, own_cols],
            swap_send.at[2 + c],
            swap_recv.at[2 + c],
            device_id=partner,
            device_id_type=MESH,
        )
        return here, there_too

    def phase(p, _):
        c = lax.rem(p, 2)
        forward = p < 2

        @pl.when(jnp.logical_not(forward))
        def _():
            arrived(rhs_copies(c))
            edge = jnp.where(spot < 64, rhs_r[c], rhs_l[c])
            put(c, exact_dot(in_lots(rhs[c], edge), place[:, : 128 * FINE]))

        solve(c, forward)

        @pl.when(forward)
        def _():
            fold(lambda tile: jnp.sum(tile, axis=0, keepdims=True))
            field = own_columns()
            depth[c] = field
            field = weight * field
            rhs[c, own_rows, :] = field
            rhs_pack[c] = with_edges(jnp.zeros((NX, 128), F32), field, 0)
            start_all(rhs_copies(c))
            for copy in depth_copies(c):
                copy.start()

        @pl.when(jnp.logical_not(forward))
        def _():
            fold(lambda tile: tile[0:1, :])
            mult[c] = own_columns()

        return 0

    lax.fori_loop(0, 4, phase, 0)

    hess_ref[...] = -friction * (base[0, 0].astype(F32) * mult[0] + base[0, 1].astype(F32) * mult[1])

    for copies in (flat_copies, visc_copies, rhs_copies(0), rhs_copies(1)):
        sent(copies)
    for c in range(2):
        for copy in depth_copies(c):
            copy.wait()


def hand_over(depth_in, hess_in, depth_out, hess_out, sem):
    copies = [
        pltpu.make_async_copy(depth_in, depth_out, sem.at[0]),
        pltpu.make_async_copy(hess_in, hess_out, sem.at[1]),
    ]
    for copy in copies:
        copy.start()
    for copy in copies:
        copy.wait()


def solution(mesh):
    gx_n, gy_n = mesh.shape["gx"], mesh.shape["gy"]

    def step(viscosity, velocity, log_friction, step_dir, obs_weight, tile_mask, contact):
        any_space = pl.BlockSpec(memory_space=pl.ANY)
        vmem, dma = pltpu.VMEM, pltpu.SemaphoreType.DMA
        nd = len(DIRS)
        results = pl.pallas_call(
            functools.partial(kernel, gx_n, gy_n),
            out_shape=(
                jax.ShapeDtypeStruct((2, NX, 2 * NY), F32),
                jax.ShapeDtypeStruct((NX, NY), F32),
            ),
            in_specs=[any_space] * 7,
            out_specs=(any_space, pl.BlockSpec(memory_space=pltpu.VMEM)),
            scratch_shapes=[
                vmem((NZ, XT, NY), BF16),
                vmem((XT, 128), BF16),
                vmem((XT, 128), BF16),
                vmem((NX, 128), BF16),
                vmem((NX, 128), BF16),
                vmem((2, 2, NX, NY), BF16),
                vmem((NX, NY), F32),
                vmem((NX, NY), F32),
                vmem((NX, NY), F32),
                vmem((NX, NY), jnp.int32),
                vmem((3, XT, NY), F32),
                vmem((NX, 128), F32),
                vmem((XT, 128), F32),
                vmem((XT, 128), F32),
                vmem((2, XT, NY), F32),
                vmem((2, NX, 128), F32),
                vmem((2, XT, 128), F32),
                vmem((2, XT, 128), F32),
                vmem((2, NX, NY), F32),
                vmem((2, NX, NY), F32),
                vmem((ROWS * NZ, 256 * LOTS), F32),
                vmem(((ROWS + 2) * (FINE + 2) * NZ, 128), F32),
                vmem((3, FINE, ROWS, 128), F32),
                vmem((FINE, ROWS, 128), F32),
                vmem((256 * LOTS, (FINE + 2) * 128), BF16),
                vmem((FINE * 128, 128 * LOTS), BF16),
                vmem((ROWS, FINE, 6, NZ, 128), F32),
                vmem((ROWS, FINE, NZ, 128), F32),
                vmem((ROWS, 2, NZ, 128), F32),
                vmem((ROWS, 2, NZ, 128), F32),
                vmem((ROWS + 2, FINE, NZ, 128), F32),
                vmem((ROWS + 2, FINE, NZ, 128), F32),
                pltpu.SMEM((1, 4), jnp.int32),
                dma((10,)),
                dma((4,)),
                dma((4,)),
                dma((nd,)),
                dma((nd,)),
                dma((nd,)),
                dma((nd,)),
                dma((2, nd)),
                dma((2, nd)),
            ],
            compiler_params=pltpu.CompilerParams(
                collective_id=0, has_side_effects=True, vmem_limit_bytes=40 * 1024 * 1024
            ),
        )(
            *(
                pltpu.with_memory_space_constraint(x, pltpu.HBM)
                for x in (viscosity, velocity, log_friction, step_dir, obs_weight, contact, tile_mask)
            )
        )
        return pl.pallas_call(
            hand_over,
            out_shape=tuple(jax.ShapeDtypeStruct(x.shape, x.dtype) for x in results),
            in_specs=[any_space, any_space],
            out_specs=(any_space, any_space),
            scratch_shapes=[dma((2,))],
            compiler_params=pltpu.CompilerParams(vmem_limit_bytes=1024 * 1024),
        )(*results)

    in_specs = (
        P("gz", "gx", "gy"),
        P(None, "gz", "gx", "gy"),
        P("gx", "gy"),
        P("gx", "gy"),
        P("gx", "gy"),
        P("gx", "gy"),
        P("gx", "gy"),
    )
    out_specs = (P(None, "gx", "gy"), P("gx", ("gy", "gz")))
    return jax.shard_map(step, mesh=mesh, in_specs=in_specs, out_specs=out_specs, check_vma=False)
```
